32 devices in a mesh: gx: 8 (over z, y), gy: 4 (over x, core).
Axes of the slice: x: 2, y: 2, z: 4, core: 2. Of those that a mesh axis runs over, the one named last changes fastest.
Arguments:
- psi: float32 [2, 256, 16, 1024], P(None, 'gx', None, 'gy'), may hold values from -6 to 6
- potential: float32 [256, 16, 1024], P('gx', None, 'gy'), may hold values from 0 to 4
Outputs:
- psi_half: float32 [2, 256, 16, 1024], P(None, 'gx', None, 'gy')
The draws below stay inside these ranges and needn't reach their ends.
All inputs are finite; a program needn't handle non-finite values.
Results may differ from the reference program's by a relative error of at most 0.00005.
Values sent between devices are 32-bit elements; how exact they have to be, the bound alone decides.
A program may use at most 64 MiB of HBM per device.

```python
import jax
import jax.numpy as jnp
from jax import lax

CX = 32
NZ = 16
RYZ = 2
NX = 256
NY = 1024


def draw_psi(key, part):
    values = jax.random.normal(key, (2, NX, NZ, NY), jnp.float32)
    return jnp.clip(values, -6.0, 6.0).astype(jnp.float32)


def level_of(rng, shape, shards, low, largest):
    def one(position, blocks):
        heights = jax.random.uniform(jax.random.fold_in(jax.random.fold_in(rng, 6), position), (blocks,), jnp.float32, low / len(shards), largest / len(shards))
        return jnp.repeat(jnp.exp(heights), shape[position] // blocks).reshape((-1,) + (1,) * (len(shape) - position - 1))

    loudness = one(*shards[0])
    for cut in shards[1:]:
        loudness = loudness * one(*cut)
    return loudness


def setup_inputs(seed: int = 0) -> dict:
    streams_of = jax.random.split(jax.random.key(seed), 3)
    psi = draw_psi(jax.random.fold_in(streams_of[2], 71), 0)
    potential = jnp.clip(4.0 * jax.random.uniform(streams_of[1], (NX, NZ, NY), jnp.float32) ** level_of(streams_of[1], (NX, NZ, NY), ((0, 8), (2, 4)), -0.2, 0.2), 0.0, 4.0)
    return dict(psi=psi, potential=potential)


def neighbours(field, axis):
    width = [(0, 0)] * field.ndim
    width[axis] = (1, 1)
    padded = jnp.pad(field, width)
    upper = lax.slice_in_dim(padded, 2, field.shape[axis] + 2, axis=axis)
    lower = lax.slice_in_dim(padded, 0, field.shape[axis], axis=axis)
    return upper + lower - 2.0 * field


def reference(psi, potential):
    coef = 256.0 * CX * CX
    real_part, imag_part = psi[0], psi[1]
    theta = 0.5 * (potential + real_part * real_part + imag_part * imag_part)
    cosine, sine = jnp.cos(theta), jnp.sin(theta)
    turn_re = real_part * cosine + imag_part * sine
    turn_im = imag_part * cosine - real_part * sine
    side_re = RYZ * (neighbours(turn_re, 2) + neighbours(turn_re, 1))
    side_im = RYZ * (neighbours(turn_im, 2) + neighbours(turn_im, 1))
    rhs_re = 2.0 * turn_re - side_im
    rhs_im = 2.0 * turn_im + side_re

    def forward(carry, row):
        cp_re, cp_im, dp_re, dp_im = carry
        f_re, f_im = row
        m_re = 1.0 - coef * cp_im
        m_im = 2.0 * coef + coef * cp_re
        denom = m_re * m_re + m_im * m_im
        new_cp_re = (-coef * m_im) / denom
        new_cp_im = (-coef * m_re) / denom
        n_re = f_re - coef * dp_im
        n_im = f_im + coef * dp_re
        new_dp_re = (n_re * m_re + n_im * m_im) / denom
        new_dp_im = (n_im * m_re - n_re * m_im) / denom
        out = (new_cp_re, new_cp_im, new_dp_re, new_dp_im)
        return out, out

    start = (jnp.zeros((), jnp.float32), jnp.zeros((), jnp.float32),
             jnp.zeros_like(rhs_re[0]), jnp.zeros_like(rhs_re[0]))
    unused, sweep = lax.scan(forward, start, (rhs_re, rhs_im))

    def backward(carry, row):
        x_re, x_im = carry
        cp_re, cp_im, dp_re, dp_im = row
        new_re = dp_re - (cp_re * x_re - cp_im * x_im)
        new_im = dp_im - (cp_re * x_im + cp_im * x_re)
        return (new_re, new_im), (new_re, new_im)

    unused, solved = lax.scan(backward, (jnp.zeros_like(rhs_re[0]), jnp.zeros_like(rhs_re[0])), sweep, reverse=True)
    return jnp.stack([solved[0] - turn_re, solved[1] - turn_im])
```

```python
import functools

import jax
import jax.numpy as jnp
import numpy as np
from jax import lax
from jax.experimental import pallas as pl
from jax.experimental.pallas import tpu as pltpu
from jax.sharding import PartitionSpec as P

RYZ = 2.0
LANES = 128
SUBLANES = 8
MESH = pl.DeviceIdType.MESH


def tables(cells, count):
    coef = 256.0 * cells * cells
    total = cells * count
    lam = np.arccosh(np.complex128(1.0 - 0.5j / coef))
    sh = lambda m: np.sinh(lam * m)
    scale = -(1j / coef) / (sh(1) * sh(total + 1))
    x0 = cells * np.arange(count, dtype=np.float64)
    end = x0 + cells
    f_q = sh(end) - sh(end + 1)
    f_e = sh(end + 1)
    r_q = sh(total + 1 - end) - sh(total - end)
    r_e = sh(total - end)
    w_l = scale * sh(total + 1 - x0)
    w_r = scale * sh(x0)
    d_l = scale * (sh(total - x0) - sh(total + 1 - x0))
    d_r = scale * (sh(x0 + 1) - sh(x0))
    rows = [f_q, f_e, r_q, r_e, w_l, w_r, d_l, d_r]
    place = np.stack([part for row in rows for part in (row.real, row.imag)], axis=1)
    return place.astype(np.float32).reshape(-1), coef


HALF_SINE = (4.442882834149953, -7.308241154547353, 3.6062889582396482, -0.8457635962213053, 0.10920575376953141)
HALF_COSINE = (1.4142134965650301, -6.9788509882409375, 5.739461170721302, -1.883562987555641, 0.3106981923194725)


def turn(re, im, pot):
    t = (pot + re * re + im * im) * np.float32(0.25 / np.pi)
    f = t - jnp.round(t)
    f2 = f * f
    s = np.float32(HALF_SINE[-1])
    for a in HALF_SINE[-2::-1]:
        s = s * f2 + np.float32(a)
    s = s * f
    c = np.float32(HALF_COSINE[-1])
    for a in HALF_COSINE[-2::-1]:
        c = c * f2 + np.float32(a)
    sine = s * c
    cosine = 1.0 - s * s
    return re * cosine + im * sine, im * cosine - re * sine


def kernel(count, wide, coef, chunk, psi, pot, place_in, turned, rho,
           start, place_ref, table_sem, psi_v, pot_v, edge, halo, fr, recv, in_sem, hs_sem, hr_sem, s_sem, r_sem,
           rim, beside, es_sem, er_sem):
    cells, planes, lines = pot_v.shape
    chunks = cells // chunk
    groups = planes // SUBLANES
    gx = lax.axis_index("gx")
    gy = lax.axis_index("gy")
    inv = np.float32(1.0 / coef)

    def load(i):
        part = pl.ds(i * chunk, chunk)
        return (
            pltpu.make_async_copy(psi.at[:, part], psi_v.at[:, part], in_sem.at[0, i]),
            pltpu.make_async_copy(pot.at[part], pot_v.at[part], in_sem.at[1, i]),
        )

    for i in range(chunks):
        for copy in load(i):
            copy.start()

    table = pltpu.make_async_copy(place_in, place_ref, table_sem.at[0])
    table.start()

    barrier = pltpu.get_barrier_semaphore()

    def greet(x, y):
        pl.semaphore_signal(barrier, inc=1, device_id={"gx": x, "gy": y}, device_id_type=MESH)

    @pl.loop(0, count)
    def _(k):
        @pl.when(k != gx)
        def _():
            greet(k, gy)

        @pl.when(gy > 0)
        def _():
            greet(k, gy - 1)

        @pl.when(gy < wide - 1)
        def _():
            greet(k, gy + 1)

    def advance(c, carry):
        e_re, e_im, q_re, q_im = carry
        t_re, t_im = turn(psi_v[0, c], psi_v[1, c], pot_v[c])
        turned[0, c] = t_re
        turned[1, c] = t_im
        e_re = e_re + (t_re + inv * q_im)
        e_im = e_im + (t_im - inv * q_re)
        return e_re, e_im, q_re + e_re, q_im + e_im

    zero = jnp.zeros((planes, lines), jnp.float32)
    carry = (zero,) * 4
    for i in range(chunks):
        for copy in load(i):
            copy.wait()
        carry = lax.fori_loop(i * chunk, (i + 1) * chunk, advance, carry, unroll=4)
    e_re, e_im, q_re, q_im = carry

    table.wait()

    def scalar(index):
        return place_ref[gx * 16 + 2 * index], place_ref[gx * 16 + 2 * index + 1]

    def both(a, x, b, y):
        return (
            (a[0] * x[0] - a[1] * x[1]) + (b[0] * y[0] - b[1] * y[1]),
            (a[0] * x[1] + a[1] * x[0]) + (b[0] * y[1] + b[1] * y[0]),
        )

    lane_rim = lax.broadcasted_iota(jnp.int32, (SUBLANES, LANES), 1)
    for which in range(2):
        value = both(scalar(2 * which), (q_re, q_im), scalar(2 * which + 1), (e_re, e_im))
        fr[which, 0] = value[0]
        fr[which, 1] = value[1]
        for side in range(2):
            tile = jnp.zeros((SUBLANES, LANES), jnp.float32)
            for part in range(2):
                for g in range(groups):
                    rows = value[part][g * SUBLANES : (g + 1) * SUBLANES]
                    column = rows[:, 0:1] if side == 0 else rows[:, lines - 1 : lines]
                    tile = jnp.where(lane_rim == part * groups + g, column, tile)
            rim[which, side] = tile

    beyond = jnp.where(gy > 0, 1, 0) + jnp.where(gy < wide - 1, 1, 0)
    pl.semaphore_wait(barrier, count - 1 + count * beyond)

    def message(peer):
        return pltpu.make_async_remote_copy(
            fr.at[jnp.where(peer < gx, 1, 0)], recv.at[gx], s_sem.at[peer], r_sem.at[gx],
            device_id={"gx": peer}, device_id_type=MESH)

    def rim_message(peer, side):
        return pltpu.make_async_remote_copy(
            rim.at[jnp.where(peer <= gx, 1, 0), side], beside.at[1 - side, gx],
            es_sem.at[side, peer], er_sem.at[1 - side, gx],
            device_id={"gx": peer, "gy": gy - 1 + 2 * side}, device_id_type=MESH)

    def dispatch(do):
        @pl.loop(0, count)
        def _(i):
            peer = jnp.where(i <= gx, i, count - i + gx)

            @pl.when(peer != gx)
            def _():
                do(message(peer))

            @pl.when(gy > 0)
            def _():
                do(rim_message(peer, 0))

            @pl.when(gy < wide - 1)
            def _():
                do(rim_message(peer, 1))

    dispatch(lambda copy: copy.start())

    lane = lax.broadcasted_iota(jnp.int32, (planes, LANES), 1)

    def pack(c, acc):
        new = []
        for part in range(2):
            src = turned.at[part, c]
            first = src[:, 0:LANES][:, 0:1]
            last = src[:, lines - LANES : lines][:, LANES - 1 : LANES]
            new.append(jnp.where(lane == c, first, acc[2 * part]))
            new.append(jnp.where(lane == c, last, acc[2 * part + 1]))
        return tuple(new)

    zero_edge = jnp.zeros((planes, LANES), jnp.float32)
    packed = lax.fori_loop(0, cells, pack, (zero_edge,) * 4, unroll=4)
    for part in range(2):
        edge[0, part] = packed[2 * part]
        edge[1, part] = packed[2 * part + 1]

    down = pltpu.make_async_remote_copy(edge.at[0], halo.at[1], hs_sem.at[0], hr_sem.at[1],
                                        device_id={"gy": gy - 1}, device_id_type=MESH)
    up = pltpu.make_async_remote_copy(edge.at[1], halo.at[0], hs_sem.at[1], hr_sem.at[0],
                                      device_id={"gy": gy + 1}, device_id_type=MESH)

    @pl.when(gy > 0)
    def _():
        down.start()

    @pl.when(gy == 0)
    def _():
        halo[0] = jnp.zeros(halo.shape[1:], jnp.float32)

    @pl.when(gy < wide - 1)
    def _():
        up.start()

    @pl.when(gy == wide - 1)
    def _():
        halo[1] = jnp.zeros(halo.shape[1:], jnp.float32)

    col = lax.broadcasted_iota(jnp.int32, (planes, lines), 1)
    row = lax.broadcasted_iota(jnp.int32, (planes, lines), 0)
    at_first, at_last = col == 0, col == lines - 1
    at_bottom, at_top = row == 0, row == planes - 1

    def lap(x, first, last):
        left = jnp.where(at_first, first, pltpu.roll(x, 1, 1))
        right = jnp.where(at_last, last, pltpu.roll(x, lines - 1, 1))
        below = jnp.where(at_bottom, 0.0, pltpu.roll(x, 1, 0))
        above = jnp.where(at_top, 0.0, pltpu.roll(x, planes - 1, 0))
        return ((left + right) + (below + above)) - 4.0 * x

    def stencil(re, im, first, last):
        lap_re = lap(re, first[0], last[0])
        lap_im = lap(im, first[1], last[1])
        return 2.0 * re - RYZ * lap_im, 2.0 * im + RYZ * lap_re

    @pl.when(gy > 0)
    def _():
        up.wait_recv()

    @pl.when(gy < wide - 1)
    def _():
        down.wait_recv()

    h_all = (halo[0, 0], halo[0, 1], halo[1, 0], halo[1, 1])

    def fill(c, h):
        first = (h[0][:, 0:1], h[1][:, 0:1])
        last = (h[2][:, 0:1], h[3][:, 0:1])
        r_re, r_im = stencil(turned[0, c], turned[1, c], first, last)
        rho[0, c] = -inv * r_im
        rho[1, c] = inv * r_re
        return tuple(pltpu.roll(x, LANES - 1, 1) for x in h)

    lax.fori_loop(0, cells, fill, h_all, unroll=4)

    def arrival(k):
        return pltpu.make_async_remote_copy(
            fr.at[0], recv.at[k], s_sem.at[k], r_sem.at[k],
            device_id={"gx": k}, device_id_type=MESH)

    def rim_arrival(k, side):
        return pltpu.make_async_remote_copy(
            rim.at[0, 0], beside.at[side, k], es_sem.at[side, k], er_sem.at[side, k],
            device_id={"gx": k, "gy": gy - 1 + 2 * side}, device_id_type=MESH)

    zero_rim = jnp.zeros((SUBLANES, LANES), jnp.float32)

    @pl.when(gy == 0)
    def _():
        beside[0] = jnp.zeros(beside.shape[1:], jnp.float32)

    @pl.when(gy == wide - 1)
    def _():
        beside[1] = jnp.zeros(beside.shape[1:], jnp.float32)

    def take_rim(k, acc):
        @pl.when(gy > 0)
        def _():
            rim_arrival(k, 0).wait_recv()

        @pl.when(gy < wide - 1)
        def _():
            rim_arrival(k, 1).wait_recv()

        return acc[0] + beside[0, k], acc[1] + beside[1, k]

    def take(k, acc):
        arrival(k).wait_recv()
        return (acc[0] + recv[k, 0], acc[1] + recv[k, 1]) + take_rim(k, acc[2:])

    left = lax.fori_loop(0, gx, take, (zero, zero, zero_rim, zero_rim))
    right = (fr[1, 0], fr[1, 1]) + take_rim(gx, (zero_rim, zero_rim))
    right = lax.fori_loop(gx + 1, count, take, right)

    def spread(total):
        columns = []
        for tile in total[2:]:
            columns.append(tuple(
                jnp.concatenate([tile[:, part * groups + g : part * groups + g + 1] for g in range(groups)], axis=0)
                for part in range(2)))
        return stencil(total[0], total[1], columns[0], columns[1])

    left = spread(left)
    right = spread(right)
    w = both(scalar(4), left, scalar(5), right)
    d = both(scalar(6), left, scalar(7), right)

    for index, value in enumerate(w + d):
        start[index] = value

    dispatch(lambda copy: copy.wait_send())

    @pl.when(gy > 0)
    def _():
        down.wait_send()

    @pl.when(gy < wide - 1)
    def _():
        up.wait_send()


def finish(coef, chunk, turned, rho, start, out, out_v, out_sem):
    cells = turned.shape[1]
    chunks = cells // chunk
    inv = np.float32(1.0 / coef)

    def store(i):
        part = pl.ds(i * chunk, chunk)
        return pltpu.make_async_copy(out_v.at[:, part], out.at[:, part], out_sem.at[i])

    def march(c, carry):
        w_re, w_im, d_re, d_im = carry
        w_re = w_re + d_re
        w_im = w_im + d_im
        out_v[0, c] = w_re - turned[0, c]
        out_v[1, c] = w_im - turned[1, c]
        d_re = d_re + (rho[0, c] + inv * w_im)
        d_im = d_im + (rho[1, c] - inv * w_re)
        return w_re, w_im, d_re, d_im

    carry = (start[0], start[1], start[2], start[3])
    for i in range(chunks):
        carry = lax.fori_loop(i * chunk, (i + 1) * chunk, march, carry, unroll=4)
        store(i).start()
    for i in range(chunks):
        store(i).wait()


def shards(psi, potential):
    unused, cells, planes, lines = psi.shape
    count = lax.axis_size("gx")
    wide = lax.axis_size("gy")
    place, coef = tables(cells, count)
    chunk = 8 if cells % 8 == 0 else cells
    chunks = cells // chunk
    block = (2, cells, planes, lines)
    plane = (planes, lines)
    vmem = pl.BlockSpec(memory_space=pltpu.VMEM)
    held = pl.pallas_call(
        functools.partial(kernel, count, wide, coef, chunk),
        out_shape=[
            jax.ShapeDtypeStruct(block, jnp.float32),
            jax.ShapeDtypeStruct(block, jnp.float32),
            jax.ShapeDtypeStruct((4,) + plane, jnp.float32),
        ],
        in_specs=[
            pl.BlockSpec(memory_space=pltpu.HBM),
            pl.BlockSpec(memory_space=pltpu.HBM),
            pl.BlockSpec(memory_space=pltpu.HBM),
        ],
        out_specs=[vmem] * 3,
        scratch_shapes=[
            pltpu.SMEM(place.shape, jnp.float32),
            pltpu.SemaphoreType.DMA((1,)),
            pltpu.VMEM(block, jnp.float32),
            pltpu.VMEM(block[1:], jnp.float32),
            pltpu.VMEM((2, 2, planes, LANES), jnp.float32),
            pltpu.VMEM((2, 2, planes, LANES), jnp.float32),
            pltpu.VMEM((2, 2) + plane, jnp.float32),
            pltpu.VMEM((count, 2) + plane, jnp.float32),
            pltpu.SemaphoreType.DMA((2, chunks)),
            pltpu.SemaphoreType.DMA((2,)),
            pltpu.SemaphoreType.DMA((2,)),
            pltpu.SemaphoreType.DMA((count,)),
            pltpu.SemaphoreType.DMA((count,)),
            pltpu.VMEM((2, 2, SUBLANES, LANES), jnp.float32),
            pltpu.VMEM((2, count, SUBLANES, LANES), jnp.float32),
            pltpu.SemaphoreType.DMA((2, count)),
            pltpu.SemaphoreType.DMA((2, count)),
        ],
        compiler_params=pltpu.CompilerParams(
            collective_id=0, has_side_effects=True, vmem_limit_bytes=24 * 2**20
        ),
    )(*(pltpu.with_memory_space_constraint(x, pltpu.HBM) for x in
        (psi, potential, jnp.asarray(place))))
    return pl.pallas_call(
        functools.partial(finish, coef, chunk),
        out_shape=jax.ShapeDtypeStruct(block, jnp.float32),
        in_specs=[vmem] * 3,
        out_specs=pl.BlockSpec(memory_space=pl.ANY),
        scratch_shapes=[
            pltpu.VMEM(block, jnp.float32),
            pltpu.SemaphoreType.DMA((chunks,)),
        ],
        compiler_params=pltpu.CompilerParams(vmem_limit_bytes=16 * 2**20),
    )(*held)


def solution(mesh):
    return jax.shard_map(
        shards,
        mesh=mesh,
        in_specs=(P(None, "gx", None, "gy"), P("gx", None, "gy")),
        out_specs=P(None, "gx", None, "gy"),
        check_vma=False,
    )
```

```python
import functools

import jax
import jax.numpy as jnp
import numpy as np
from jax import lax
from jax.experimental import pallas as pl
from jax.experimental.pallas import tpu as pltpu
from jax.sharding import PartitionSpec as P

RYZ = 2.0
LANES = 128
MESH = pl.DeviceIdType.MESH


def tables(cells, count):
    coef = 256.0 * cells * cells
    total = cells * count
    lam = np.arccosh(np.complex128(1.0 - 0.5j / coef))
    sh = lambda m: np.sinh(lam * m)
    scale = -(1j / coef) / (sh(1) * sh(total + 1))
    x0 = cells * np.arange(count, dtype=np.float64)
    end = x0 + cells
    f_q = sh(end) - sh(end + 1)
    f_e = sh(end + 1)
    r_q = sh(total + 1 - end) - sh(total - end)
    r_e = sh(total - end)
    w_l = scale * sh(total + 1 - x0)
    w_r = scale * sh(x0)
    d_l = scale * (sh(total - x0) - sh(total + 1 - x0))
    d_r = scale * (sh(x0 + 1) - sh(x0))
    rows = [f_q, f_e, r_q, r_e, w_l, w_r, d_l, d_r]
    place = np.stack([part for row in rows for part in (row.real, row.imag)], axis=1)
    return place.astype(np.float32).reshape(-1), coef


HALF_SINE = (4.442882834149953, -7.308241154547353, 3.6062889582396482, -0.8457635962213053, 0.10920575376953141)
HALF_COSINE = (1.4142134965650301, -6.9788509882409375, 5.739461170721302, -1.883562987555641, 0.3106981923194725)


def turn(re, im, pot):
    t = (pot + re * re + im * im) * np.float32(0.25 / np.pi)
    f = t - jnp.round(t)
    f2 = f * f
    s = np.float32(HALF_SINE[-1])
    for a in HALF_SINE[-2::-1]:
        s = s * f2 + np.float32(a)
    s = s * f
    c = np.float32(HALF_COSINE[-1])
    for a in HALF_COSINE[-2::-1]:
        c = c * f2 + np.float32(a)
    sine = s * c
    cosine = 1.0 - s * s
    return re * cosine + im * sine, im * cosine - re * sine


def kernel(count, wide, coef, chunk, psi, pot, place_in, turned, rho,
           start, place_ref, table_sem, psi_v, pot_v, edge, halo, fr, recv, in_sem, hs_sem, hr_sem, s_sem, r_sem,
           rim, beside, es_sem, er_sem, band, ready):
    cells, planes, lines = pot_v.shape
    chunks = cells // chunk
    gx = lax.axis_index("gx")
    gy = lax.axis_index("gy")
    inv = np.float32(1.0 / coef)

    def load(i):
        part = pl.ds(i * chunk, chunk)
        return (
            pltpu.make_async_copy(psi.at[:, part], psi_v.at[:, part], in_sem.at[0, i]),
            pltpu.make_async_copy(pot.at[part], pot_v.at[part], in_sem.at[1, i]),
        )

    for i in range(chunks):
        for copy in load(i):
            copy.start()

    table = pltpu.make_async_copy(place_in, place_ref, table_sem.at[0])
    table.start()

    barrier = pltpu.get_barrier_semaphore()
    not_low, not_high = gy > 0, gy < wide - 1
    beyond = jnp.where(not_low, 1, 0) + jnp.where(not_high, 1, 0)

    def beside_do(do):
        @pl.when(not_low)
        def _():
            do(gy - 1)

        @pl.when(not_high)
        def _():
            do(gy + 1)

    def greet(x, y):
        pl.semaphore_signal(barrier, inc=1, device_id={"gx": x, "gy": y}, device_id_type=MESH)

    beside_do(lambda y: greet(gx, y))

    @pl.loop(gx + 1, count)
    def _(k):
        greet(k, gy)
        beside_do(lambda y: greet(k, y))

    across = lax.broadcasted_iota(jnp.int32, (lines, lines), 0) - lax.broadcasted_iota(jnp.int32, (lines, lines), 1)
    band[...] = jnp.where(across == 0, -4.0, jnp.where(jnp.abs(across) == 1, 1.0, 0.0)).astype(jnp.bfloat16)

    def tell(x, y):
        pl.semaphore_signal(ready.at[gx], inc=1, device_id={"gx": x, "gy": y}, device_id_type=MESH)

    def meet():
        pl.semaphore_wait(barrier, gx * (1 + beyond) + beyond)

        @pl.loop(0, gx)
        def _(k):
            tell(k, gy)
            beside_do(lambda y: tell(k, y))

    def advance(c, carry):
        e_re, e_im, q_re, q_im = carry
        t_re, t_im = turn(psi_v[0, c], psi_v[1, c], pot_v[c])
        turned[0, c] = t_re
        turned[1, c] = t_im
        e_re = e_re + (t_re + inv * q_im)
        e_im = e_im + (t_im - inv * q_re)
        return e_re, e_im, q_re + e_re, q_im + e_im

    zero = jnp.zeros((planes, lines), jnp.float32)
    carry = (zero,) * 4
    for i in range(chunks):
        for copy in load(i):
            copy.wait()
        carry = lax.fori_loop(i * chunk, (i + 1) * chunk, advance, carry, unroll=4)
        if i == 3:
            meet()
    e_re, e_im, q_re, q_im = carry

    table.wait()

    def scalar(index):
        return place_ref[gx * 16 + 2 * index], place_ref[gx * 16 + 2 * index + 1]

    def both(a, x, b, y):
        return (
            (a[0] * x[0] - a[1] * x[1]) + (b[0] * y[0] - b[1] * y[1]),
            (a[0] * x[1] + a[1] * x[0]) + (b[0] * y[1] + b[1] * y[0]),
        )

    lane = lax.broadcasted_iota(jnp.int32, (planes, LANES), 1)
    row_rim = lane - lax.broadcasted_iota(jnp.int32, (planes, LANES), 0)

    def interface(which):
        value = both(scalar(2 * which), (q_re, q_im), scalar(2 * which + 1), (e_re, e_im))
        fr[which, 0] = value[0]
        fr[which, 1] = value[1]
        for side in range(2):
            at = side * (lines - 1)
            tile = jnp.where(row_rim == 0, value[0][:, at : at + 1],
                             jnp.where(row_rim == planes, value[1][:, at : at + 1], 0.0))
            rim[which, side] = jnp.sum(tile, axis=0, keepdims=True)

    def message(peer):
        return pltpu.make_async_remote_copy(
            fr.at[jnp.where(peer < gx, 1, 0)], recv.at[gx], s_sem.at[peer], r_sem.at[gx],
            device_id={"gx": peer}, device_id_type=MESH)

    def rim_message(peer, side):
        return pltpu.make_async_remote_copy(
            rim.at[jnp.where(peer <= gx, 1, 0), side], beside.at[1 - side, gx],
            es_sem.at[side, peer], er_sem.at[1 - side, gx],
            device_id={"gx": peer, "gy": gy - 1 + 2 * side}, device_id_type=MESH)

    def rims(peer, do):
        @pl.when(not_low)
        def _():
            do(rim_message(peer, 0))

        @pl.when(not_high)
        def _():
            do(rim_message(peer, 1))

    def begin(copy):
        copy.start()

    def end(copy):
        copy.wait_send()

    interface(1)
    @pl.loop(0, gx + 1)
    def _(peer):
        rims(peer, begin)

    @pl.loop(0, gx)
    def _(peer):
        message(peer).start()

    interface(0)

    def pack(c, acc):
        new = []
        for part in range(2):
            src = turned.at[part, c]
            first = src[:, 0:LANES][:, 0:1]
            last = src[:, lines - LANES : lines][:, LANES - 1 : LANES]
            new.append(jnp.where(lane == lax.rem(2 * c + LANES - 1, LANES), first, acc[2 * part]))
            new.append(jnp.where(lane == 2 * c, last, acc[2 * part + 1]))
        return tuple(new)

    zero_edge = jnp.zeros((planes, LANES), jnp.float32)
    packed = lax.fori_loop(0, cells, pack, (zero_edge,) * 4, unroll=4)
    for part in range(2):
        edge[0, part] = packed[2 * part]
        edge[1, part] = packed[2 * part + 1]

    down = pltpu.make_async_remote_copy(edge.at[0], halo.at[1], hs_sem.at[0], hr_sem.at[1],
                                        device_id={"gy": gy - 1}, device_id_type=MESH)
    up = pltpu.make_async_remote_copy(edge.at[1], halo.at[0], hs_sem.at[1], hr_sem.at[0],
                                      device_id={"gy": gy + 1}, device_id_type=MESH)

    @pl.when(gy > 0)
    def _():
        down.start()

    @pl.when(gy == 0)
    def _():
        halo[0] = jnp.zeros(halo.shape[1:], jnp.float32)

    @pl.when(gy < wide - 1)
    def _():
        up.start()

    @pl.when(gy == wide - 1)
    def _():
        halo[1] = jnp.zeros(halo.shape[1:], jnp.float32)

    col = lax.broadcasted_iota(jnp.int32, (planes, lines), 1)
    row = lax.broadcasted_iota(jnp.int32, (planes, lines), 0)
    at_first, at_last = col == 0, col == lines - 1
    at_bottom, at_top = row == 0, row == planes - 1

    def lap(x, first, last):
        left = jnp.where(at_first, first, pltpu.roll(x, 1, 1))
        right = jnp.where(at_last, last, pltpu.roll(x, lines - 1, 1))
        below = jnp.where(at_bottom, 0.0, pltpu.roll(x, 1, 0))
        above = jnp.where(at_top, 0.0, pltpu.roll(x, planes - 1, 0))
        return ((left + right) + (below + above)) - 4.0 * x

    def stencil(re, im, first, last):
        lap_re = lap(re, first[0], last[0])
        lap_im = lap(im, first[1], last[1])
        return 2.0 * re - RYZ * lap_im, 2.0 * im + RYZ * lap_re

    def fill(i, unused):
        part = pl.ds(i * group, group)
        laps = []
        for p in range(2):
            x = turned[p, part].reshape(group * planes, lines)
            high = x.astype(jnp.bfloat16)
            low = (x - high.astype(jnp.float32)).astype(jnp.bfloat16)
            y = (jnp.dot(high, band[...], preferred_element_type=jnp.float32)
                 + jnp.dot(low, band[...], preferred_element_type=jnp.float32))
            laps.append(y.reshape(group, planes, lines))
        for n in range(group):
            c = i * group + n
            lap_of = []
            for p in range(2):
                x = turned[p, c]
                below = jnp.where(at_bottom, 0.0, pltpu.roll(x, 1, 0))
                above = jnp.where(at_top, 0.0, pltpu.roll(x, planes - 1, 0))
                lap_of.append(laps[p][n] + (below + above))
            rho[0, c] = -inv * (2.0 * turned[1, c] + RYZ * lap_of[0])
            rho[1, c] = inv * (2.0 * turned[0, c] - RYZ * lap_of[1])
        return unused

    group = chunk
    lax.fori_loop(0, cells // group, fill, 0)

    @pl.loop(0, count - 1 - gx)
    def _(i):
        peer = gx + 1 + i
        pl.semaphore_wait(ready.at[peer], 1 + beyond)
        message(peer).start()
        rims(peer, begin)

    @pl.when(not_low)
    def _():
        up.wait_recv()

    @pl.when(not_high)
    def _():
        down.wait_recv()

    wanted = [(inv * RYZ) * (halo[0, p] + halo[1, p]) for p in range(2)]

    def mend(c, unused):
        for p in range(2):
            h = pltpu.roll(wanted[p], LANES - 2 * c, 1)
            for side, at in enumerate((0, lines - LANES)):
                old = rho[p, c, :, at : at + LANES]
                rho[p, c, :, at : at + LANES] = jnp.where(lane == side * (LANES - 1), old - h, old)
        return unused

    lax.fori_loop(0, cells, mend, 0, unroll=8)

    def arrival(k):
        return pltpu.make_async_remote_copy(
            fr.at[0], recv.at[k], s_sem.at[k], r_sem.at[k],
            device_id={"gx": k}, device_id_type=MESH)

    def rim_arrival(k, side):
        return pltpu.make_async_remote_copy(
            rim.at[0, 0], beside.at[side, k], es_sem.at[side, k], er_sem.at[side, k],
            device_id={"gx": k, "gy": gy - 1 + 2 * side}, device_id_type=MESH)

    zero_rim = jnp.zeros((1, LANES), jnp.float32)

    @pl.when(gy == 0)
    def _():
        beside[0] = jnp.zeros(beside.shape[1:], jnp.float32)

    @pl.when(gy == wide - 1)
    def _():
        beside[1] = jnp.zeros(beside.shape[1:], jnp.float32)

    def take_rim(k, acc):
        @pl.when(gy > 0)
        def _():
            rim_arrival(k, 0).wait_recv()

        @pl.when(gy < wide - 1)
        def _():
            rim_arrival(k, 1).wait_recv()

        return acc[0] + beside[0, k], acc[1] + beside[1, k]

    def take(k, acc):
        arrival(k).wait_recv()
        return (acc[0] + recv[k, 0], acc[1] + recv[k, 1]) + take_rim(k, acc[2:])

    @pl.loop(0, count)
    def _(peer):
        @pl.when(peer != gx)
        def _():
            message(peer).wait_send()

        rims(peer, end)

    @pl.when(not_low)
    def _():
        down.wait_send()

    @pl.when(not_high)
    def _():
        up.wait_send()

    left = lax.fori_loop(0, gx, take, (zero, zero, zero_rim, zero_rim))
    right = (fr[1, 0], fr[1, 1]) + take_rim(gx, (zero_rim, zero_rim))
    right = lax.fori_loop(gx + 1, count, take, right)

    def spread(total):
        columns = []
        for tile in total[2:]:
            columns.append(tuple(
                jnp.sum(jnp.where(row_rim == part * planes, tile, 0.0), axis=1, keepdims=True) for part in range(2)))
        return stencil(total[0], total[1], columns[0], columns[1])

    left = spread(left)
    right = spread(right)
    w = both(scalar(4), left, scalar(5), right)
    d = both(scalar(6), left, scalar(7), right)

    for index, value in enumerate(w + d):
        start[index] = value


def finish(coef, chunk, turned, rho, start, out, out_v, out_sem):
    cells = turned.shape[1]
    chunks = cells // chunk
    inv = np.float32(1.0 / coef)

    def store(i):
        part = pl.ds(i * chunk, chunk)
        return pltpu.make_async_copy(out_v.at[:, part], out.at[:, part], out_sem.at[i])

    def march(c, carry):
        w_re, w_im, d_re, d_im = carry
        w_re = w_re + d_re
        w_im = w_im + d_im
        out_v[0, c] = w_re - turned[0, c]
        out_v[1, c] = w_im - turned[1, c]
        d_re = d_re + (rho[0, c] + inv * w_im)
        d_im = d_im + (rho[1, c] - inv * w_re)
        return w_re, w_im, d_re, d_im

    carry = (start[0], start[1], start[2], start[3])
    for i in range(chunks):
        carry = lax.fori_loop(i * chunk, (i + 1) * chunk, march, carry, unroll=4)
        store(i).start()
    for i in range(chunks):
        store(i).wait()


def shards(psi, potential):
    unused, cells, planes, lines = psi.shape
    count = lax.axis_size("gx")
    wide = lax.axis_size("gy")
    place, coef = tables(cells, count)
    chunk = 8 if cells % 8 == 0 else cells
    chunks = cells // chunk
    block = (2, cells, planes, lines)
    plane = (planes, lines)
    vmem = pl.BlockSpec(memory_space=pltpu.VMEM)
    held = pl.pallas_call(
        functools.partial(kernel, count, wide, coef, chunk),
        out_shape=[
            jax.ShapeDtypeStruct(block, jnp.float32),
            jax.ShapeDtypeStruct(block, jnp.float32),
            jax.ShapeDtypeStruct((4,) + plane, jnp.float32),
        ],
        in_specs=[
            pl.BlockSpec(memory_space=pltpu.HBM),
            pl.BlockSpec(memory_space=pltpu.HBM),
            pl.BlockSpec(memory_space=pltpu.HBM),
        ],
        out_specs=[vmem] * 3,
        scratch_shapes=[
            pltpu.SMEM(place.shape, jnp.float32),
            pltpu.SemaphoreType.DMA((1,)),
            pltpu.VMEM(block, jnp.float32),
            pltpu.VMEM(block[1:], jnp.float32),
            pltpu.VMEM((2, 2, planes, LANES), jnp.float32),
            pltpu.VMEM((2, 2, planes, LANES), jnp.float32),
            pltpu.VMEM((2, 2) + plane, jnp.float32),
            pltpu.VMEM((count, 2) + plane, jnp.float32),
            pltpu.SemaphoreType.DMA((2, chunks)),
            pltpu.SemaphoreType.DMA((2,)),
            pltpu.SemaphoreType.DMA((2,)),
            pltpu.SemaphoreType.DMA((count,)),
            pltpu.SemaphoreType.DMA((count,)),
            pltpu.VMEM((2, 2, 1, LANES), jnp.float32),
            pltpu.VMEM((2, count, 1, LANES), jnp.float32),
            pltpu.SemaphoreType.DMA((2, count)),
            pltpu.SemaphoreType.DMA((2, count)),
            pltpu.VMEM((lines, lines), jnp.bfloat16),
            pltpu.SemaphoreType.REGULAR((count,)),
        ],
        compiler_params=pltpu.CompilerParams(
            collective_id=0, has_side_effects=True, vmem_limit_bytes=24 * 2**20
        ),
    )(*(pltpu.with_memory_space_constraint(x, pltpu.HBM) for x in
        (psi, potential, jnp.asarray(place))))
    return pl.pallas_call(
        functools.partial(finish, coef, chunk),
        out_shape=jax.ShapeDtypeStruct(block, jnp.float32),
        in_specs=[vmem] * 3,
        out_specs=pl.BlockSpec(memory_space=pl.ANY),
        scratch_shapes=[
            pltpu.VMEM(block, jnp.float32),
            pltpu.SemaphoreType.DMA((chunks,)),
        ],
        compiler_params=pltpu.CompilerParams(vmem_limit_bytes=16 * 2**20),
    )(*held)


def solution(mesh):
    return jax.shard_map(
        shards,
        mesh=mesh,
        in_specs=(P(None, "gx", None, "gy"), P("gx", None, "gy")),
        out_specs=P(None, "gx", None, "gy"),
        check_vma=False,
    )
```

```python
import functools

import jax
import jax.numpy as jnp
import numpy as np
from jax import lax
from jax.experimental import pallas as pl
from jax.experimental.pallas import tpu as pltpu
from jax.sharding import PartitionSpec as P

RYZ = 2.0
LANES = 128
MESH = pl.DeviceIdType.MESH


def tables(cells, count):
    coef = 256.0 * cells * cells
    total = cells * count
    lam = np.arccosh(np.complex128(1.0 - 0.5j / coef))
    sh = lambda m: np.sinh(lam * m)
    scale = -(1j / coef) / (sh(1) * sh(total + 1))
    x0 = cells * np.arange(count, dtype=np.float64)
    end = x0 + cells
    f_q = sh(end) - sh(end + 1)
    f_e = sh(end + 1)
    r_q = sh(total + 1 - end) - sh(total - end)
    r_e = sh(total - end)
    w_l = scale * sh(total + 1 - x0)
    w_r = scale * sh(x0)
    d_l = scale * (sh(total - x0) - sh(total + 1 - x0))
    d_r = scale * (sh(x0 + 1) - sh(x0))
    rows = [f_q, f_e, r_q, r_e, w_l, w_r, d_l, d_r]
    place = np.stack([part for row in rows for part in (row.real, row.imag)], axis=1)
    return place.astype(np.float32).reshape(-1), coef


HALF_SINE = (4.442882834149953, -7.308241154547353, 3.6062889582396482, -0.8457635962213053, 0.10920575376953141)
HALF_COSINE = (1.4142134965650301, -6.9788509882409375, 5.739461170721302, -1.883562987555641, 0.3106981923194725)


def turn(re, im, pot):
    t = (pot + re * re + im * im) * np.float32(0.25 / np.pi)
    f = t - jnp.round(t)
    f2 = f * f
    s = np.float32(HALF_SINE[-1])
    for a in HALF_SINE[-2::-1]:
        s = s * f2 + np.float32(a)
    s = s * f
    c = np.float32(HALF_COSINE[-1])
    for a in HALF_COSINE[-2::-1]:
        c = c * f2 + np.float32(a)
    sine = s * c
    cosine = 1.0 - s * s
    return re * cosine + im * sine, im * cosine - re * sine


def kernel(count, wide, coef, chunk, psi, pot, place_in, turned, rho,
           start, place_ref, table_sem, psi_v, pot_v, edge, halo, fr, recv, in_sem, hs_sem, hr_sem, s_sem, r_sem,
           rim, beside, es_sem, er_sem, band, ready, relay, rim_sum, twin, t_sem, total):
    cells, planes, lines = pot_v.shape
    chunks = cells // chunk
    gx = lax.axis_index("gx")
    gy = lax.axis_index("gy")
    inv = np.float32(1.0 / coef)

    def load(i):
        part = pl.ds(i * chunk, chunk)
        return (
            pltpu.make_async_copy(psi.at[:, part], psi_v.at[:, part], in_sem.at[0, i]),
            pltpu.make_async_copy(pot.at[part], pot_v.at[part], in_sem.at[1, i]),
        )

    for i in range(chunks):
        for copy in load(i):
            copy.start()

    table = pltpu.make_async_copy(place_in, place_ref, table_sem.at[0])
    table.start()

    barrier = pltpu.get_barrier_semaphore()
    not_low, not_high = gy > 0, gy < wide - 1
    beyond = jnp.where(not_low, 1, 0) + jnp.where(not_high, 1, 0)

    def beside_do(do):
        @pl.when(not_low)
        def _():
            do(gy - 1)

        @pl.when(not_high)
        def _():
            do(gy + 1)

    def greet(x, y):
        pl.semaphore_signal(barrier, inc=1, device_id={"gx": x, "gy": y}, device_id_type=MESH)

    beside_do(lambda y: greet(gx, y))

    @pl.loop(gx + 1, count)
    def _(k):
        greet(k, gy)
        beside_do(lambda y: greet(k, y))

    across = lax.broadcasted_iota(jnp.int32, (lines, lines), 0) - lax.broadcasted_iota(jnp.int32, (lines, lines), 1)
    band[...] = jnp.where(across == 0, -4.0, jnp.where(jnp.abs(across) == 1, 1.0, 0.0)).astype(jnp.bfloat16)

    def tell(x, y):
        pl.semaphore_signal(ready.at[jnp.where(y == gy, 0, 1), gx], inc=1, device_id={"gx": x, "gy": y},
                            device_id_type=MESH)

    def meet():
        pl.semaphore_wait(barrier, gx * (1 + beyond) + beyond)

        @pl.loop(0, gx)
        def _(k):
            tell(k, gy)
            beside_do(lambda y: tell(k, y))

    def advance(c, carry):
        e_re, e_im, q_re, q_im = carry
        t_re, t_im = turn(psi_v[0, c], psi_v[1, c], pot_v[c])
        turned[0, c] = t_re
        turned[1, c] = t_im
        e_re = e_re + (t_re + inv * q_im)
        e_im = e_im + (t_im - inv * q_re)
        return e_re, e_im, q_re + e_re, q_im + e_im

    zero = jnp.zeros((planes, lines), jnp.float32)
    carry = (zero,) * 4
    pl.when(lax.rem(gy, 2) == 0)(meet)
    for i in range(chunks):
        for copy in load(i):
            copy.wait()
        carry = lax.fori_loop(i * chunk, (i + 1) * chunk, advance, carry, unroll=4)
        if i == chunks - 1:
            pl.when(lax.rem(gy, 2) == 1)(meet)
    e_re, e_im, q_re, q_im = carry

    table.wait()

    def scalar(index):
        return place_ref[gx * 16 + 2 * index], place_ref[gx * 16 + 2 * index + 1]

    def both(a, x, b, y):
        return (
            (a[0] * x[0] - a[1] * x[1]) + (b[0] * y[0] - b[1] * y[1]),
            (a[0] * x[1] + a[1] * x[0]) + (b[0] * y[1] + b[1] * y[0]),
        )

    lane = lax.broadcasted_iota(jnp.int32, (planes, LANES), 1)
    row_rim = lane - lax.broadcasted_iota(jnp.int32, (planes, LANES), 0)

    def interface(which):
        value = both(scalar(2 * which), (q_re, q_im), scalar(2 * which + 1), (e_re, e_im))
        fr[which, 0] = value[0]
        fr[which, 1] = value[1]
        for side in range(2):
            at = side * (lines - 1)
            tile = jnp.where(row_rim == 0, value[0][:, at : at + 1],
                             jnp.where(row_rim == planes, value[1][:, at : at + 1], 0.0))
            rim[which, side] = jnp.sum(tile, axis=0, keepdims=True)

    half = count // 2
    split = count >= 8 and count % 4 == 0
    odd = lax.rem(gy, 2) == 1

    def by_hub(peer):
        if not split:
            return peer < 0
        return ((gx < half) & (peer >= half)) | ((gx >= half) & (peer >= 2) & (peer < half) & odd)

    def message(peer):
        return pltpu.make_async_remote_copy(
            fr.at[jnp.where(peer < gx, 1, 0)], recv.at[gx], s_sem.at[peer], r_sem.at[gx],
            device_id={"gx": peer}, device_id_type=MESH)

    def hub_message(which, peer):
        return pltpu.make_async_remote_copy(
            relay.at[which], recv.at[gx], s_sem.at[peer], r_sem.at[gx],
            device_id={"gx": peer}, device_id_type=MESH)

    def twin_message(which, peer):
        return pltpu.make_async_remote_copy(
            fr.at[which], twin, t_sem.at[0], t_sem.at[1],
            device_id={"gx": peer}, device_id_type=MESH)

    def hub_do(which, do):
        parity = lax.rem(gx, 2)

        @pl.loop(0, half // 2 - which)
        def _(n):
            do(hub_message(which, (half if which == 0 else 2) + 2 * n + parity))

    def rim_message(peer, side):
        return pltpu.make_async_remote_copy(
            rim.at[jnp.where(peer <= gx, 1, 0), side], beside.at[1 - side, gx],
            es_sem.at[side, peer], er_sem.at[1 - side, gx],
            device_id={"gx": peer, "gy": gy - 1 + 2 * side}, device_id_type=MESH)

    def rims(peer, do):
        @pl.when(not_low)
        def _():
            do(rim_message(peer, 0))

        @pl.when(not_high)
        def _():
            do(rim_message(peer, 1))

    def begin(copy):
        copy.start()

    def end(copy):
        copy.wait_send()

    interface(1)
    urgent = jnp.minimum(gx, 2)

    @pl.loop(0, urgent)
    def _(peer):
        rims(peer, begin)

    @pl.loop(0, urgent)
    def _(peer):
        message(peer).start()

    @pl.loop(urgent, gx + 1)
    def _(peer):
        rims(peer, begin)

    @pl.loop(urgent, gx)
    def _(peer):
        @pl.when(jnp.logical_not(by_hub(peer)))
        def _():
            message(peer).start()

    interface(0)

    def pack(c, acc):
        new = []
        for part in range(2):
            src = turned.at[part, c]
            first = src[:, 0:LANES][:, 0:1]
            last = src[:, lines - LANES : lines][:, LANES - 1 : LANES]
            new.append(jnp.where(lane == lax.rem(2 * c + LANES - 1, LANES), first, acc[2 * part]))
            new.append(jnp.where(lane == 2 * c, last, acc[2 * part + 1]))
        return tuple(new)

    zero_edge = jnp.zeros((planes, LANES), jnp.float32)
    packed = lax.fori_loop(0, cells, pack, (zero_edge,) * 4, unroll=4)
    for part in range(2):
        edge[0, part] = packed[2 * part]
        edge[1, part] = packed[2 * part + 1]

    down = pltpu.make_async_remote_copy(edge.at[0], halo.at[1], hs_sem.at[0], hr_sem.at[1],
                                        device_id={"gy": gy - 1}, device_id_type=MESH)
    up = pltpu.make_async_remote_copy(edge.at[1], halo.at[0], hs_sem.at[1], hr_sem.at[0],
                                      device_id={"gy": gy + 1}, device_id_type=MESH)

    @pl.when(gy > 0)
    def _():
        down.start()

    @pl.when(gy == 0)
    def _():
        halo[0] = jnp.zeros(halo.shape[1:], jnp.float32)

    @pl.when(gy < wide - 1)
    def _():
        up.start()

    @pl.when(gy == wide - 1)
    def _():
        halo[1] = jnp.zeros(halo.shape[1:], jnp.float32)

    col = lax.broadcasted_iota(jnp.int32, (planes, lines), 1)
    row = lax.broadcasted_iota(jnp.int32, (planes, lines), 0)
    at_first, at_last = col == 0, col == lines - 1
    at_bottom, at_top = row == 0, row == planes - 1

    def lap(x, first, last):
        left = jnp.where(at_first, first, pltpu.roll(x, 1, 1))
        right = jnp.where(at_last, last, pltpu.roll(x, lines - 1, 1))
        below = jnp.where(at_bottom, 0.0, pltpu.roll(x, 1, 0))
        above = jnp.where(at_top, 0.0, pltpu.roll(x, planes - 1, 0))
        return ((left + right) + (below + above)) - 4.0 * x

    def stencil(re, im, first, last):
        lap_re = lap(re, first[0], last[0])
        lap_im = lap(im, first[1], last[1])
        return 2.0 * re - RYZ * lap_im, 2.0 * im + RYZ * lap_re

    def fill(i, unused):
        part = pl.ds(i * group, group)
        laps = []
        for p in range(2):
            x = turned[p, part].reshape(group * planes, lines)
            high = x.astype(jnp.bfloat16)
            low = (x - high.astype(jnp.float32)).astype(jnp.bfloat16)
            y = (jnp.dot(high, band[...], preferred_element_type=jnp.float32)
                 + jnp.dot(low, band[...], preferred_element_type=jnp.float32))
            laps.append(y.reshape(group, planes, lines))
        for n in range(group):
            c = i * group + n
            lap_of = []
            for p in range(2):
                x = turned[p, c]
                below = jnp.where(at_bottom, 0.0, pltpu.roll(x, 1, 0))
                above = jnp.where(at_top, 0.0, pltpu.roll(x, planes - 1, 0))
                lap_of.append(laps[p][n] + (below + above))
            rho[0, c] = -inv * (2.0 * turned[1, c] + RYZ * lap_of[0])
            rho[1, c] = inv * (2.0 * turned[0, c] - RYZ * lap_of[1])
        return unused

    group = chunk
    lax.fori_loop(0, cells // group, fill, 0)

    @pl.loop(0, count - 1 - gx)
    def _(i):
        peer = gx + 1 + i
        pl.semaphore_wait(ready.at[0, peer], 1)

        @pl.when(jnp.logical_not(by_hub(peer)))
        def _():
            message(peer).start()

    if split:
        @pl.when((gx == half) & odd)
        def _():
            twin_message(1, half + 1).start()

        @pl.when(gx == half - 1)
        def _():
            twin_message(0, half - 2).start()

    @pl.loop(gx + 1, count)
    def _(peer):
        pl.semaphore_wait(ready.at[1, peer], beyond)
        rims(peer, begin)

    @pl.when(not_low)
    def _():
        up.wait_recv()

    @pl.when(not_high)
    def _():
        down.wait_recv()

    wanted = [(inv * RYZ) * (halo[0, p] + halo[1, p]) for p in range(2)]

    def mend(c, unused):
        for p in range(2):
            h = pltpu.roll(wanted[p], LANES - 2 * c, 1)
            for side, at in enumerate((0, lines - LANES)):
                old = rho[p, c, :, at : at + LANES]
                rho[p, c, :, at : at + LANES] = jnp.where(lane == side * (LANES - 1), old - h, old)
        return unused

    lax.fori_loop(0, cells, mend, 0, unroll=8)

    def arrival(k):
        return pltpu.make_async_remote_copy(
            fr.at[0], recv.at[k], s_sem.at[k], r_sem.at[k],
            device_id={"gx": k}, device_id_type=MESH)

    def rim_arrival(k, side):
        return pltpu.make_async_remote_copy(
            rim.at[0, 0], beside.at[side, k], es_sem.at[side, k], er_sem.at[side, k],
            device_id={"gx": k, "gy": gy - 1 + 2 * side}, device_id_type=MESH)

    zero_rim = jnp.zeros((1, LANES), jnp.float32)

    @pl.when(gy == 0)
    def _():
        beside[0] = jnp.zeros(beside.shape[1:], jnp.float32)

    @pl.when(gy == wide - 1)
    def _():
        beside[1] = jnp.zeros(beside.shape[1:], jnp.float32)

    def take_rim(k, acc):
        @pl.when(gy > 0)
        def _():
            rim_arrival(k, 0).wait_recv()

        @pl.when(gy < wide - 1)
        def _():
            rim_arrival(k, 1).wait_recv()

        return acc[0] + beside[0, k], acc[1] + beside[1, k]

    @pl.loop(0, count)
    def _(peer):
        @pl.when((peer != gx) & jnp.logical_not(by_hub(peer)))
        def _():
            message(peer).wait_send()

        rims(peer, end)

    @pl.when(not_low)
    def _():
        down.wait_send()

    @pl.when(not_high)
    def _():
        up.wait_send()

    def take(k, acc):
        arrival(k).wait_recv()
        return acc[0] + recv[k, 0], acc[1] + recv[k, 1]

    def sum_rims():
        for n, total in enumerate(lax.fori_loop(0, gx, take_rim, (zero_rim, zero_rim))
                                  + lax.fori_loop(gx, count, take_rim, (zero_rim, zero_rim))):
            rim_sum[n] = total

    def keep(which, value):
        total[which, 0] = value[0]
        total[which, 1] = value[1]

    def pass_on(which, value):
        relay[which, 0] = value[0]
        relay[which, 1] = value[1]
        hub_do(which, begin)

    def take_twin(value):
        twin_message(0, gx).wait_recv()
        return value[0] + twin[0], value[1] + twin[1]

    def take_left():
        if not split:
            keep(0, lax.fori_loop(0, gx, take, (zero, zero)))
            return
        above = gx >= half
        value = lax.fori_loop(jnp.where(above, half, 0), gx, take, (zero, zero))
        hub = half - 2 + lax.rem(gx, 2)
        value = lax.fori_loop(hub, hub + jnp.where(above, 1, 0), take, value)
        keep(0, value)
        value = value[0] + fr[0, 0], value[1] + fr[0, 1]

        @pl.when(gx == half - 1)
        def _():
            pass_on(0, value)

        @pl.when(gx == half - 2)
        def _():
            pass_on(0, take_twin(value))

    def take_right():
        own = (fr[1, 0], fr[1, 1])
        if not split:
            keep(1, lax.fori_loop(gx + 1, count, take, own))
            return
        between = (gx >= 2) & (gx < half) & odd
        value = lax.fori_loop(gx + 1, jnp.where(between, half, count), take, own)
        hub = half + lax.rem(gx, 2)
        value = lax.fori_loop(hub, hub + jnp.where(between, 1, 0), take, value)
        keep(1, value)

        @pl.when((gx == half) & odd)
        def _():
            pass_on(1, value)

        @pl.when((gx == half + 1) & odd)
        def _():
            pass_on(1, take_twin(value))

    is_hub = (gx >= half - 2) & (gx < half + 2) & split
    pl.when(jnp.logical_not(is_hub))(sum_rims)
    pl.when(gx < half)(take_left)
    take_right()
    pl.when(gx >= half)(take_left)
    pl.when(is_hub)(sum_rims)
    left = (total[0, 0], total[0, 1], rim_sum[0], rim_sum[1])
    right = (total[1, 0], total[1, 1], rim_sum[2], rim_sum[3])

    def spread(side):
        columns = []
        for tile in side[2:]:
            columns.append(tuple(
                jnp.sum(jnp.where(row_rim == part * planes, tile, 0.0), axis=1, keepdims=True) for part in range(2)))
        return stencil(side[0], side[1], columns[0], columns[1])

    left = spread(left)
    right = spread(right)
    w = both(scalar(4), left, scalar(5), right)
    d = both(scalar(6), left, scalar(7), right)

    for index, value in enumerate(w + d):
        start[index] = value

    if split:
        pl.when((gx == half - 2) | (gx == half - 1))(lambda: hub_do(0, end))
        pl.when(((gx == half) | (gx == half + 1)) & odd)(lambda: hub_do(1, end))

        @pl.when((gx == half - 1) | ((gx == half) & odd))
        def _():
            twin_message(0, gx).wait_send()


def finish(coef, chunk, turned, rho, start, out, out_v, out_sem):
    cells = turned.shape[1]
    chunks = cells // chunk
    inv = np.float32(1.0 / coef)

    def store(i):
        part = pl.ds(i * chunk, chunk)
        return pltpu.make_async_copy(out_v.at[:, part], out.at[:, part], out_sem.at[i])

    def march(c, carry):
        w_re, w_im, d_re, d_im = carry
        w_re = w_re + d_re
        w_im = w_im + d_im
        out_v[0, c] = w_re - turned[0, c]
        out_v[1, c] = w_im - turned[1, c]
        d_re = d_re + (rho[0, c] + inv * w_im)
        d_im = d_im + (rho[1, c] - inv * w_re)
        return w_re, w_im, d_re, d_im

    carry = (start[0], start[1], start[2], start[3])
    for i in range(chunks):
        carry = lax.fori_loop(i * chunk, (i + 1) * chunk, march, carry, unroll=4)
        store(i).start()
    for i in range(chunks):
        store(i).wait()


def shards(psi, potential):
    unused, cells, planes, lines = psi.shape
    count = lax.axis_size("gx")
    wide = lax.axis_size("gy")
    place, coef = tables(cells, count)
    chunk = 8 if cells % 8 == 0 else cells
    chunks = cells // chunk
    block = (2, cells, planes, lines)
    plane = (planes, lines)
    vmem = pl.BlockSpec(memory_space=pltpu.VMEM)
    held = pl.pallas_call(
        functools.partial(kernel, count, wide, coef, chunk),
        out_shape=[
            jax.ShapeDtypeStruct(block, jnp.float32),
            jax.ShapeDtypeStruct(block, jnp.float32),
            jax.ShapeDtypeStruct((4,) + plane, jnp.float32),
        ],
        in_specs=[
            pl.BlockSpec(memory_space=pltpu.HBM),
            pl.BlockSpec(memory_space=pltpu.HBM),
            pl.BlockSpec(memory_space=pltpu.HBM),
        ],
        out_specs=[vmem] * 3,
        scratch_shapes=[
            pltpu.SMEM(place.shape, jnp.float32),
            pltpu.SemaphoreType.DMA((1,)),
            pltpu.VMEM(block, jnp.float32),
            pltpu.VMEM(block[1:], jnp.float32),
            pltpu.VMEM((2, 2, planes, LANES), jnp.float32),
            pltpu.VMEM((2, 2, planes, LANES), jnp.float32),
            pltpu.VMEM((2, 2) + plane, jnp.float32),
            pltpu.VMEM((count, 2) + plane, jnp.float32),
            pltpu.SemaphoreType.DMA((2, chunks)),
            pltpu.SemaphoreType.DMA((2,)),
            pltpu.SemaphoreType.DMA((2,)),
            pltpu.SemaphoreType.DMA((count,)),
            pltpu.SemaphoreType.DMA((count,)),
            pltpu.VMEM((2, 2, 1, LANES), jnp.float32),
            pltpu.VMEM((2, count, 1, LANES), jnp.float32),
            pltpu.SemaphoreType.DMA((2, count)),
            pltpu.SemaphoreType.DMA((2, count)),
            pltpu.VMEM((lines, lines), jnp.bfloat16),
            pltpu.SemaphoreType.REGULAR((2, count)),
            pltpu.VMEM((2, 2) + plane, jnp.float32),
            pltpu.VMEM((4, 1, LANES), jnp.float32),
            pltpu.VMEM((2,) + plane, jnp.float32),
            pltpu.SemaphoreType.DMA((2,)),
            pltpu.VMEM((2, 2) + plane, jnp.float32),
        ],
        compiler_params=pltpu.CompilerParams(
            collective_id=0, has_side_effects=True, vmem_limit_bytes=24 * 2**20
        ),
    )(*(pltpu.with_memory_space_constraint(x, pltpu.HBM) for x in
        (psi, potential, jnp.asarray(place))))
    return pl.pallas_call(
        functools.partial(finish, coef, chunk),
        out_shape=jax.ShapeDtypeStruct(block, jnp.float32),
        in_specs=[vmem] * 3,
        out_specs=pl.BlockSpec(memory_space=pl.ANY),
        scratch_shapes=[
            pltpu.VMEM(block, jnp.float32),
            pltpu.SemaphoreType.DMA((chunks,)),
        ],
        compiler_params=pltpu.CompilerParams(vmem_limit_bytes=16 * 2**20),
    )(*held)


def solution(mesh):
    return jax.shard_map(
        shards,
        mesh=mesh,
        in_specs=(P(None, "gx", None, "gy"), P("gx", None, "gy")),
        out_specs=P(None, "gx", None, "gy"),
        check_vma=False,
    )
```

```python
import functools

import jax
import jax.numpy as jnp
import numpy as np
from jax import lax
from jax.experimental import pallas as pl
from jax.experimental.pallas import tpu as pltpu
from jax.sharding import PartitionSpec as P

RYZ = 2.0
LANES = 128
MESH = pl.DeviceIdType.MESH


def tables(cells, count):
    coef = 256.0 * cells * cells
    total = cells * count
    lam = np.arccosh(np.complex128(1.0 - 0.5j / coef))
    sh = lambda m: np.sinh(lam * m)
    scale = -(1j / coef) / (sh(1) * sh(total + 1))
    x0 = cells * np.arange(count, dtype=np.float64)
    end = x0 + cells
    f_q = sh(end) - sh(end + 1)
    f_e = sh(end + 1)
    r_q = sh(total + 1 - end) - sh(total - end)
    r_e = sh(total - end)
    w_l = scale * sh(total + 1 - x0)
    w_r = scale * sh(x0)
    d_l = scale * (sh(total - x0) - sh(total + 1 - x0))
    d_r = scale * (sh(x0 + 1) - sh(x0))
    rows = [f_q, f_e, r_q, r_e, w_l, w_r, d_l, d_r]
    place = np.stack([part for row in rows for part in (row.real, row.imag)], axis=1)
    return place.astype(np.float32).reshape(-1), coef


HALF_SINE = (4.442882834149953, -7.308241154547353, 3.6062889582396482, -0.8457635962213053, 0.10920575376953141)
HALF_COSINE = (1.4142134965650301, -6.9788509882409375, 5.739461170721302, -1.883562987555641, 0.3106981923194725)


def turn(re, im, pot):
    t = (pot + re * re + im * im) * np.float32(0.25 / np.pi)
    f = t - jnp.round(t)
    f2 = f * f
    s = np.float32(HALF_SINE[-1])
    for a in HALF_SINE[-2::-1]:
        s = s * f2 + np.float32(a)
    s = s * f
    c = np.float32(HALF_COSINE[-1])
    for a in HALF_COSINE[-2::-1]:
        c = c * f2 + np.float32(a)
    sine = s * c
    cosine = 1.0 - s * s
    return re * cosine + im * sine, im * cosine - re * sine


def kernel(count, wide, coef, chunk, psi, pot, place_in, turned, rho,
           start, place_ref, table_sem, psi_v, pot_v, edge, halo, fr, recv, in_sem, hs_sem, hr_sem, s_sem, r_sem,
           rim, beside, es_sem, er_sem, band, ready, relay, rim_sum, twin, t_sem, total):
    cells, planes, lines = pot_v.shape
    chunks = cells // chunk
    gx = lax.axis_index("gx")
    gy = lax.axis_index("gy")
    inv = np.float32(1.0 / coef)

    def load(i):
        part = pl.ds(i * chunk, chunk)
        return (
            pltpu.make_async_copy(psi.at[:, part], psi_v.at[:, part], in_sem.at[0, i]),
            pltpu.make_async_copy(pot.at[part], pot_v.at[part], in_sem.at[1, i]),
        )

    for i in range(chunks):
        for copy in load(i):
            copy.start()

    table = pltpu.make_async_copy(place_in, place_ref, table_sem.at[0])
    table.start()

    barrier = pltpu.get_barrier_semaphore()
    not_low, not_high = gy > 0, gy < wide - 1
    beyond = jnp.where(not_low, 1, 0) + jnp.where(not_high, 1, 0)

    def beside_do(do):
        @pl.when(not_low)
        def _():
            do(gy - 1)

        @pl.when(not_high)
        def _():
            do(gy + 1)

    def greet(x, y):
        pl.semaphore_signal(barrier, inc=1, device_id={"gx": x, "gy": y}, device_id_type=MESH)

    beside_do(lambda y: greet(gx, y))

    @pl.loop(gx + 1, count)
    def _(k):
        greet(k, gy)
        beside_do(lambda y: greet(k, y))

    across = lax.broadcasted_iota(jnp.int32, (lines, lines), 0) - lax.broadcasted_iota(jnp.int32, (lines, lines), 1)
    band[...] = jnp.where(across == 0, -4.0, jnp.where(jnp.abs(across) == 1, 1.0, 0.0)).astype(jnp.bfloat16)

    def tell(x, y):
        pl.semaphore_signal(ready.at[jnp.where(y == gy, 0, 1), gx], inc=1, device_id={"gx": x, "gy": y},
                            device_id_type=MESH)

    def meet():
        pl.semaphore_wait(barrier, gx * (1 + beyond) + beyond)

        @pl.loop(0, gx)
        def _(k):
            tell(k, gy)
            beside_do(lambda y: tell(k, y))

    def advance(c, carry):
        e_re, e_im, q_re, q_im = carry
        t_re, t_im = turn(psi_v[0, c], psi_v[1, c], pot_v[c])
        turned[0, c] = t_re
        turned[1, c] = t_im
        e_re = e_re + (t_re + inv * q_im)
        e_im = e_im + (t_im - inv * q_re)
        return e_re, e_im, q_re + e_re, q_im + e_im

    zero = jnp.zeros((planes, lines), jnp.float32)
    carry = (zero,) * 4
    pl.when(lax.rem(gy, 2) == 0)(meet)
    for i in range(chunks):
        for copy in load(i):
            copy.wait()
        carry = lax.fori_loop(i * chunk, (i + 1) * chunk, advance, carry, unroll=4)
        if i == chunks - 1:
            pl.when(lax.rem(gy, 2) == 1)(meet)
    e_re, e_im, q_re, q_im = carry

    table.wait()

    def scalar(index):
        return place_ref[gx * 16 + 2 * index], place_ref[gx * 16 + 2 * index + 1]

    def both(a, x, b, y):
        return (
            (a[0] * x[0] - a[1] * x[1]) + (b[0] * y[0] - b[1] * y[1]),
            (a[0] * x[1] + a[1] * x[0]) + (b[0] * y[1] + b[1] * y[0]),
        )

    lane = lax.broadcasted_iota(jnp.int32, (planes, LANES), 1)
    row_rim = lane - lax.broadcasted_iota(jnp.int32, (planes, LANES), 0)

    def interface(which):
        value = both(scalar(2 * which), (q_re, q_im), scalar(2 * which + 1), (e_re, e_im))
        fr[which, 0] = value[0]
        fr[which, 1] = value[1]
        for side in range(2):
            at = side * (lines - 1)
            tile = jnp.where(row_rim == 0, value[0][:, at : at + 1],
                             jnp.where(row_rim == planes, value[1][:, at : at + 1], 0.0))
            rim[which, side] = jnp.sum(tile, axis=0, keepdims=True)

    half = count // 2
    split = count >= 8 and count % 4 == 0
    odd = lax.rem(gy, 2) == 1

    def by_hub(peer):
        if not split:
            return peer < 0
        return ((gx < half) & (peer >= half)) | ((gx >= half) & (peer >= 2) & (peer < half) & odd)

    def message(peer):
        return pltpu.make_async_remote_copy(
            fr.at[jnp.where(peer < gx, 1, 0)], recv.at[gx], s_sem.at[peer], r_sem.at[gx],
            device_id={"gx": peer}, device_id_type=MESH)

    def hub_message(which, peer):
        return pltpu.make_async_remote_copy(
            relay.at[which], recv.at[gx], s_sem.at[peer], r_sem.at[gx],
            device_id={"gx": peer}, device_id_type=MESH)

    def twin_message(which, peer):
        return pltpu.make_async_remote_copy(
            fr.at[which], twin, t_sem.at[0], t_sem.at[1],
            device_id={"gx": peer}, device_id_type=MESH)

    def hub_do(which, do):
        parity = lax.rem(gx, 2)

        @pl.loop(0, half // 2 - which)
        def _(n):
            do(hub_message(which, (half if which == 0 else 2) + 2 * n + parity))

    def rim_message(peer, side):
        return pltpu.make_async_remote_copy(
            rim.at[jnp.where(peer <= gx, 1, 0), side], beside.at[1 - side, gx],
            es_sem.at[side, peer], er_sem.at[1 - side, gx],
            device_id={"gx": peer, "gy": gy - 1 + 2 * side}, device_id_type=MESH)

    def rims(peer, do):
        @pl.when(not_low)
        def _():
            do(rim_message(peer, 0))

        @pl.when(not_high)
        def _():
            do(rim_message(peer, 1))

    def begin(copy):
        copy.start()

    def end(copy):
        copy.wait_send()

    interface(1)
    def send_down(start, stop, but=lambda peer: peer < 0):
        @pl.loop(start, stop)
        def _(peer):
            @pl.when(jnp.logical_not(by_hub(peer) | but(peer)))
            def _():
                message(peer).start()

    urgent = jnp.minimum(gx, 2)

    @pl.loop(0, urgent)
    def _(peer):
        rims(peer, begin)

    if False:
        at_hubs = lambda peer: (gx >= half + 2) & (peer >= half) & (peer < half + 2)
    else:
        at_hubs = lambda peer: peer < 0

    @pl.when(odd)
    def _():
        if False:
            @pl.when(gx >= half + 2)
            def _():
                send_down(half, half + 2)
        send_down(0, gx, at_hubs)

    @pl.when(jnp.logical_not(odd))
    def _():
        send_down(0, jnp.minimum(gx, 1))

    @pl.loop(urgent, gx + 1)
    def _(peer):
        rims(peer, begin)

    interface(0)

    if split:
        @pl.when(gx == half - 1)
        def _():
            twin_message(0, half - 2).start()

    def pack(c, acc):
        new = []
        for part in range(2):
            src = turned.at[part, c]
            first = src[:, 0:LANES][:, 0:1]
            last = src[:, lines - LANES : lines][:, LANES - 1 : LANES]
            new.append(jnp.where(lane == lax.rem(2 * c + LANES - 1, LANES), first, acc[2 * part]))
            new.append(jnp.where(lane == 2 * c, last, acc[2 * part + 1]))
        return tuple(new)

    zero_edge = jnp.zeros((planes, LANES), jnp.float32)
    packed = lax.fori_loop(0, cells, pack, (zero_edge,) * 4, unroll=4)
    for part in range(2):
        edge[0, part] = packed[2 * part]
        edge[1, part] = packed[2 * part + 1]

    down = pltpu.make_async_remote_copy(edge.at[0], halo.at[1], hs_sem.at[0], hr_sem.at[1],
                                        device_id={"gy": gy - 1}, device_id_type=MESH)
    up = pltpu.make_async_remote_copy(edge.at[1], halo.at[0], hs_sem.at[1], hr_sem.at[0],
                                      device_id={"gy": gy + 1}, device_id_type=MESH)

    @pl.when(gy > 0)
    def _():
        down.start()

    @pl.when(gy == 0)
    def _():
        halo[0] = jnp.zeros(halo.shape[1:], jnp.float32)

    @pl.when(gy < wide - 1)
    def _():
        up.start()

    @pl.when(gy == wide - 1)
    def _():
        halo[1] = jnp.zeros(halo.shape[1:], jnp.float32)

    pl.when(jnp.logical_not(odd))(lambda: send_down(1, gx))

    near = jnp.where(gx < half, half, count) if split else count

    @pl.loop(gx + 1, near)
    def _(peer):
        pl.semaphore_wait(ready.at[0, peer], 1)
        message(peer).start()

    if split:
        @pl.when((gx == half) & odd)
        def _():
            twin_message(1, half + 1).start()

    col = lax.broadcasted_iota(jnp.int32, (planes, lines), 1)
    row = lax.broadcasted_iota(jnp.int32, (planes, lines), 0)
    at_first, at_last = col == 0, col == lines - 1
    at_bottom, at_top = row == 0, row == planes - 1

    def lap(x, first, last):
        left = jnp.where(at_first, first, pltpu.roll(x, 1, 1))
        right = jnp.where(at_last, last, pltpu.roll(x, lines - 1, 1))
        below = jnp.where(at_bottom, 0.0, pltpu.roll(x, 1, 0))
        above = jnp.where(at_top, 0.0, pltpu.roll(x, planes - 1, 0))
        return ((left + right) + (below + above)) - 4.0 * x

    def stencil(re, im, first, last):
        lap_re = lap(re, first[0], last[0])
        lap_im = lap(im, first[1], last[1])
        return 2.0 * re - RYZ * lap_im, 2.0 * im + RYZ * lap_re

    def fill(i, unused):
        part = pl.ds(i * group, group)
        laps = []
        for p in range(2):
            x = turned[p, part].reshape(group * planes, lines)
            high = x.astype(jnp.bfloat16)
            low = (x - high.astype(jnp.float32)).astype(jnp.bfloat16)
            y = (jnp.dot(high, band[...], preferred_element_type=jnp.float32)
                 + jnp.dot(low, band[...], preferred_element_type=jnp.float32))
            laps.append(y.reshape(group, planes, lines))
        for n in range(group):
            c = i * group + n
            lap_of = []
            for p in range(2):
                x = turned[p, c]
                below = jnp.where(at_bottom, 0.0, pltpu.roll(x, 1, 0))
                above = jnp.where(at_top, 0.0, pltpu.roll(x, planes - 1, 0))
                lap_of.append(laps[p][n] + (below + above))
            rho[0, c] = -inv * (2.0 * turned[1, c] + RYZ * lap_of[0])
            rho[1, c] = inv * (2.0 * turned[0, c] - RYZ * lap_of[1])
        return unused

    group = chunk
    lax.fori_loop(0, cells // group, fill, 0)

    @pl.loop(gx + 1, count)
    def _(peer):
        pl.semaphore_wait(ready.at[1, peer], beyond)
        rims(peer, begin)

    @pl.loop(near, count)
    def _(peer):
        pl.semaphore_wait(ready.at[0, peer], 1)

    def arrival(k):
        return pltpu.make_async_remote_copy(
            fr.at[0], recv.at[k], s_sem.at[k], r_sem.at[k],
            device_id={"gx": k}, device_id_type=MESH)

    def rim_arrival(k, side):
        return pltpu.make_async_remote_copy(
            rim.at[0, 0], beside.at[side, k], es_sem.at[side, k], er_sem.at[side, k],
            device_id={"gx": k, "gy": gy - 1 + 2 * side}, device_id_type=MESH)

    zero_rim = jnp.zeros((1, LANES), jnp.float32)

    @pl.when(gy == 0)
    def _():
        beside[0] = jnp.zeros(beside.shape[1:], jnp.float32)

    @pl.when(gy == wide - 1)
    def _():
        beside[1] = jnp.zeros(beside.shape[1:], jnp.float32)

    def take_rim(k, acc):
        @pl.when(gy > 0)
        def _():
            rim_arrival(k, 0).wait_recv()

        @pl.when(gy < wide - 1)
        def _():
            rim_arrival(k, 1).wait_recv()

        return acc[0] + beside[0, k], acc[1] + beside[1, k]

    def take(k, acc):
        arrival(k).wait_recv()
        return acc[0] + recv[k, 0], acc[1] + recv[k, 1]

    def keep(which, value):
        total[which, 0] = value[0]
        total[which, 1] = value[1]

    def pass_on(which, value):
        relay[which, 0] = value[0]
        relay[which, 1] = value[1]
        hub_do(which, begin)

    def take_twin(value):
        twin_message(0, gx).wait_recv()
        return value[0] + twin[0], value[1] + twin[1]

    def take_left():
        if not split:
            keep(0, lax.fori_loop(0, gx, take, (zero, zero)))
            return
        above = gx >= half
        value = lax.fori_loop(jnp.where(above, half, 0), gx, take, (zero, zero))
        hub = half - 2 + lax.rem(gx, 2)
        value = lax.fori_loop(hub, hub + jnp.where(above, 1, 0), take, value)
        keep(0, value)
        value = value[0] + fr[0, 0], value[1] + fr[0, 1]

        @pl.when(gx == half - 1)
        def _():
            pass_on(0, value)

        @pl.when(gx == half - 2)
        def _():
            pass_on(0, take_twin(value))

    def take_right():
        own = (fr[1, 0], fr[1, 1])
        if not split:
            keep(1, lax.fori_loop(gx + 1, count, take, own))
            return
        between = (gx >= 2) & (gx < half) & odd
        value = lax.fori_loop(gx + 1, jnp.where(between, half, count), take, own)
        hub = half + lax.rem(gx, 2)
        value = lax.fori_loop(hub, hub + jnp.where(between, 1, 0), take, value)
        keep(1, value)

        @pl.when((gx == half) & odd)
        def _():
            pass_on(1, value)

        @pl.when((gx == half + 1) & odd)
        def _():
            pass_on(1, take_twin(value))

    def settle():
        @pl.when(not_low)
        def _():
            up.wait_recv()

        @pl.when(not_high)
        def _():
            down.wait_recv()

        wanted = [(inv * RYZ) * (halo[0, p] + halo[1, p]) for p in range(2)]

        def mend(c, unused):
            for p in range(2):
                h = pltpu.roll(wanted[p], LANES - 2 * c, 1)
                for side, at in enumerate((0, lines - LANES)):
                    old = rho[p, c, :, at : at + LANES]
                    rho[p, c, :, at : at + LANES] = jnp.where(lane == side * (LANES - 1), old - h, old)
            return unused

        lax.fori_loop(0, cells, mend, 0, unroll=8)

        @pl.loop(0, count)
        def _(peer):
            @pl.when((peer != gx) & jnp.logical_not(by_hub(peer)))
            def _():
                message(peer).wait_send()

            rims(peer, end)

        @pl.when(not_low)
        def _():
            down.wait_send()

        @pl.when(not_high)
        def _():
            up.wait_send()

        for n, total in enumerate(lax.fori_loop(0, gx, take_rim, (zero_rim, zero_rim))
                                  + lax.fori_loop(gx, count, take_rim, (zero_rim, zero_rim))):
            rim_sum[n] = total

    pl.when(gx < half)(take_left)
    pl.when(gx >= half)(take_right)
    settle()
    pl.when(gx < half)(take_right)
    pl.when(gx >= half)(take_left)
    left = (total[0, 0], total[0, 1], rim_sum[0], rim_sum[1])
    right = (total[1, 0], total[1, 1], rim_sum[2], rim_sum[3])

    def spread(side):
        columns = []
        for tile in side[2:]:
            columns.append(tuple(
                jnp.sum(jnp.where(row_rim == part * planes, tile, 0.0), axis=1, keepdims=True) for part in range(2)))
        return stencil(side[0], side[1], columns[0], columns[1])

    left = spread(left)
    right = spread(right)
    w = both(scalar(4), left, scalar(5), right)
    d = both(scalar(6), left, scalar(7), right)

    for index, value in enumerate(w + d):
        start[index] = value

    if split:
        pl.when((gx == half - 2) | (gx == half - 1))(lambda: hub_do(0, end))
        pl.when(((gx == half) | (gx == half + 1)) & odd)(lambda: hub_do(1, end))

        @pl.when((gx == half - 1) | ((gx == half) & odd))
        def _():
            twin_message(0, gx).wait_send()


def finish(coef, chunk, turned, rho, start, out, out_v, out_sem):
    cells = turned.shape[1]
    chunks = cells // chunk
    inv = np.float32(1.0 / coef)

    def store(i):
        part = pl.ds(i * chunk, chunk)
        return pltpu.make_async_copy(out_v.at[:, part], out.at[:, part], out_sem.at[i])

    def march(c, carry):
        w_re, w_im, d_re, d_im = carry
        w_re = w_re + d_re
        w_im = w_im + d_im
        out_v[0, c] = w_re - turned[0, c]
        out_v[1, c] = w_im - turned[1, c]
        d_re = d_re + (rho[0, c] + inv * w_im)
        d_im = d_im + (rho[1, c] - inv * w_re)
        return w_re, w_im, d_re, d_im

    carry = (start[0], start[1], start[2], start[3])
    for i in range(chunks):
        carry = lax.fori_loop(i * chunk, (i + 1) * chunk, march, carry, unroll=4)
        store(i).start()
    for i in range(chunks):
        store(i).wait()


def shards(psi, potential):
    unused, cells, planes, lines = psi.shape
    count = lax.axis_size("gx")
    wide = lax.axis_size("gy")
    place, coef = tables(cells, count)
    chunk = 8 if cells % 8 == 0 else cells
    chunks = cells // chunk
    block = (2, cells, planes, lines)
    plane = (planes, lines)
    vmem = pl.BlockSpec(memory_space=pltpu.VMEM)
    held = pl.pallas_call(
        functools.partial(kernel, count, wide, coef, chunk),
        out_shape=[
            jax.ShapeDtypeStruct(block, jnp.float32),
            jax.ShapeDtypeStruct(block, jnp.float32),
            jax.ShapeDtypeStruct((4,) + plane, jnp.float32),
        ],
        in_specs=[
            pl.BlockSpec(memory_space=pltpu.HBM),
            pl.BlockSpec(memory_space=pltpu.HBM),
            pl.BlockSpec(memory_space=pltpu.HBM),
        ],
        out_specs=[vmem] * 3,
        scratch_shapes=[
            pltpu.SMEM(place.shape, jnp.float32),
            pltpu.SemaphoreType.DMA((1,)),
            pltpu.VMEM(block, jnp.float32),
            pltpu.VMEM(block[1:], jnp.float32),
            pltpu.VMEM((2, 2, planes, LANES), jnp.float32),
            pltpu.VMEM((2, 2, planes, LANES), jnp.float32),
            pltpu.VMEM((2, 2) + plane, jnp.float32),
            pltpu.VMEM((count, 2) + plane, jnp.float32),
            pltpu.SemaphoreType.DMA((2, chunks)),
            pltpu.SemaphoreType.DMA((2,)),
            pltpu.SemaphoreType.DMA((2,)),
            pltpu.SemaphoreType.DMA((count,)),
            pltpu.SemaphoreType.DMA((count,)),
            pltpu.VMEM((2, 2, 1, LANES), jnp.float32),
            pltpu.VMEM((2, count, 1, LANES), jnp.float32),
            pltpu.SemaphoreType.DMA((2, count)),
            pltpu.SemaphoreType.DMA((2, count)),
            pltpu.VMEM((lines, lines), jnp.bfloat16),
            pltpu.SemaphoreType.REGULAR((2, count)),
            pltpu.VMEM((2, 2) + plane, jnp.float32),
            pltpu.VMEM((4, 1, LANES), jnp.float32),
            pltpu.VMEM((2,) + plane, jnp.float32),
            pltpu.SemaphoreType.DMA((2,)),
            pltpu.VMEM((2, 2) + plane, jnp.float32),
        ],
        compiler_params=pltpu.CompilerParams(
            collective_id=0, has_side_effects=True, vmem_limit_bytes=24 * 2**20
        ),
    )(*(pltpu.with_memory_space_constraint(x, pltpu.HBM) for x in
        (psi, potential, jnp.asarray(place))))
    return pl.pallas_call(
        functools.partial(finish, coef, chunk),
        out_shape=jax.ShapeDtypeStruct(block, jnp.float32),
        in_specs=[vmem] * 3,
        out_specs=pl.BlockSpec(memory_space=pl.ANY),
        scratch_shapes=[
            pltpu.VMEM(block, jnp.float32),
            pltpu.SemaphoreType.DMA((chunks,)),
        ],
        compiler_params=pltpu.CompilerParams(vmem_limit_bytes=16 * 2**20),
    )(*held)


def solution(mesh):
    return jax.shard_map(
        shards,
        mesh=mesh,
        in_specs=(P(None, "gx", None, "gy"), P("gx", None, "gy")),
        out_specs=P(None, "gx", None, "gy"),
        check_vma=False,
    )
```

```python
import functools

import jax
import jax.numpy as jnp
import numpy as np
from jax import lax
from jax.experimental import pallas as pl
from jax.experimental.pallas import tpu as pltpu
from jax.sharding import PartitionSpec as P

RYZ = 2.0
LANES = 128
MESH = pl.DeviceIdType.MESH


def tables(cells, count):
    coef = 256.0 * cells * cells
    total = cells * count
    lam = np.arccosh(np.complex128(1.0 - 0.5j / coef))
    sh = lambda m: np.sinh(lam * m)
    scale = -(1j / coef) / (sh(1) * sh(total + 1))
    x0 = cells * np.arange(count, dtype=np.float64)
    end = x0 + cells
    f_q = sh(end) - sh(end + 1)
    f_e = sh(end + 1)
    r_q = sh(total + 1 - end) - sh(total - end)
    r_e = sh(total - end)
    w_l = scale * sh(total + 1 - x0)
    w_r = scale * sh(x0)
    d_l = scale * (sh(total - x0) - sh(total + 1 - x0))
    d_r = scale * (sh(x0 + 1) - sh(x0))
    rows = [f_q, f_e, r_q, r_e, w_l, w_r, d_l, d_r]
    place = np.stack([part for row in rows for part in (row.real, row.imag)], axis=1)
    return place.astype(np.float32).reshape(-1), coef


HALF_SINE = (4.442882834149953, -7.308241154547353, 3.6062889582396482, -0.8457635962213053, 0.10920575376953141)
HALF_COSINE = (1.4142134965650301, -6.9788509882409375, 5.739461170721302, -1.883562987555641, 0.3106981923194725)


def turn(re, im, pot):
    t = (pot + re * re + im * im) * np.float32(0.25 / np.pi)
    f = t - jnp.round(t)
    f2 = f * f
    s = np.float32(HALF_SINE[-1])
    for a in HALF_SINE[-2::-1]:
        s = s * f2 + np.float32(a)
    s = s * f
    c = np.float32(HALF_COSINE[-1])
    for a in HALF_COSINE[-2::-1]:
        c = c * f2 + np.float32(a)
    sine = s * c
    cosine = 1.0 - s * s
    return re * cosine + im * sine, im * cosine - re * sine


def kernel(count, wide, coef, chunk, psi, pot, place_in, turned, rho,
           start, place_ref, table_sem, psi_v, pot_v, edge, halo, fr, recv, in_sem, hs_sem, hr_sem, s_sem, r_sem,
           rim, beside, es_sem, er_sem, band, ready, relay, rim_sum, twin, t_sem, total, cut_sem, c_sem):
    cells, planes, lines = pot_v.shape
    gx = lax.axis_index("gx")
    gy = lax.axis_index("gy")
    inv = np.float32(1.0 / coef)

    rows = [pl.ds(part * (planes // 2), planes // 2) for part in range(2)]
    loads = 2 if cells % 2 == 0 else 1
    step = cells // loads

    def load(part, i):
        at = pl.ds(i * step, step)
        return (
            pltpu.make_async_copy(psi.at[:, at, rows[part]], psi_v.at[:, at, rows[part]], in_sem.at[0, part, i]),
            pltpu.make_async_copy(pot.at[at, rows[part]], pot_v.at[at, rows[part]], in_sem.at[1, part, i]),
        )

    for part in range(2):
        for i in range(loads):
            for copy in load(part, i):
                copy.start()

    table = pltpu.make_async_copy(place_in, place_ref, table_sem.at[0])
    table.start()

    barrier = pltpu.get_barrier_semaphore()
    not_low, not_high = gy > 0, gy < wide - 1
    beyond = jnp.where(not_low, 1, 0) + jnp.where(not_high, 1, 0)

    def beside_do(do):
        @pl.when(not_low)
        def _():
            do(gy - 1)

        @pl.when(not_high)
        def _():
            do(gy + 1)

    def greet(x, y):
        pl.semaphore_signal(barrier, inc=1, device_id={"gx": x, "gy": y}, device_id_type=MESH)

    beside_do(lambda y: greet(gx, y))

    @pl.loop(gx + 1, count)
    def _(k):
        greet(k, gy)
        beside_do(lambda y: greet(k, y))

    across = lax.broadcasted_iota(jnp.int32, (lines, lines), 0) - lax.broadcasted_iota(jnp.int32, (lines, lines), 1)
    band[...] = jnp.where(across == 0, -4.0, jnp.where(jnp.abs(across) == 1, 1.0, 0.0)).astype(jnp.bfloat16)

    def tell(x, y):
        pl.semaphore_signal(ready.at[jnp.where(y == gy, 0, 1), gx], inc=1, device_id={"gx": x, "gy": y},
                            device_id_type=MESH)

    def meet():
        pl.semaphore_wait(barrier, gx * (1 + beyond) + beyond)

        @pl.loop(0, gx)
        def _(k):
            tell(k, gy)
            beside_do(lambda y: tell(k, y))

    def scalar(index):
        return place_ref[gx * 16 + 2 * index], place_ref[gx * 16 + 2 * index + 1]

    def both(a, x, b, y):
        return (
            (a[0] * x[0] - a[1] * x[1]) + (b[0] * y[0] - b[1] * y[1]),
            (a[0] * x[1] + a[1] * x[0]) + (b[0] * y[1] + b[1] * y[0]),
        )

    lane = lax.broadcasted_iota(jnp.int32, (planes, LANES), 1)
    row_rim = lane - lax.broadcasted_iota(jnp.int32, (planes, LANES), 0)

    def interface(which, part):
        e_re, e_im, q_re, q_im = sums[part]
        value = both(scalar(2 * which), (q_re, q_im), scalar(2 * which + 1), (e_re, e_im))
        fr[which, 0, rows[part]] = value[0]
        fr[which, 1, rows[part]] = value[1]

    def edges(which):
        value = fr[which, 0], fr[which, 1]
        for side in range(2):
            at = side * (lines - 1)
            tile = jnp.where(row_rim == 0, value[0][:, at : at + 1],
                             jnp.where(row_rim == planes, value[1][:, at : at + 1], 0.0))
            rim[which, side] = jnp.sum(tile, axis=0, keepdims=True)

    half = count // 2
    split = count >= 8 and count % 4 == 0
    odd = lax.rem(gy, 2) == 1

    def by_hub(peer):
        if not split:
            return peer < 0
        return ((gx < half) & (peer >= half)) | ((gx >= half) & (peer >= 2) & (peer < half) & odd)

    def message(peer):
        return pltpu.make_async_remote_copy(
            fr.at[jnp.where(peer < gx, 1, 0)], recv.at[gx], s_sem.at[peer], r_sem.at[gx],
            device_id={"gx": peer}, device_id_type=MESH)

    def cut_message(part):
        return pltpu.make_async_remote_copy(
            fr.at[1, :, rows[part]], recv.at[gx, :, rows[part]], cut_sem.at[0, part], c_sem.at[part, gx],
            device_id={"gx": 0}, device_id_type=MESH)

    def hub_message(which, peer):
        return pltpu.make_async_remote_copy(
            relay.at[which], recv.at[gx], s_sem.at[peer], r_sem.at[gx],
            device_id={"gx": peer}, device_id_type=MESH)

    def twin_message(which, peer):
        return pltpu.make_async_remote_copy(
            fr.at[which], twin, t_sem.at[0], t_sem.at[1],
            device_id={"gx": peer}, device_id_type=MESH)

    def hub_do(which, do):
        parity = lax.rem(gx, 2)

        @pl.loop(0, half // 2 - which)
        def _(n):
            do(hub_message(which, (half if which == 0 else 2) + 2 * n + parity))

    def rim_message(peer, side):
        return pltpu.make_async_remote_copy(
            rim.at[jnp.where(peer <= gx, 1, 0), side], beside.at[1 - side, gx],
            es_sem.at[side, peer], er_sem.at[1 - side, gx],
            device_id={"gx": peer, "gy": gy - 1 + 2 * side}, device_id_type=MESH)

    def rims(peer, do):
        @pl.when(not_low)
        def _():
            do(rim_message(peer, 0))

        @pl.when(not_high)
        def _():
            do(rim_message(peer, 1))

    def begin(copy):
        copy.start()

    def end(copy):
        copy.wait_send()

    def advance(part):
        at = rows[part]

        def one(c, carry):
            e_re, e_im, q_re, q_im = carry
            t_re, t_im = turn(psi_v[0, c, at], psi_v[1, c, at], pot_v[c, at])
            turned[0, c, at] = t_re
            turned[1, c, at] = t_im
            e_re = e_re + (t_re + inv * q_im)
            e_im = e_im + (t_im - inv * q_re)
            return e_re, e_im, q_re + e_re, q_im + e_im

        carry = (jnp.zeros((planes // 2, lines), jnp.float32),) * 4
        for i in range(loads):
            for copy in load(part, i):
                copy.wait()
            carry = lax.fori_loop(i * step, (i + 1) * step, one, carry, unroll=4)
        return carry

    zero = jnp.zeros((planes, lines), jnp.float32)
    even = jnp.logical_not(odd)
    pl.when(even)(meet)
    sums = [advance(0)]
    table.wait()
    interface(1, 0)

    @pl.when(even & (gx > 0))
    def _():
        cut_message(0).start()

    sums.append(advance(1))
    interface(1, 1)
    pl.when(odd)(meet)
    edges(1)

    def send_down(start, stop):
        @pl.loop(start, stop)
        def _(peer):
            @pl.when(jnp.logical_not(by_hub(peer)))
            def _():
                message(peer).start()

    urgent = jnp.minimum(gx, 2)

    @pl.loop(0, urgent)
    def _(peer):
        rims(peer, begin)

    @pl.when(odd)
    def _():
        send_down(0, gx)

    @pl.when(even & (gx > 0))
    def _():
        cut_message(1).start()

    @pl.loop(urgent, gx + 1)
    def _(peer):
        rims(peer, begin)

    interface(0, 0)
    interface(0, 1)
    edges(0)

    if split:
        @pl.when(gx == half - 1)
        def _():
            twin_message(0, half - 2).start()

    def pack(c, acc):
        new = []
        for part in range(2):
            src = turned.at[part, c]
            first = src[:, 0:LANES][:, 0:1]
            last = src[:, lines - LANES : lines][:, LANES - 1 : LANES]
            new.append(jnp.where(lane == lax.rem(2 * c + LANES - 1, LANES), first, acc[2 * part]))
            new.append(jnp.where(lane == 2 * c, last, acc[2 * part + 1]))
        return tuple(new)

    zero_edge = jnp.zeros((planes, LANES), jnp.float32)
    packed = lax.fori_loop(0, cells, pack, (zero_edge,) * 4, unroll=4)
    for part in range(2):
        edge[0, part] = packed[2 * part]
        edge[1, part] = packed[2 * part + 1]

    down = pltpu.make_async_remote_copy(edge.at[0], halo.at[1], hs_sem.at[0], hr_sem.at[1],
                                        device_id={"gy": gy - 1}, device_id_type=MESH)
    up = pltpu.make_async_remote_copy(edge.at[1], halo.at[0], hs_sem.at[1], hr_sem.at[0],
                                      device_id={"gy": gy + 1}, device_id_type=MESH)

    @pl.when(gy > 0)
    def _():
        down.start()

    @pl.when(gy == 0)
    def _():
        halo[0] = jnp.zeros(halo.shape[1:], jnp.float32)

    @pl.when(gy < wide - 1)
    def _():
        up.start()

    @pl.when(gy == wide - 1)
    def _():
        halo[1] = jnp.zeros(halo.shape[1:], jnp.float32)

    pl.when(even)(lambda: send_down(1, gx))

    near = jnp.where(gx < half, half, count) if split else count

    @pl.loop(gx + 1, near)
    def _(peer):
        pl.semaphore_wait(ready.at[0, peer], 1)
        message(peer).start()

    if split:
        @pl.when((gx == half) & odd)
        def _():
            twin_message(1, half + 1).start()

    col = lax.broadcasted_iota(jnp.int32, (planes, lines), 1)
    row = lax.broadcasted_iota(jnp.int32, (planes, lines), 0)
    at_first, at_last = col == 0, col == lines - 1
    at_bottom, at_top = row == 0, row == planes - 1

    def lap(x, first, last):
        left = jnp.where(at_first, first, pltpu.roll(x, 1, 1))
        right = jnp.where(at_last, last, pltpu.roll(x, lines - 1, 1))
        below = jnp.where(at_bottom, 0.0, pltpu.roll(x, 1, 0))
        above = jnp.where(at_top, 0.0, pltpu.roll(x, planes - 1, 0))
        return ((left + right) + (below + above)) - 4.0 * x

    def stencil(re, im, first, last):
        lap_re = lap(re, first[0], last[0])
        lap_im = lap(im, first[1], last[1])
        return 2.0 * re - RYZ * lap_im, 2.0 * im + RYZ * lap_re

    def fill(i, unused):
        part = pl.ds(i * group, group)
        laps = []
        for p in range(2):
            x = turned[p, part].reshape(group * planes, lines)
            high = x.astype(jnp.bfloat16)
            low = (x - high.astype(jnp.float32)).astype(jnp.bfloat16)
            y = (jnp.dot(high, band[...], preferred_element_type=jnp.float32)
                 + jnp.dot(low, band[...], preferred_element_type=jnp.float32))
            laps.append(y.reshape(group, planes, lines))
        for n in range(group):
            c = i * group + n
            lap_of = []
            for p in range(2):
                x = turned[p, c]
                below = jnp.where(at_bottom, 0.0, pltpu.roll(x, 1, 0))
                above = jnp.where(at_top, 0.0, pltpu.roll(x, planes - 1, 0))
                lap_of.append(laps[p][n] + (below + above))
            rho[0, c] = -inv * (2.0 * turned[1, c] + RYZ * lap_of[0])
            rho[1, c] = inv * (2.0 * turned[0, c] - RYZ * lap_of[1])
        return unused

    group = chunk
    lax.fori_loop(0, cells // group, fill, 0)

    @pl.loop(gx + 1, count)
    def _(peer):
        pl.semaphore_wait(ready.at[1, peer], beyond)
        rims(peer, begin)

    @pl.loop(near, count)
    def _(peer):
        pl.semaphore_wait(ready.at[0, peer], 1)

    def arrival(k):
        return pltpu.make_async_remote_copy(
            fr.at[0], recv.at[k], s_sem.at[k], r_sem.at[k],
            device_id={"gx": k}, device_id_type=MESH)

    def rim_arrival(k, side):
        return pltpu.make_async_remote_copy(
            rim.at[0, 0], beside.at[side, k], es_sem.at[side, k], er_sem.at[side, k],
            device_id={"gx": k, "gy": gy - 1 + 2 * side}, device_id_type=MESH)

    zero_rim = jnp.zeros((1, LANES), jnp.float32)

    @pl.when(gy == 0)
    def _():
        beside[0] = jnp.zeros(beside.shape[1:], jnp.float32)

    @pl.when(gy == wide - 1)
    def _():
        beside[1] = jnp.zeros(beside.shape[1:], jnp.float32)

    def take_rim(k, acc):
        @pl.when(gy > 0)
        def _():
            rim_arrival(k, 0).wait_recv()

        @pl.when(gy < wide - 1)
        def _():
            rim_arrival(k, 1).wait_recv()

        return acc[0] + beside[0, k], acc[1] + beside[1, k]

    def take(k, acc):
        cut = even & (gx == 0)

        @pl.when(cut)
        def _():
            for part in range(2):
                pltpu.make_async_remote_copy(
                    fr.at[1, :, rows[part]], recv.at[k, :, rows[part]], cut_sem.at[0, part], c_sem.at[part, k],
                    device_id={"gx": k}, device_id_type=MESH).wait_recv()

        @pl.when(jnp.logical_not(cut))
        def _():
            arrival(k).wait_recv()

        return acc[0] + recv[k, 0], acc[1] + recv[k, 1]

    def keep(which, value):
        total[which, 0] = value[0]
        total[which, 1] = value[1]

    def pass_on(which, value):
        relay[which, 0] = value[0]
        relay[which, 1] = value[1]
        hub_do(which, begin)

    def take_twin(value):
        twin_message(0, gx).wait_recv()
        return value[0] + twin[0], value[1] + twin[1]

    def take_left():
        if not split:
            keep(0, lax.fori_loop(0, gx, take, (zero, zero)))
            return
        above = gx >= half
        value = lax.fori_loop(jnp.where(above, half, 0), gx, take, (zero, zero))
        hub = half - 2 + lax.rem(gx, 2)
        value = lax.fori_loop(hub, hub + jnp.where(above, 1, 0), take, value)
        keep(0, value)
        value = value[0] + fr[0, 0], value[1] + fr[0, 1]

        @pl.when(gx == half - 1)
        def _():
            pass_on(0, value)

        @pl.when(gx == half - 2)
        def _():
            pass_on(0, take_twin(value))

    def take_right():
        own = (fr[1, 0], fr[1, 1])
        if not split:
            keep(1, lax.fori_loop(gx + 1, count, take, own))
            return
        between = (gx >= 2) & (gx < half) & odd
        value = lax.fori_loop(gx + 1, jnp.where(between, half, count), take, own)
        hub = half + lax.rem(gx, 2)
        value = lax.fori_loop(hub, hub + jnp.where(between, 1, 0), take, value)
        keep(1, value)

        @pl.when((gx == half) & odd)
        def _():
            pass_on(1, value)

        @pl.when((gx == half + 1) & odd)
        def _():
            pass_on(1, take_twin(value))

    def settle():
        @pl.when(not_low)
        def _():
            up.wait_recv()

        @pl.when(not_high)
        def _():
            down.wait_recv()

        wanted = [(inv * RYZ) * (halo[0, p] + halo[1, p]) for p in range(2)]

        def mend(c, unused):
            for p in range(2):
                h = pltpu.roll(wanted[p], LANES - 2 * c, 1)
                for side, at in enumerate((0, lines - LANES)):
                    old = rho[p, c, :, at : at + LANES]
                    rho[p, c, :, at : at + LANES] = jnp.where(lane == side * (LANES - 1), old - h, old)
            return unused

        lax.fori_loop(0, cells, mend, 0, unroll=8)

        @pl.when(even & (gx > 0))
        def _():
            for part in range(2):
                cut_message(part).wait_send()

        @pl.loop(0, count)
        def _(peer):
            @pl.when((peer != gx) & jnp.logical_not(by_hub(peer)) & (odd | (peer > 0)))
            def _():
                message(peer).wait_send()

            rims(peer, end)

        @pl.when(not_low)
        def _():
            down.wait_send()

        @pl.when(not_high)
        def _():
            up.wait_send()

        for n, total in enumerate(lax.fori_loop(0, gx, take_rim, (zero_rim, zero_rim))
                                  + lax.fori_loop(gx, count, take_rim, (zero_rim, zero_rim))):
            rim_sum[n] = total

    pl.when(gx < half)(take_left)
    pl.when(gx >= half)(take_right)
    settle()
    pl.when(gx < half)(take_right)
    pl.when(gx >= half)(take_left)
    left = (total[0, 0], total[0, 1], rim_sum[0], rim_sum[1])
    right = (total[1, 0], total[1, 1], rim_sum[2], rim_sum[3])

    def spread(side):
        columns = []
        for tile in side[2:]:
            columns.append(tuple(
                jnp.sum(jnp.where(row_rim == part * planes, tile, 0.0), axis=1, keepdims=True) for part in range(2)))
        return stencil(side[0], side[1], columns[0], columns[1])

    left = spread(left)
    right = spread(right)
    w = both(scalar(4), left, scalar(5), right)
    d = both(scalar(6), left, scalar(7), right)

    for index, value in enumerate(w + d):
        start[index] = value

    if split:
        pl.when((gx == half - 2) | (gx == half - 1))(lambda: hub_do(0, end))
        pl.when(((gx == half) | (gx == half + 1)) & odd)(lambda: hub_do(1, end))

        @pl.when((gx == half - 1) | ((gx == half) & odd))
        def _():
            twin_message(0, gx).wait_send()


def finish(coef, chunk, turned, rho, start, out, out_v, out_sem):
    cells = turned.shape[1]
    chunks = cells // chunk
    inv = np.float32(1.0 / coef)

    def store(i):
        part = pl.ds(i * chunk, chunk)
        return pltpu.make_async_copy(out_v.at[:, part], out.at[:, part], out_sem.at[i])

    def march(c, carry):
        w_re, w_im, d_re, d_im = carry
        w_re = w_re + d_re
        w_im = w_im + d_im
        out_v[0, c] = w_re - turned[0, c]
        out_v[1, c] = w_im - turned[1, c]
        d_re = d_re + (rho[0, c] + inv * w_im)
        d_im = d_im + (rho[1, c] - inv * w_re)
        return w_re, w_im, d_re, d_im

    carry = (start[0], start[1], start[2], start[3])
    for i in range(chunks):
        carry = lax.fori_loop(i * chunk, (i + 1) * chunk, march, carry, unroll=4)
        store(i).start()
    for i in range(chunks):
        store(i).wait()


def shards(psi, potential):
    unused, cells, planes, lines = psi.shape
    count = lax.axis_size("gx")
    wide = lax.axis_size("gy")
    place, coef = tables(cells, count)
    chunk = 8 if cells % 8 == 0 else cells
    chunks = cells // chunk
    block = (2, cells, planes, lines)
    plane = (planes, lines)
    vmem = pl.BlockSpec(memory_space=pltpu.VMEM)
    held = pl.pallas_call(
        functools.partial(kernel, count, wide, coef, chunk),
        out_shape=[
            jax.ShapeDtypeStruct(block, jnp.float32),
            jax.ShapeDtypeStruct(block, jnp.float32),
            jax.ShapeDtypeStruct((4,) + plane, jnp.float32),
        ],
        in_specs=[
            pl.BlockSpec(memory_space=pltpu.HBM),
            pl.BlockSpec(memory_space=pltpu.HBM),
            pl.BlockSpec(memory_space=pltpu.HBM),
        ],
        out_specs=[vmem] * 3,
        scratch_shapes=[
            pltpu.SMEM(place.shape, jnp.float32),
            pltpu.SemaphoreType.DMA((1,)),
            pltpu.VMEM(block, jnp.float32),
            pltpu.VMEM(block[1:], jnp.float32),
            pltpu.VMEM((2, 2, planes, LANES), jnp.float32),
            pltpu.VMEM((2, 2, planes, LANES), jnp.float32),
            pltpu.VMEM((2, 2) + plane, jnp.float32),
            pltpu.VMEM((count, 2) + plane, jnp.float32),
            pltpu.SemaphoreType.DMA((2, 2, 2)),
            pltpu.SemaphoreType.DMA((2,)),
            pltpu.SemaphoreType.DMA((2,)),
            pltpu.SemaphoreType.DMA((count,)),
            pltpu.SemaphoreType.DMA((count,)),
            pltpu.VMEM((2, 2, 1, LANES), jnp.float32),
            pltpu.VMEM((2, count, 1, LANES), jnp.float32),
            pltpu.SemaphoreType.DMA((2, count)),
            pltpu.SemaphoreType.DMA((2, count)),
            pltpu.VMEM((lines, lines), jnp.bfloat16),
            pltpu.SemaphoreType.REGULAR((2, count)),
            pltpu.VMEM((2, 2) + plane, jnp.float32),
            pltpu.VMEM((4, 1, LANES), jnp.float32),
            pltpu.VMEM((2,) + plane, jnp.float32),
            pltpu.SemaphoreType.DMA((2,)),
            pltpu.VMEM((2, 2) + plane, jnp.float32),
            pltpu.SemaphoreType.DMA((1, 2)),
            pltpu.SemaphoreType.DMA((2, count)),
        ],
        compiler_params=pltpu.CompilerParams(
            collective_id=0, has_side_effects=True, vmem_limit_bytes=24 * 2**20
        ),
    )(*(pltpu.with_memory_space_constraint(x, pltpu.HBM) for x in
        (psi, potential, jnp.asarray(place))))
    return pl.pallas_call(
        functools.partial(finish, coef, chunk),
        out_shape=jax.ShapeDtypeStruct(block, jnp.float32),
        in_specs=[vmem] * 3,
        out_specs=pl.BlockSpec(memory_space=pl.ANY),
        scratch_shapes=[
            pltpu.VMEM(block, jnp.float32),
            pltpu.SemaphoreType.DMA((chunks,)),
        ],
        compiler_params=pltpu.CompilerParams(vmem_limit_bytes=16 * 2**20),
    )(*held)


def solution(mesh):
    return jax.shard_map(
        shards,
        mesh=mesh,
        in_specs=(P(None, "gx", None, "gy"), P("gx", None, "gy")),
        out_specs=P(None, "gx", None, "gy"),
        check_vma=False,
    )
```

```python
import functools

import jax
import jax.numpy as jnp
import numpy as np
from jax import lax
from jax.experimental import pallas as pl
from jax.experimental.pallas import tpu as pltpu
from jax.sharding import PartitionSpec as P

RYZ = 2.0
LANES = 128
MESH = pl.DeviceIdType.MESH


def tables(cells, count):
    coef = 256.0 * cells * cells
    total = cells * count
    lam = np.arccosh(np.complex128(1.0 - 0.5j / coef))
    sh = lambda m: np.sinh(lam * m)
    scale = -(1j / coef) / (sh(1) * sh(total + 1))
    x0 = cells * np.arange(count, dtype=np.float64)
    end = x0 + cells
    f_q = sh(end) - sh(end + 1)
    f_e = sh(end + 1)
    r_q = sh(total + 1 - end) - sh(total - end)
    r_e = sh(total - end)
    w_l = scale * sh(total + 1 - x0)
    w_r = scale * sh(x0)
    d_l = scale * (sh(total - x0) - sh(total + 1 - x0))
    d_r = scale * (sh(x0 + 1) - sh(x0))
    rows = [f_q, f_e, r_q, r_e, w_l, w_r, d_l, d_r]
    place = np.stack([part for row in rows for part in (row.real, row.imag)], axis=1)
    return place.astype(np.float32).reshape(-1), coef


HALF_SINE = (4.442882834149953, -7.308241154547353, 3.6062889582396482, -0.8457635962213053, 0.10920575376953141)
HALF_COSINE = (1.4142134965650301, -6.9788509882409375, 5.739461170721302, -1.883562987555641, 0.3106981923194725)


def turn(re, im, pot):
    t = (pot + re * re + im * im) * np.float32(0.25 / np.pi)
    f = t - jnp.round(t)
    f2 = f * f
    s = np.float32(HALF_SINE[-1])
    for a in HALF_SINE[-2::-1]:
        s = s * f2 + np.float32(a)
    s = s * f
    c = np.float32(HALF_COSINE[-1])
    for a in HALF_COSINE[-2::-1]:
        c = c * f2 + np.float32(a)
    sine = s * c
    cosine = 1.0 - s * s
    return re * cosine + im * sine, im * cosine - re * sine


def kernel(count, wide, coef, chunk, psi, pot, place_in, turned, rho,
           start, place_ref, table_sem, psi_v, pot_v, edge, halo, fr, recv, in_sem, hs_sem, hr_sem, s_sem, r_sem,
           rim, beside, es_sem, er_sem, band, ready, relay, rim_sum, twin, t_sem, total, cut_sem, c_sem):
    cells, planes, lines = pot_v.shape
    gx = lax.axis_index("gx")
    gy = lax.axis_index("gy")
    inv = np.float32(1.0 / coef)

    rows = [pl.ds(part * (planes // 2), planes // 2) for part in range(2)]
    loads = 2 if cells % 2 == 0 else 1
    step = cells // loads

    def load(part, i):
        at = pl.ds(i * step, step)
        return (
            pltpu.make_async_copy(psi.at[:, at, rows[part]], psi_v.at[:, at, rows[part]], in_sem.at[0, part, i]),
            pltpu.make_async_copy(pot.at[at, rows[part]], pot_v.at[at, rows[part]], in_sem.at[1, part, i]),
        )

    for part in range(2):
        for i in range(loads):
            for copy in load(part, i):
                copy.start()

    table = pltpu.make_async_copy(place_in, place_ref, table_sem.at[0])
    table.start()

    barrier = pltpu.get_barrier_semaphore()
    not_low, not_high = gy > 0, gy < wide - 1
    beyond = jnp.where(not_low, 1, 0) + jnp.where(not_high, 1, 0)

    def beside_do(do):
        @pl.when(not_low)
        def _():
            do(gy - 1)

        @pl.when(not_high)
        def _():
            do(gy + 1)

    def greet(x, y):
        pl.semaphore_signal(barrier, inc=1, device_id={"gx": x, "gy": y}, device_id_type=MESH)

    beside_do(lambda y: greet(gx, y))

    @pl.loop(gx + 1, count)
    def _(k):
        greet(k, gy)
        beside_do(lambda y: greet(k, y))

    across = lax.broadcasted_iota(jnp.int32, (lines, lines), 0) - lax.broadcasted_iota(jnp.int32, (lines, lines), 1)
    band[...] = jnp.where(across == 0, -4.0, jnp.where(jnp.abs(across) == 1, 1.0, 0.0)).astype(jnp.bfloat16)

    def tell(x, y):
        pl.semaphore_signal(ready.at[jnp.where(y == gy, 0, 1), gx], inc=1, device_id={"gx": x, "gy": y},
                            device_id_type=MESH)

    def meet():
        pl.semaphore_wait(barrier, gx * (1 + beyond) + beyond)

        @pl.loop(0, gx)
        def _(k):
            tell(k, gy)
            beside_do(lambda y: tell(k, y))

    def scalar(index):
        return place_ref[gx * 16 + 2 * index], place_ref[gx * 16 + 2 * index + 1]

    def both(a, x, b, y):
        return (
            (a[0] * x[0] - a[1] * x[1]) + (b[0] * y[0] - b[1] * y[1]),
            (a[0] * x[1] + a[1] * x[0]) + (b[0] * y[1] + b[1] * y[0]),
        )

    lane = lax.broadcasted_iota(jnp.int32, (planes, LANES), 1)
    lane_row = lane - lax.broadcasted_iota(jnp.int32, (planes, LANES), 0)
    row_rim = lane_row[0 : planes // 2]

    def interface(which, part):
        e_re, e_im, q_re, q_im = sums[part]
        value = both(scalar(2 * which), (q_re, q_im), scalar(2 * which + 1), (e_re, e_im))
        fr[which, 0, rows[part]] = value[0]
        fr[which, 1, rows[part]] = value[1]
        shift = part * (planes // 2)
        for side in range(2):
            at = side * (lines - 1)
            tile = jnp.where(row_rim == shift, value[0][:, at : at + 1],
                             jnp.where(row_rim == shift + planes, value[1][:, at : at + 1], 0.0))
            row = jnp.sum(tile, axis=0, keepdims=True)
            rim[which, side] = row if part == 0 else rim[which, side] + row

    half = count // 2
    split = count >= 8 and count % 4 == 0
    odd = lax.rem(gy, 2) == 1

    def by_hub(peer):
        if not split:
            return peer < 0
        return ((gx < half) & (peer >= half)) | ((gx >= half) & (peer >= 2) & (peer < half) & odd)

    def message(peer):
        return pltpu.make_async_remote_copy(
            fr.at[jnp.where(peer < gx, 1, 0)], recv.at[gx], s_sem.at[peer], r_sem.at[gx],
            device_id={"gx": peer}, device_id_type=MESH)

    def cut_message(part):
        return pltpu.make_async_remote_copy(
            fr.at[1, :, rows[part]], recv.at[gx, :, rows[part]], cut_sem.at[0, part], c_sem.at[part, gx],
            device_id={"gx": 0}, device_id_type=MESH)

    def hub_message(which, peer):
        return pltpu.make_async_remote_copy(
            relay.at[which], recv.at[gx], s_sem.at[peer], r_sem.at[gx],
            device_id={"gx": peer}, device_id_type=MESH)

    def twin_message(which, peer):
        return pltpu.make_async_remote_copy(
            fr.at[which], twin, t_sem.at[0], t_sem.at[1],
            device_id={"gx": peer}, device_id_type=MESH)

    def hub_do(which, do):
        parity = lax.rem(gx, 2)

        @pl.loop(0, half // 2 - which)
        def _(n):
            do(hub_message(which, (half if which == 0 else 2) + 2 * n + parity))

    def rim_message(peer, side):
        return pltpu.make_async_remote_copy(
            rim.at[jnp.where(peer <= gx, 1, 0), side], beside.at[1 - side, gx],
            es_sem.at[side, peer], er_sem.at[1 - side, gx],
            device_id={"gx": peer, "gy": gy - 1 + 2 * side}, device_id_type=MESH)

    def rims(peer, do):
        @pl.when(not_low)
        def _():
            do(rim_message(peer, 0))

        @pl.when(not_high)
        def _():
            do(rim_message(peer, 1))

    def begin(copy):
        copy.start()

    def end(copy):
        copy.wait_send()

    def advance(part):
        at = rows[part]

        def one(c, carry):
            e_re, e_im, q_re, q_im = carry
            t_re, t_im = turn(psi_v[0, c, at], psi_v[1, c, at], pot_v[c, at])
            turned[0, c, at] = t_re
            turned[1, c, at] = t_im
            e_re = (e_re + t_re) + inv * q_im
            e_im = (e_im + t_im) - inv * q_re
            return e_re, e_im, q_re + e_re, q_im + e_im

        carry = (jnp.zeros((planes // 2, lines), jnp.float32),) * 4
        for i in range(loads):
            for copy in load(part, i):
                copy.wait()
            carry = lax.fori_loop(i * step, (i + 1) * step, one, carry, unroll=8)
        return carry

    zero = jnp.zeros((planes, lines), jnp.float32)
    even = jnp.logical_not(odd)
    pl.when(even)(meet)
    sums = [advance(0)]
    table.wait()
    interface(1, 0)

    @pl.when(even & (gx > 0))
    def _():
        cut_message(0).start()

    sums.append(advance(1))
    interface(1, 1)
    pl.when(odd)(meet)

    def send_down(start, stop):
        @pl.loop(start, stop)
        def _(peer):
            @pl.when(jnp.logical_not(by_hub(peer)))
            def _():
                message(peer).start()

    urgent = jnp.minimum(gx, 2)

    @pl.loop(0, urgent)
    def _(peer):
        rims(peer, begin)

    @pl.when(odd)
    def _():
        send_down(0, jnp.minimum(gx, 1))
        send_down(2, gx)

    @pl.when(even & (gx > 0))
    def _():
        cut_message(1).start()

    @pl.loop(urgent, gx + 1)
    def _(peer):
        rims(peer, begin)

    interface(0, 0)
    interface(0, 1)

    if split:
        @pl.when(gx == half - 1)
        def _():
            twin_message(0, half - 2).start()

    def pack(c, acc):
        new = []
        for part in range(2):
            src = turned.at[part, c]
            first = src[:, 0:LANES][:, 0:1]
            last = src[:, lines - LANES : lines][:, LANES - 1 : LANES]
            new.append(jnp.where(lane == lax.rem(2 * c + LANES - 1, LANES), first, acc[2 * part]))
            new.append(jnp.where(lane == 2 * c, last, acc[2 * part + 1]))
        return tuple(new)

    zero_edge = jnp.zeros((planes, LANES), jnp.float32)
    packed = lax.fori_loop(0, cells, pack, (zero_edge,) * 4, unroll=4)
    for part in range(2):
        edge[0, part] = packed[2 * part]
        edge[1, part] = packed[2 * part + 1]

    down = pltpu.make_async_remote_copy(edge.at[0], halo.at[1], hs_sem.at[0], hr_sem.at[1],
                                        device_id={"gy": gy - 1}, device_id_type=MESH)
    up = pltpu.make_async_remote_copy(edge.at[1], halo.at[0], hs_sem.at[1], hr_sem.at[0],
                                      device_id={"gy": gy + 1}, device_id_type=MESH)

    @pl.when(gy > 0)
    def _():
        down.start()

    @pl.when(gy == 0)
    def _():
        halo[0] = jnp.zeros(halo.shape[1:], jnp.float32)

    @pl.when(gy < wide - 1)
    def _():
        up.start()

    @pl.when(gy == wide - 1)
    def _():
        halo[1] = jnp.zeros(halo.shape[1:], jnp.float32)

    pl.when(odd)(lambda: send_down(1, jnp.minimum(gx, 2)))
    pl.when(even)(lambda: send_down(1, gx))

    near = jnp.where(gx < half, half, count) if split else count

    @pl.loop(gx + 1, near)
    def _(peer):
        pl.semaphore_wait(ready.at[0, peer], 1)
        message(peer).start()

    if split:
        @pl.when((gx == half) & odd)
        def _():
            twin_message(1, half + 1).start()

    col = lax.broadcasted_iota(jnp.int32, (planes, lines), 1)
    row = lax.broadcasted_iota(jnp.int32, (planes, lines), 0)
    at_first, at_last = col == 0, col == lines - 1
    at_bottom, at_top = row == 0, row == planes - 1

    def lap(x, first, last):
        left = jnp.where(at_first, first, pltpu.roll(x, 1, 1))
        right = jnp.where(at_last, last, pltpu.roll(x, lines - 1, 1))
        below = jnp.where(at_bottom, 0.0, pltpu.roll(x, 1, 0))
        above = jnp.where(at_top, 0.0, pltpu.roll(x, planes - 1, 0))
        return ((left + right) + (below + above)) - 4.0 * x

    def stencil(re, im, first, last):
        lap_re = lap(re, first[0], last[0])
        lap_im = lap(im, first[1], last[1])
        return 2.0 * re - RYZ * lap_im, 2.0 * im + RYZ * lap_re

    def fill(i, unused):
        part = pl.ds(i * group, group)
        laps = []
        for p in range(2):
            x = turned[p, part].reshape(group * planes, lines)
            high = x.astype(jnp.bfloat16)
            low = (x - high.astype(jnp.float32)).astype(jnp.bfloat16)
            y = (jnp.dot(high, band[...], preferred_element_type=jnp.float32)
                 + jnp.dot(low, band[...], preferred_element_type=jnp.float32))
            laps.append(y.reshape(group, planes, lines))
        for n in range(group):
            c = i * group + n
            lap_of = []
            for p in range(2):
                x = turned[p, c]
                below = jnp.where(at_bottom, 0.0, pltpu.roll(x, 1, 0))
                above = jnp.where(at_top, 0.0, pltpu.roll(x, planes - 1, 0))
                lap_of.append(laps[p][n] + (below + above))
            rho[0, c] = -inv * (2.0 * turned[1, c] + RYZ * lap_of[0])
            rho[1, c] = inv * (2.0 * turned[0, c] - RYZ * lap_of[1])
        return unused

    group = chunk
    lax.fori_loop(0, cells // group, fill, 0)

    @pl.loop(gx + 1, count)
    def _(peer):
        pl.semaphore_wait(ready.at[1, peer], beyond)
        rims(peer, begin)

    @pl.loop(near, count)
    def _(peer):
        pl.semaphore_wait(ready.at[0, peer], 1)

    def arrival(k):
        return pltpu.make_async_remote_copy(
            fr.at[0], recv.at[k], s_sem.at[k], r_sem.at[k],
            device_id={"gx": k}, device_id_type=MESH)

    def rim_arrival(k, side):
        return pltpu.make_async_remote_copy(
            rim.at[0, 0], beside.at[side, k], es_sem.at[side, k], er_sem.at[side, k],
            device_id={"gx": k, "gy": gy - 1 + 2 * side}, device_id_type=MESH)

    zero_rim = jnp.zeros((1, LANES), jnp.float32)

    @pl.when(gy == 0)
    def _():
        beside[0] = jnp.zeros(beside.shape[1:], jnp.float32)

    @pl.when(gy == wide - 1)
    def _():
        beside[1] = jnp.zeros(beside.shape[1:], jnp.float32)

    def take_rim(k, acc):
        @pl.when(gy > 0)
        def _():
            rim_arrival(k, 0).wait_recv()

        @pl.when(gy < wide - 1)
        def _():
            rim_arrival(k, 1).wait_recv()

        return acc[0] + beside[0, k], acc[1] + beside[1, k]

    def take(k, acc):
        cut = even & (gx == 0)

        @pl.when(cut)
        def _():
            for part in range(2):
                pltpu.make_async_remote_copy(
                    fr.at[1, :, rows[part]], recv.at[k, :, rows[part]], cut_sem.at[0, part], c_sem.at[part, k],
                    device_id={"gx": k}, device_id_type=MESH).wait_recv()

        @pl.when(jnp.logical_not(cut))
        def _():
            arrival(k).wait_recv()

        return acc[0] + recv[k, 0], acc[1] + recv[k, 1]

    def keep(which, value):
        total[which, 0] = value[0]
        total[which, 1] = value[1]

    def pass_on(which, value):
        relay[which, 0] = value[0]
        relay[which, 1] = value[1]
        hub_do(which, begin)

    def take_twin(value):
        twin_message(0, gx).wait_recv()
        return value[0] + twin[0], value[1] + twin[1]

    def take_left():
        if not split:
            keep(0, lax.fori_loop(0, gx, take, (zero, zero)))
            return
        above = gx >= half
        value = lax.fori_loop(jnp.where(above, half, 0), gx, take, (zero, zero))
        hub = half - 2 + lax.rem(gx, 2)
        value = lax.fori_loop(hub, hub + jnp.where(above, 1, 0), take, value)
        keep(0, value)
        value = value[0] + fr[0, 0], value[1] + fr[0, 1]

        @pl.when(gx == half - 1)
        def _():
            pass_on(0, value)

        @pl.when(gx == half - 2)
        def _():
            pass_on(0, take_twin(value))

    def take_right():
        own = (fr[1, 0], fr[1, 1])
        value = lax.fori_loop(gx + 1, count, take, own)
        keep(1, value)

        if not split:
            return

        @pl.when((gx == half) & odd)
        def _():
            pass_on(1, value)

        @pl.when((gx == half + 1) & odd)
        def _():
            pass_on(1, take_twin(value))

    def settle():
        @pl.when(not_low)
        def _():
            up.wait_recv()

        @pl.when(not_high)
        def _():
            down.wait_recv()

        wanted = [(inv * RYZ) * (halo[0, p] + halo[1, p]) for p in range(2)]

        def mend(c, unused):
            for p in range(2):
                h = pltpu.roll(wanted[p], LANES - 2 * c, 1)
                for side, at in enumerate((0, lines - LANES)):
                    old = rho[p, c, :, at : at + LANES]
                    rho[p, c, :, at : at + LANES] = jnp.where(lane == side * (LANES - 1), old - h, old)
            return unused

        lax.fori_loop(0, cells, mend, 0, unroll=8)

        @pl.when(even & (gx > 0))
        def _():
            for part in range(2):
                cut_message(part).wait_send()

        @pl.loop(0, count)
        def _(peer):
            @pl.when((peer != gx) & jnp.logical_not(by_hub(peer)) & (odd | (peer > 0)))
            def _():
                message(peer).wait_send()

            rims(peer, end)

        @pl.when(not_low)
        def _():
            down.wait_send()

        @pl.when(not_high)
        def _():
            up.wait_send()

        for n, row in enumerate(lax.fori_loop(0, gx, take_rim, (zero_rim, zero_rim))
                                + lax.fori_loop(gx, jnp.where(gx < half, gx + 1, count), take_rim,
                                                (zero_rim, zero_rim))):
            rim_sum[n] = row

    def take_right_low():
        between = (gx >= 2) & (gx < half) & odd & split
        stop = jnp.where(between, half, count)

        def take_both(k, acc):
            return take(k, acc[:2]) + take_rim(k, acc[2:])

        acc = lax.fori_loop(gx + 1, stop, take_both, (fr[1, 0], fr[1, 1], rim_sum[2], rim_sum[3]))
        value, row = acc[:2], lax.fori_loop(stop, count, take_rim, acc[2:])
        hub = half + lax.rem(gx, 2)
        keep(1, lax.fori_loop(hub, hub + jnp.where(between, 1, 0), take, value))
        rim_sum[2] = row[0]
        rim_sum[3] = row[1]

    pl.when(gx < half)(take_left)
    pl.when(gx >= half)(take_right)
    settle()
    pl.when(gx < half)(take_right_low)
    pl.when(gx >= half)(take_left)
    left = (total[0, 0], total[0, 1], rim_sum[0], rim_sum[1])
    right = (total[1, 0], total[1, 1], rim_sum[2], rim_sum[3])

    def spread(side):
        columns = []
        for tile in side[2:]:
            columns.append(tuple(
                jnp.sum(jnp.where(lane_row == part * planes, tile, 0.0), axis=1, keepdims=True) for part in range(2)))
        return stencil(side[0], side[1], columns[0], columns[1])

    left = spread(left)
    right = spread(right)
    w = both(scalar(4), left, scalar(5), right)
    d = both(scalar(6), left, scalar(7), right)

    for index, value in enumerate(w + d):
        start[index] = value

    if split:
        pl.when((gx == half - 2) | (gx == half - 1))(lambda: hub_do(0, end))
        pl.when(((gx == half) | (gx == half + 1)) & odd)(lambda: hub_do(1, end))

        @pl.when((gx == half - 1) | ((gx == half) & odd))
        def _():
            twin_message(0, gx).wait_send()


def finish(coef, chunk, turned, rho, start, out, out_v, out_sem):
    cells = turned.shape[1]
    chunks = cells // chunk
    inv = np.float32(1.0 / coef)

    def store(i):
        part = pl.ds(i * chunk, chunk)
        return pltpu.make_async_copy(out_v.at[:, part], out.at[:, part], out_sem.at[i])

    def march(c, carry):
        w_re, w_im, d_re, d_im = carry
        w_re = w_re + d_re
        w_im = w_im + d_im
        out_v[0, c] = w_re - turned[0, c]
        out_v[1, c] = w_im - turned[1, c]
        d_re = (d_re + rho[0, c]) + inv * w_im
        d_im = (d_im + rho[1, c]) - inv * w_re
        return w_re, w_im, d_re, d_im

    carry = (start[0], start[1], start[2], start[3])
    for i in range(chunks):
        carry = lax.fori_loop(i * chunk, (i + 1) * chunk, march, carry, unroll=4)
        store(i).start()
    for i in range(chunks):
        store(i).wait()


def shards(psi, potential):
    unused, cells, planes, lines = psi.shape
    count = lax.axis_size("gx")
    wide = lax.axis_size("gy")
    place, coef = tables(cells, count)
    chunk = 8 if cells % 8 == 0 else cells
    chunks = cells // chunk
    block = (2, cells, planes, lines)
    plane = (planes, lines)
    vmem = pl.BlockSpec(memory_space=pltpu.VMEM)
    held = pl.pallas_call(
        functools.partial(kernel, count, wide, coef, chunk),
        out_shape=[
            jax.ShapeDtypeStruct(block, jnp.float32),
            jax.ShapeDtypeStruct(block, jnp.float32),
            jax.ShapeDtypeStruct((4,) + plane, jnp.float32),
        ],
        in_specs=[
            pl.BlockSpec(memory_space=pltpu.HBM),
            pl.BlockSpec(memory_space=pltpu.HBM),
            pl.BlockSpec(memory_space=pltpu.HBM),
        ],
        out_specs=[vmem] * 3,
        scratch_shapes=[
            pltpu.SMEM(place.shape, jnp.float32),
            pltpu.SemaphoreType.DMA((1,)),
            pltpu.VMEM(block, jnp.float32),
            pltpu.VMEM(block[1:], jnp.float32),
            pltpu.VMEM((2, 2, planes, LANES), jnp.float32),
            pltpu.VMEM((2, 2, planes, LANES), jnp.float32),
            pltpu.VMEM((2, 2) + plane, jnp.float32),
            pltpu.VMEM((count, 2) + plane, jnp.float32),
            pltpu.SemaphoreType.DMA((2, 2, 2)),
            pltpu.SemaphoreType.DMA((2,)),
            pltpu.SemaphoreType.DMA((2,)),
            pltpu.SemaphoreType.DMA((count,)),
            pltpu.SemaphoreType.DMA((count,)),
            pltpu.VMEM((2, 2, 1, LANES), jnp.float32),
            pltpu.VMEM((2, count, 1, LANES), jnp.float32),
            pltpu.SemaphoreType.DMA((2, count)),
            pltpu.SemaphoreType.DMA((2, count)),
            pltpu.VMEM((lines, lines), jnp.bfloat16),
            pltpu.SemaphoreType.REGULAR((2, count)),
            pltpu.VMEM((2, 2) + plane, jnp.float32),
            pltpu.VMEM((4, 1, LANES), jnp.float32),
            pltpu.VMEM((2,) + plane, jnp.float32),
            pltpu.SemaphoreType.DMA((2,)),
            pltpu.VMEM((2, 2) + plane, jnp.float32),
            pltpu.SemaphoreType.DMA((1, 2)),
            pltpu.SemaphoreType.DMA((2, count)),
        ],
        compiler_params=pltpu.CompilerParams(
            collective_id=0, has_side_effects=True, vmem_limit_bytes=24 * 2**20
        ),
    )(*(pltpu.with_memory_space_constraint(x, pltpu.HBM) for x in
        (psi, potential, jnp.asarray(place))))
    return pl.pallas_call(
        functools.partial(finish, coef, chunk),
        out_shape=jax.ShapeDtypeStruct(block, jnp.float32),
        in_specs=[vmem] * 3,
        out_specs=pl.BlockSpec(memory_space=pl.ANY),
        scratch_shapes=[
            pltpu.VMEM(block, jnp.float32),
            pltpu.SemaphoreType.DMA((chunks,)),
        ],
        compiler_params=pltpu.CompilerParams(vmem_limit_bytes=16 * 2**20),
    )(*held)


def solution(mesh):
    return jax.shard_map(
        shards,
        mesh=mesh,
        in_specs=(P(None, "gx", None, "gy"), P("gx", None, "gy")),
        out_specs=P(None, "gx", None, "gy"),
        check_vma=False,
    )
```

```python
import functools

import jax
import jax.numpy as jnp
import numpy as np
from jax import lax
from jax.experimental import pallas as pl
from jax.experimental.pallas import tpu as pltpu
from jax.sharding import PartitionSpec as P

RYZ = 2.0
LANES = 128
MESH = pl.DeviceIdType.MESH


def tables(cells, count):
    coef = 256.0 * cells * cells
    total = cells * count
    lam = np.arccosh(np.complex128(1.0 - 0.5j / coef))
    sh = lambda m: np.sinh(lam * m)
    scale = -(1j / coef) / (sh(1) * sh(total + 1))
    x0 = cells * np.arange(count, dtype=np.float64)
    end = x0 + cells
    f_q = sh(end) - sh(end + 1)
    f_e = sh(end + 1)
    r_q = sh(total + 1 - end) - sh(total - end)
    r_e = sh(total - end)
    w_l = scale * sh(total + 1 - x0)
    w_r = scale * sh(x0)
    d_l = scale * (sh(total - x0) - sh(total + 1 - x0))
    d_r = scale * (sh(x0 + 1) - sh(x0))
    rows = [f_q, f_e, r_q, r_e, w_l, w_r, d_l, d_r]
    place = np.stack([part for row in rows for part in (row.real, row.imag)], axis=1)
    return place.astype(np.float32).reshape(-1), coef


HALF_SINE = (4.442882834149953, -7.308241154547353, 3.6062889582396482, -0.8457635962213053, 0.10920575376953141)
HALF_COSINE = (1.4142134965650301, -6.9788509882409375, 5.739461170721302, -1.883562987555641, 0.3106981923194725)


def turn(re, im, pot):
    t = (pot + re * re + im * im) * np.float32(0.25 / np.pi)
    f = t - jnp.round(t)
    f2 = f * f
    s = np.float32(HALF_SINE[-1])
    for a in HALF_SINE[-2::-1]:
        s = s * f2 + np.float32(a)
    s = s * f
    c = np.float32(HALF_COSINE[-1])
    for a in HALF_COSINE[-2::-1]:
        c = c * f2 + np.float32(a)
    sine = s * c
    cosine = 1.0 - s * s
    return re * cosine + im * sine, im * cosine - re * sine


def kernel(count, wide, coef, chunk, psi, pot, place_in, turned, rho,
           start, place_ref, table_sem, psi_v, pot_v, edge, halo, fr, recv, in_sem, hs_sem, hr_sem, s_sem, r_sem,
           rim, beside, es_sem, er_sem, band, ready, relay, rim_sum, twin, t_sem, total, cut_sem, c_sem):
    cells, planes, lines = pot_v.shape
    gx = lax.axis_index("gx")
    gy = lax.axis_index("gy")
    inv = np.float32(1.0 / coef)

    rows = [pl.ds(part * (planes // 2), planes // 2) for part in range(2)]
    loads = 2 if cells % 2 == 0 else 1
    step = cells // loads

    def load(part, i):
        at = pl.ds(i * step, step)
        return (
            pltpu.make_async_copy(psi.at[:, at, rows[part]], psi_v.at[:, at, rows[part]], in_sem.at[0, part, i]),
            pltpu.make_async_copy(pot.at[at, rows[part]], pot_v.at[at, rows[part]], in_sem.at[1, part, i]),
        )

    for part in range(2):
        for i in range(loads):
            for copy in load(part, i):
                copy.start()

    table = pltpu.make_async_copy(place_in, place_ref, table_sem.at[0])
    table.start()

    barrier = pltpu.get_barrier_semaphore()
    not_low, not_high = gy > 0, gy < wide - 1
    beyond = jnp.where(not_low, 1, 0) + jnp.where(not_high, 1, 0)

    def beside_do(do):
        @pl.when(not_low)
        def _():
            do(gy - 1)

        @pl.when(not_high)
        def _():
            do(gy + 1)

    def greet(x, y):
        pl.semaphore_signal(barrier, inc=1, device_id={"gx": x, "gy": y}, device_id_type=MESH)

    beside_do(lambda y: greet(gx, y))

    @pl.loop(gx + 1, count)
    def _(k):
        greet(k, gy)
        beside_do(lambda y: greet(k, y))

    across = lax.broadcasted_iota(jnp.int32, (lines, lines), 0) - lax.broadcasted_iota(jnp.int32, (lines, lines), 1)
    band[...] = jnp.where(across == 0, -4.0, jnp.where(jnp.abs(across) == 1, 1.0, 0.0)).astype(jnp.bfloat16)

    def tell(x, y):
        pl.semaphore_signal(ready.at[jnp.where(y == gy, gx, count)], inc=1, device_id={"gx": x, "gy": y},
                            device_id_type=MESH)

    def meet():
        pl.semaphore_wait(barrier, gx * (1 + beyond) + beyond)

        @pl.loop(0, gx)
        def _(k):
            tell(k, gy)
            beside_do(lambda y: tell(k, y))

    def scalar(index):
        return place_ref[gx * 16 + 2 * index], place_ref[gx * 16 + 2 * index + 1]

    def both(a, x, b, y):
        return (
            (a[0] * x[0] - a[1] * x[1]) + (b[0] * y[0] - b[1] * y[1]),
            (a[0] * x[1] + a[1] * x[0]) + (b[0] * y[1] + b[1] * y[0]),
        )

    lane = lax.broadcasted_iota(jnp.int32, (planes, LANES), 1)
    lane_row = lane - lax.broadcasted_iota(jnp.int32, (planes, LANES), 0)
    row_rim = lane_row[0 : planes // 2]

    def interface(which, part):
        e_re, e_im, q_re, q_im = sums[part]
        value = both(scalar(2 * which), (q_re, q_im), scalar(2 * which + 1), (e_re, e_im))
        fr[which, 0, rows[part]] = value[0]
        fr[which, 1, rows[part]] = value[1]
        shift = part * (planes // 2)
        for side in range(2):
            at = side * (lines - 1)
            tile = jnp.where(row_rim == shift, value[0][:, at : at + 1],
                             jnp.where(row_rim == shift + planes, value[1][:, at : at + 1], 0.0))
            row = jnp.sum(tile, axis=0, keepdims=True)
            rim[which, side] = row if part == 0 else rim[which, side] + row

    half = count // 2
    split = count >= 8 and count % 4 == 0
    odd = lax.rem(gy, 2) == 1

    def by_hub(peer):
        if not split:
            return peer < 0
        return ((gx < half) & (peer >= half)) | ((gx >= half) & (peer >= 2) & (peer < half) & odd)

    def message(peer):
        return pltpu.make_async_remote_copy(
            fr.at[jnp.where(peer < gx, 1, 0)], recv.at[gx], s_sem.at[peer], r_sem.at[gx],
            device_id={"gx": peer}, device_id_type=MESH)

    def cut_message(part):
        return pltpu.make_async_remote_copy(
            fr.at[1, :, rows[part]], recv.at[gx, :, rows[part]], s_sem.at[0] if part else cut_sem.at[0], r_sem.at[gx] if part else c_sem.at[gx],
            device_id={"gx": 0}, device_id_type=MESH)

    def hub_message(which, peer):
        return pltpu.make_async_remote_copy(
            relay.at[which], recv.at[gx], s_sem.at[peer], r_sem.at[gx],
            device_id={"gx": peer}, device_id_type=MESH)

    def twin_message(which, peer):
        return pltpu.make_async_remote_copy(
            fr.at[which], twin, t_sem.at[0], t_sem.at[1],
            device_id={"gx": peer}, device_id_type=MESH)

    def hub_do(which, do):
        parity = lax.rem(gx, 2)

        @pl.loop(0, half // 2 - which)
        def _(n):
            do(hub_message(which, (half if which == 0 else 2) + 2 * n + parity))

    def rim_message(peer, side):
        return pltpu.make_async_remote_copy(
            rim.at[jnp.where(peer <= gx, 1, 0), side], beside.at[1 - side, gx],
            es_sem.at[side], er_sem.at[1 - side],
            device_id={"gx": peer, "gy": gy - 1 + 2 * side}, device_id_type=MESH)

    def rims(peer, do):
        @pl.when(not_low)
        def _():
            do(rim_message(peer, 0))

        @pl.when(not_high)
        def _():
            do(rim_message(peer, 1))

    def begin(copy):
        copy.start()

    def end(copy):
        copy.wait_send()

    def advance(part):
        at = rows[part]

        def one(c, carry):
            e_re, e_im, q_re, q_im = carry
            t_re, t_im = turn(psi_v[0, c, at], psi_v[1, c, at], pot_v[c, at])
            turned[0, c, at] = t_re
            turned[1, c, at] = t_im
            e_re = (e_re + t_re) + inv * q_im
            e_im = (e_im + t_im) - inv * q_re
            return e_re, e_im, q_re + e_re, q_im + e_im

        carry = (jnp.zeros((planes // 2, lines), jnp.float32),) * 4
        for i in range(loads):
            for copy in load(part, i):
                copy.wait()
            carry = lax.fori_loop(i * step, (i + 1) * step, one, carry, unroll=8)
        return carry

    zero = jnp.zeros((planes, lines), jnp.float32)
    even = jnp.logical_not(odd)
    pl.when(even)(meet)
    sums = [advance(0)]
    table.wait()
    interface(1, 0)

    @pl.when(even & (gx > 0))
    def _():
        cut_message(0).start()

    sums.append(advance(1))
    interface(1, 1)
    pl.when(odd)(meet)

    def send_down(start, stop):
        @pl.loop(start, stop)
        def _(peer):
            @pl.when(jnp.logical_not(by_hub(peer)))
            def _():
                message(peer).start()

    urgent = jnp.minimum(gx, 2)

    @pl.loop(0, urgent)
    def _(peer):
        rims(peer, begin)

    @pl.when(odd)
    def _():
        send_down(0, jnp.minimum(gx, 1))
        send_down(2, gx)

    @pl.when(even & (gx > 0))
    def _():
        cut_message(1).start()

    @pl.loop(urgent, gx + 1)
    def _(peer):
        rims(peer, begin)

    interface(0, 0)
    interface(0, 1)

    if split:
        @pl.when(gx == half - 1)
        def _():
            twin_message(0, half - 2).start()

    def pack(c, acc):
        new = []
        for part in range(2):
            src = turned.at[part, c]
            first = src[:, 0:LANES][:, 0:1]
            last = src[:, lines - LANES : lines][:, LANES - 1 : LANES]
            new.append(jnp.where(lane == lax.rem(2 * c + LANES - 1, LANES), first, acc[2 * part]))
            new.append(jnp.where(lane == 2 * c, last, acc[2 * part + 1]))
        return tuple(new)

    zero_edge = jnp.zeros((planes, LANES), jnp.float32)
    packed = lax.fori_loop(0, cells, pack, (zero_edge,) * 4, unroll=4)
    for part in range(2):
        edge[0, part] = packed[2 * part]
        edge[1, part] = packed[2 * part + 1]

    down = pltpu.make_async_remote_copy(edge.at[0], halo.at[1], hs_sem.at[0], hr_sem.at[1],
                                        device_id={"gy": gy - 1}, device_id_type=MESH)
    up = pltpu.make_async_remote_copy(edge.at[1], halo.at[0], hs_sem.at[1], hr_sem.at[0],
                                      device_id={"gy": gy + 1}, device_id_type=MESH)

    @pl.when(gy > 0)
    def _():
        down.start()

    @pl.when(gy == 0)
    def _():
        halo[0] = jnp.zeros(halo.shape[1:], jnp.float32)

    @pl.when(gy < wide - 1)
    def _():
        up.start()

    @pl.when(gy == wide - 1)
    def _():
        halo[1] = jnp.zeros(halo.shape[1:], jnp.float32)

    pl.when(odd)(lambda: send_down(1, jnp.minimum(gx, 2)))
    pl.when(even)(lambda: send_down(1, gx))

    near = jnp.where(gx < half, half, count) if split else count

    @pl.loop(gx + 1, near)
    def _(peer):
        pl.semaphore_wait(ready.at[peer], 1)
        message(peer).start()

    if split:
        @pl.when((gx == half) & odd)
        def _():
            twin_message(1, half + 1).start()

    col = lax.broadcasted_iota(jnp.int32, (planes, lines), 1)
    row = lax.broadcasted_iota(jnp.int32, (planes, lines), 0)
    at_first, at_last = col == 0, col == lines - 1
    at_bottom, at_top = row == 0, row == planes - 1

    def lap(x, first, last):
        left = jnp.where(at_first, first, pltpu.roll(x, 1, 1))
        right = jnp.where(at_last, last, pltpu.roll(x, lines - 1, 1))
        below = jnp.where(at_bottom, 0.0, pltpu.roll(x, 1, 0))
        above = jnp.where(at_top, 0.0, pltpu.roll(x, planes - 1, 0))
        return ((left + right) + (below + above)) - 4.0 * x

    def stencil(re, im, first, last):
        lap_re = lap(re, first[0], last[0])
        lap_im = lap(im, first[1], last[1])
        return 2.0 * re - RYZ * lap_im, 2.0 * im + RYZ * lap_re

    def fill(i, unused):
        part = pl.ds(i * group, group)
        laps = []
        for p in range(2):
            x = turned[p, part].reshape(group * planes, lines)
            high = x.astype(jnp.bfloat16)
            low = (x - high.astype(jnp.float32)).astype(jnp.bfloat16)
            y = (jnp.dot(high, band[...], preferred_element_type=jnp.float32)
                 + jnp.dot(low, band[...], preferred_element_type=jnp.float32))
            laps.append(y.reshape(group, planes, lines))
        for n in range(group):
            c = i * group + n
            lap_of = []
            for p in range(2):
                x = turned[p, c]
                below = jnp.where(at_bottom, 0.0, pltpu.roll(x, 1, 0))
                above = jnp.where(at_top, 0.0, pltpu.roll(x, planes - 1, 0))
                lap_of.append(laps[p][n] + (below + above))
            rho[0, c] = -inv * (2.0 * turned[1, c] + RYZ * lap_of[0])
            rho[1, c] = inv * (2.0 * turned[0, c] - RYZ * lap_of[1])
        return unused

    group = chunk
    lax.fori_loop(0, cells // group, fill, 0)

    @pl.when((gx < count - 1) & (beyond > 0))
    def _():
        pl.semaphore_wait(ready.at[count], beyond * (count - 1 - gx))

    @pl.loop(gx + 1, count)
    def _(peer):
        rims(peer, begin)

    @pl.loop(near, count)
    def _(peer):
        pl.semaphore_wait(ready.at[peer], 1)

    def arrival(k):
        return pltpu.make_async_remote_copy(
            fr.at[0], recv.at[k], s_sem.at[k], r_sem.at[k],
            device_id={"gx": k}, device_id_type=MESH)

    def all_rims(side):
        return pltpu.make_async_remote_copy(
            beside.at[side], beside.at[side], es_sem.at[side], er_sem.at[side],
            device_id={"gy": gy - 1 + 2 * side}, device_id_type=MESH)

    def both_rims(do):
        @pl.when(not_low)
        def _():
            do(all_rims(0))

        @pl.when(not_high)
        def _():
            do(all_rims(1))

    zero_rim = jnp.zeros((1, LANES), jnp.float32)

    @pl.when(gy == 0)
    def _():
        beside[0] = jnp.zeros(beside.shape[1:], jnp.float32)

    @pl.when(gy == wide - 1)
    def _():
        beside[1] = jnp.zeros(beside.shape[1:], jnp.float32)

    def sum_rims():
        both_rims(lambda copy: copy.wait_recv())

        def add(k, acc):
            return acc[0] + beside[0, k], acc[1] + beside[1, k]

        for n, row in enumerate(lax.fori_loop(0, gx, add, (zero_rim, zero_rim))
                                + lax.fori_loop(gx, count, add, (zero_rim, zero_rim))):
            rim_sum[n] = row

    def take(k, acc):
        cut = even & (gx == 0)

        @pl.when(cut)
        def _():
            for part in range(2):
                pltpu.make_async_remote_copy(
                    fr.at[1, :, rows[part]], recv.at[k, :, rows[part]], s_sem.at[0] if part else cut_sem.at[0], r_sem.at[k] if part else c_sem.at[k],
                    device_id={"gx": k}, device_id_type=MESH).wait_recv()

        @pl.when(jnp.logical_not(cut))
        def _():
            arrival(k).wait_recv()

        return acc[0] + recv[k, 0], acc[1] + recv[k, 1]

    def keep(which, value):
        total[which, 0] = value[0]
        total[which, 1] = value[1]

    def pass_on(which, value):
        relay[which, 0] = value[0]
        relay[which, 1] = value[1]
        hub_do(which, begin)

    def take_twin(value):
        twin_message(0, gx).wait_recv()
        return value[0] + twin[0], value[1] + twin[1]

    def take_left():
        if not split:
            keep(0, lax.fori_loop(0, gx, take, (zero, zero)))
            return
        above = gx >= half
        value = lax.fori_loop(jnp.where(above, half, 0), gx, take, (zero, zero))
        hub = half - 2 + lax.rem(gx, 2)
        value = lax.fori_loop(hub, hub + jnp.where(above, 1, 0), take, value)
        keep(0, value)
        value = value[0] + fr[0, 0], value[1] + fr[0, 1]

        @pl.when(gx == half - 1)
        def _():
            pass_on(0, value)

        @pl.when(gx == half - 2)
        def _():
            pass_on(0, take_twin(value))

    def take_right():
        own = (fr[1, 0], fr[1, 1])
        value = lax.fori_loop(gx + 1, count, take, own)
        keep(1, value)

        if not split:
            return

        @pl.when((gx == half) & odd)
        def _():
            pass_on(1, value)

        @pl.when((gx == half + 1) & odd)
        def _():
            pass_on(1, take_twin(value))

    def settle():
        @pl.when(not_low)
        def _():
            up.wait_recv()

        @pl.when(not_high)
        def _():
            down.wait_recv()

        wanted = [(inv * RYZ) * (halo[0, p] + halo[1, p]) for p in range(2)]

        def mend(c, unused):
            for p in range(2):
                h = pltpu.roll(wanted[p], LANES - 2 * c, 1)
                for side, at in enumerate((0, lines - LANES)):
                    old = rho[p, c, :, at : at + LANES]
                    rho[p, c, :, at : at + LANES] = jnp.where(lane == side * (LANES - 1), old - h, old)
            return unused

        lax.fori_loop(0, cells, mend, 0, unroll=8)

        @pl.when(even & (gx > 0))
        def _():
            for part in range(2):
                cut_message(part).wait_send()

        @pl.loop(0, count)
        def _(peer):
            @pl.when((peer != gx) & jnp.logical_not(by_hub(peer)) & (odd | (peer > 0)))
            def _():
                message(peer).wait_send()

        @pl.when(not_low)
        def _():
            down.wait_send()

        @pl.when(not_high)
        def _():
            up.wait_send()

        both_rims(end)
        pl.when(gx >= half)(sum_rims)

    def take_right_low():
        between = (gx >= 2) & (gx < half) & odd & split
        stop = jnp.where(between, half, count)

        value = lax.fori_loop(gx + 1, stop, take, (fr[1, 0], fr[1, 1]))
        hub = half + lax.rem(gx, 2)
        keep(1, lax.fori_loop(hub, hub + jnp.where(between, 1, 0), take, value))
        sum_rims()

    pl.when(gx < half)(take_left)
    pl.when(gx >= half)(take_right)
    settle()
    pl.when(gx < half)(take_right_low)
    pl.when(gx >= half)(take_left)
    left = (total[0, 0], total[0, 1], rim_sum[0], rim_sum[1])
    right = (total[1, 0], total[1, 1], rim_sum[2], rim_sum[3])

    def spread(side):
        columns = []
        for tile in side[2:]:
            columns.append(tuple(
                jnp.sum(jnp.where(lane_row == part * planes, tile, 0.0), axis=1, keepdims=True) for part in range(2)))
        return stencil(side[0], side[1], columns[0], columns[1])

    left = spread(left)
    right = spread(right)
    w = both(scalar(4), left, scalar(5), right)
    d = both(scalar(6), left, scalar(7), right)

    for index, value in enumerate(w + d):
        start[index] = value

    if split:
        pl.when((gx == half - 2) | (gx == half - 1))(lambda: hub_do(0, end))
        pl.when(((gx == half) | (gx == half + 1)) & odd)(lambda: hub_do(1, end))

        @pl.when((gx == half - 1) | ((gx == half) & odd))
        def _():
            twin_message(0, gx).wait_send()


def finish(coef, chunk, turned, rho, start, out, out_v, out_sem):
    cells = turned.shape[1]
    chunks = cells // chunk
    inv = np.float32(1.0 / coef)

    def store(i):
        part = pl.ds(i * chunk, chunk)
        return pltpu.make_async_copy(out_v.at[:, part], out.at[:, part], out_sem.at[0])

    def march(c, carry):
        w_re, w_im, d_re, d_im = carry
        w_re = w_re + d_re
        w_im = w_im + d_im
        out_v[0, c] = w_re - turned[0, c]
        out_v[1, c] = w_im - turned[1, c]
        d_re = (d_re + rho[0, c]) + inv * w_im
        d_im = (d_im + rho[1, c]) - inv * w_re
        return w_re, w_im, d_re, d_im

    carry = (start[0], start[1], start[2], start[3])
    for i in range(chunks):
        carry = lax.fori_loop(i * chunk, (i + 1) * chunk, march, carry, unroll=4)
        store(i).start()
    pltpu.make_async_copy(out_v, out, out_sem.at[0]).wait()


def shards(psi, potential):
    unused, cells, planes, lines = psi.shape
    count = lax.axis_size("gx")
    wide = lax.axis_size("gy")
    place, coef = tables(cells, count)
    chunk = 8 if cells % 8 == 0 else cells
    chunks = cells // chunk
    block = (2, cells, planes, lines)
    plane = (planes, lines)
    vmem = pl.BlockSpec(memory_space=pltpu.VMEM)
    held = pl.pallas_call(
        functools.partial(kernel, count, wide, coef, chunk),
        out_shape=[
            jax.ShapeDtypeStruct(block, jnp.float32),
            jax.ShapeDtypeStruct(block, jnp.float32),
            jax.ShapeDtypeStruct((4,) + plane, jnp.float32),
        ],
        in_specs=[
            pl.BlockSpec(memory_space=pltpu.HBM),
            pl.BlockSpec(memory_space=pltpu.HBM),
            pl.BlockSpec(memory_space=pltpu.HBM),
        ],
        out_specs=[vmem] * 3,
        scratch_shapes=[
            pltpu.SMEM(place.shape, jnp.float32),
            pltpu.SemaphoreType.DMA((1,)),
            pltpu.VMEM(block, jnp.float32),
            pltpu.VMEM(block[1:], jnp.float32),
            pltpu.VMEM((2, 2, planes, LANES), jnp.float32),
            pltpu.VMEM((2, 2, planes, LANES), jnp.float32),
            pltpu.VMEM((2, 2) + plane, jnp.float32),
            pltpu.VMEM((count, 2) + plane, jnp.float32),
            pltpu.SemaphoreType.DMA((2, 2, 2)),
            pltpu.SemaphoreType.DMA((2,)),
            pltpu.SemaphoreType.DMA((2,)),
            pltpu.SemaphoreType.DMA((count,)),
            pltpu.SemaphoreType.DMA((count,)),
            pltpu.VMEM((2, 2, 1, LANES), jnp.float32),
            pltpu.VMEM((2, count, 1, LANES), jnp.float32),
            pltpu.SemaphoreType.DMA((2,)),
            pltpu.SemaphoreType.DMA((2,)),
            pltpu.VMEM((lines, lines), jnp.bfloat16),
            pltpu.SemaphoreType.REGULAR((count + 1,)),
            pltpu.VMEM((2, 2) + plane, jnp.float32),
            pltpu.VMEM((4, 1, LANES), jnp.float32),
            pltpu.VMEM((2,) + plane, jnp.float32),
            pltpu.SemaphoreType.DMA((2,)),
            pltpu.VMEM((2, 2) + plane, jnp.float32),
            pltpu.SemaphoreType.DMA((1,)),
            pltpu.SemaphoreType.DMA((count,)),
        ],
        compiler_params=pltpu.CompilerParams(
            collective_id=0, has_side_effects=True, vmem_limit_bytes=24 * 2**20
        ),
    )(*(pltpu.with_memory_space_constraint(x, pltpu.HBM) for x in
        (psi, potential, jnp.asarray(place))))
    return pl.pallas_call(
        functools.partial(finish, coef, chunk),
        out_shape=jax.ShapeDtypeStruct(block, jnp.float32),
        in_specs=[vmem] * 3,
        out_specs=pl.BlockSpec(memory_space=pl.ANY),
        scratch_shapes=[
            pltpu.VMEM(block, jnp.float32),
            pltpu.SemaphoreType.DMA((1,)),
        ],
        compiler_params=pltpu.CompilerParams(vmem_limit_bytes=16 * 2**20),
    )(*held)


def solution(mesh):
    return jax.shard_map(
        shards,
        mesh=mesh,
        in_specs=(P(None, "gx", None, "gy"), P("gx", None, "gy")),
        out_specs=P(None, "gx", None, "gy"),
        check_vma=False,
    )
```

```python
import functools

import jax
import jax.numpy as jnp
import numpy as np
from jax import lax
from jax.experimental import pallas as pl
from jax.experimental.pallas import tpu as pltpu
from jax.sharding import PartitionSpec as P

RYZ = 2.0
LANES = 128
MESH = pl.DeviceIdType.MESH


def tables(cells, count):
    coef = 256.0 * cells * cells
    total = cells * count
    lam = np.arccosh(np.complex128(1.0 - 0.5j / coef))
    sh = lambda m: np.sinh(lam * m)
    scale = -(1j / coef) / (sh(1) * sh(total + 1))
    x0 = cells * np.arange(count, dtype=np.float64)
    end = x0 + cells
    f_q = sh(end) - sh(end + 1)
    f_e = sh(end + 1)
    r_q = sh(total + 1 - end) - sh(total - end)
    r_e = sh(total - end)
    w_l = scale * sh(total + 1 - x0)
    w_r = scale * sh(x0)
    d_l = scale * (sh(total - x0) - sh(total + 1 - x0))
    d_r = scale * (sh(x0 + 1) - sh(x0))
    rows = [f_q, f_e, r_q, r_e, w_l, w_r, d_l, d_r]
    place = np.stack([part for row in rows for part in (row.real, row.imag)], axis=1)
    return place.astype(np.float32).reshape(-1), coef


HALF_SINE = (4.442882834149953, -7.308241154547353, 3.6062889582396482, -0.8457635962213053, 0.10920575376953141)
HALF_COSINE = (1.4142134965650301, -6.9788509882409375, 5.739461170721302, -1.883562987555641, 0.3106981923194725)


def turn(re, im, pot):
    t = (pot + re * re + im * im) * np.float32(0.25 / np.pi)
    f = t - jnp.round(t)
    f2 = f * f
    s = np.float32(HALF_SINE[-1])
    for a in HALF_SINE[-2::-1]:
        s = s * f2 + np.float32(a)
    s = s * f
    c = np.float32(HALF_COSINE[-1])
    for a in HALF_COSINE[-2::-1]:
        c = c * f2 + np.float32(a)
    sine = s * c
    cosine = 1.0 - s * s
    return re * cosine + im * sine, im * cosine - re * sine


def kernel(count, wide, coef, chunk, psi, pot, place_in, turned, rho,
           start, place_ref, table_sem, psi_v, pot_v, edge, halo, fr, recv, in_sem, hs_sem, hr_sem, s_sem, r_sem,
           rim, beside, es_sem, er_sem, band, ready, relay, rim_sum, twin, t_sem, total, cut_sem, c_sem):
    cells, planes, lines = pot_v.shape
    gx = lax.axis_index("gx")
    gy = lax.axis_index("gy")
    inv = np.float32(1.0 / coef)

    rows = [pl.ds(part * (planes // 2), planes // 2) for part in range(2)]
    loads = 2 if cells % 2 == 0 else 1
    step = cells // loads

    def load(part, i):
        at = pl.ds(i * step, step)
        return (
            pltpu.make_async_copy(psi.at[:, at, rows[part]], psi_v.at[:, at, rows[part]], in_sem.at[0, part, i]),
            pltpu.make_async_copy(pot.at[at, rows[part]], pot_v.at[at, rows[part]], in_sem.at[1, part, i]),
        )

    for part in range(2):
        for i in range(loads):
            for copy in load(part, i):
                copy.start()

    table = pltpu.make_async_copy(place_in, place_ref, table_sem.at[0])
    table.start()

    barrier = pltpu.get_barrier_semaphore()
    not_low, not_high = gy > 0, gy < wide - 1
    beyond = jnp.where(not_low, 1, 0) + jnp.where(not_high, 1, 0)

    def beside_do(do):
        @pl.when(not_low)
        def _():
            do(gy - 1)

        @pl.when(not_high)
        def _():
            do(gy + 1)

    def greet(x, y):
        pl.semaphore_signal(barrier, inc=1, device_id={"gx": x, "gy": y}, device_id_type=MESH)

    beside_do(lambda y: greet(gx, y))

    @pl.loop(gx + 1, count)
    def _(k):
        greet(k, gy)
        beside_do(lambda y: greet(k, y))

    across = lax.broadcasted_iota(jnp.int32, (lines, lines), 0) - lax.broadcasted_iota(jnp.int32, (lines, lines), 1)
    band[...] = jnp.where(across == 0, -4.0, jnp.where(jnp.abs(across) == 1, 1.0, 0.0)).astype(jnp.bfloat16)

    def tell(x, y):
        pl.semaphore_signal(ready.at[jnp.where(y == gy, gx, count)], inc=1, device_id={"gx": x, "gy": y},
                            device_id_type=MESH)

    def meet():
        pl.semaphore_wait(barrier, gx * (1 + beyond) + beyond)

        @pl.loop(0, gx)
        def _(k):
            tell(k, gy)
            beside_do(lambda y: tell(k, y))

    def scalar(index):
        return place_ref[gx * 16 + 2 * index], place_ref[gx * 16 + 2 * index + 1]

    def both(a, x, b, y):
        return (
            (a[0] * x[0] - a[1] * x[1]) + (b[0] * y[0] - b[1] * y[1]),
            (a[0] * x[1] + a[1] * x[0]) + (b[0] * y[1] + b[1] * y[0]),
        )

    lane = lax.broadcasted_iota(jnp.int32, (planes, LANES), 1)
    lane_row = lane - lax.broadcasted_iota(jnp.int32, (planes, LANES), 0)
    row_rim = lane_row[0 : planes // 2]

    def interface(which, part):
        e_re, e_im, q_re, q_im = sums[part]
        value = both(scalar(2 * which), (q_re, q_im), scalar(2 * which + 1), (e_re, e_im))
        fr[which, 0, rows[part]] = value[0]
        fr[which, 1, rows[part]] = value[1]
        shift = part * (planes // 2)
        for side in range(2):
            at = side * (lines - 1)
            tile = jnp.where(row_rim == shift, value[0][:, at : at + 1],
                             jnp.where(row_rim == shift + planes, value[1][:, at : at + 1], 0.0))
            row = jnp.sum(tile, axis=0, keepdims=True)
            rim[which, side] = row if part == 0 else rim[which, side] + row

    half = count // 2
    split = count >= 8 and count % 4 == 0
    odd = lax.rem(gy, 2) == 1

    def by_hub(peer):
        if not split:
            return peer < 0
        return ((gx < half) & (peer >= half)) | ((gx >= half) & (peer >= 2) & (peer < half) & odd)

    def message(peer):
        return pltpu.make_async_remote_copy(
            fr.at[jnp.where(peer < gx, 1, 0)], recv.at[gx], s_sem.at[peer], r_sem.at[gx],
            device_id={"gx": peer}, device_id_type=MESH)

    def cut_message(part):
        return pltpu.make_async_remote_copy(
            fr.at[1, :, rows[part]], recv.at[gx, :, rows[part]], s_sem.at[0] if part else cut_sem.at[0], r_sem.at[gx] if part else c_sem.at[0],
            device_id={"gx": 0}, device_id_type=MESH)

    def hub_message(which, peer):
        return pltpu.make_async_remote_copy(
            relay.at[which], recv.at[gx], s_sem.at[peer], r_sem.at[gx],
            device_id={"gx": peer}, device_id_type=MESH)

    def twin_message(which, peer):
        return pltpu.make_async_remote_copy(
            fr.at[which], twin, t_sem.at[0], t_sem.at[1],
            device_id={"gx": peer}, device_id_type=MESH)

    def hub_do(which, do):
        parity = lax.rem(gx, 2)

        @pl.loop(0, half // 2 - which)
        def _(n):
            do(hub_message(which, (half if which == 0 else 2) + 2 * n + parity))

    def rim_message(peer, side):
        return pltpu.make_async_remote_copy(
            rim.at[jnp.where(peer <= gx, 1, 0), side], beside.at[1 - side, gx],
            es_sem.at[side], er_sem.at[1 - side],
            device_id={"gx": peer, "gy": gy - 1 + 2 * side}, device_id_type=MESH)

    def rims(peer, do):
        @pl.when(not_low)
        def _():
            do(rim_message(peer, 0))

        @pl.when(not_high)
        def _():
            do(rim_message(peer, 1))

    def begin(copy):
        copy.start()

    def end(copy):
        copy.wait_send()

    def advance(part):
        at = rows[part]

        def one(c, carry):
            e_re, e_im, q_re, q_im = carry
            t_re, t_im = turn(psi_v[0, c, at], psi_v[1, c, at], pot_v[c, at])
            turned[0, c, at] = t_re
            turned[1, c, at] = t_im
            e_re = (e_re + t_re) + inv * q_im
            e_im = (e_im + t_im) - inv * q_re
            return e_re, e_im, q_re + e_re, q_im + e_im

        carry = (jnp.zeros((planes // 2, lines), jnp.float32),) * 4
        for i in range(loads):
            for copy in load(part, i):
                copy.wait()
            carry = lax.fori_loop(i * step, (i + 1) * step, one, carry, unroll=8)
        return carry

    zero = jnp.zeros((planes, lines), jnp.float32)
    even = jnp.logical_not(odd)
    pl.when(even)(meet)
    sums = [advance(0)]
    table.wait()
    interface(1, 0)

    @pl.when(even & (gx > 0))
    def _():
        cut_message(0).start()

    sums.append(advance(1))
    interface(1, 1)
    pl.when(odd)(meet)

    def send_down(start, stop):
        @pl.loop(start, stop)
        def _(peer):
            @pl.when(jnp.logical_not(by_hub(peer)))
            def _():
                message(peer).start()

    urgent = jnp.minimum(gx, 2)

    @pl.loop(0, urgent)
    def _(peer):
        rims(peer, begin)

    @pl.when(odd)
    def _():
        send_down(0, jnp.minimum(gx, 1))
        send_down(2, gx)

    @pl.when(even & (gx > 0))
    def _():
        cut_message(1).start()

    @pl.loop(urgent, gx + 1)
    def _(peer):
        rims(peer, begin)

    interface(0, 0)
    interface(0, 1)

    if split:
        @pl.when(gx == half - 1)
        def _():
            twin_message(0, half - 2).start()

    def pack(c, acc):
        new = []
        for part in range(2):
            src = turned.at[part, c]
            first = src[:, 0:LANES][:, 0:1]
            last = src[:, lines - LANES : lines][:, LANES - 1 : LANES]
            new.append(jnp.where(lane == lax.rem(2 * c + LANES - 1, LANES), first, acc[2 * part]))
            new.append(jnp.where(lane == 2 * c, last, acc[2 * part + 1]))
        return tuple(new)

    zero_edge = jnp.zeros((planes, LANES), jnp.float32)
    packed = lax.fori_loop(0, cells, pack, (zero_edge,) * 4, unroll=4)
    for part in range(2):
        edge[0, part] = packed[2 * part]
        edge[1, part] = packed[2 * part + 1]

    down = pltpu.make_async_remote_copy(edge.at[0], halo.at[1], hs_sem.at[0], hr_sem.at[1],
                                        device_id={"gy": gy - 1}, device_id_type=MESH)
    up = pltpu.make_async_remote_copy(edge.at[1], halo.at[0], hs_sem.at[1], hr_sem.at[0],
                                      device_id={"gy": gy + 1}, device_id_type=MESH)

    @pl.when(gy > 0)
    def _():
        down.start()

    @pl.when(gy == 0)
    def _():
        halo[0] = jnp.zeros(halo.shape[1:], jnp.float32)

    @pl.when(gy < wide - 1)
    def _():
        up.start()

    @pl.when(gy == wide - 1)
    def _():
        halo[1] = jnp.zeros(halo.shape[1:], jnp.float32)

    pl.when(odd)(lambda: send_down(1, jnp.minimum(gx, 2)))
    pl.when(even)(lambda: send_down(1, gx))

    near = jnp.where(gx < half, half, count) if split else count

    @pl.loop(gx + 1, near)
    def _(peer):
        pl.semaphore_wait(ready.at[peer], 1)
        message(peer).start()

    if split:
        @pl.when((gx == half) & odd)
        def _():
            twin_message(1, half + 1).start()

    col = lax.broadcasted_iota(jnp.int32, (planes, lines), 1)
    row = lax.broadcasted_iota(jnp.int32, (planes, lines), 0)
    at_first, at_last = col == 0, col == lines - 1
    at_bottom, at_top = row == 0, row == planes - 1

    def lap(x, first, last):
        left = jnp.where(at_first, first, pltpu.roll(x, 1, 1))
        right = jnp.where(at_last, last, pltpu.roll(x, lines - 1, 1))
        below = jnp.where(at_bottom, 0.0, pltpu.roll(x, 1, 0))
        above = jnp.where(at_top, 0.0, pltpu.roll(x, planes - 1, 0))
        return ((left + right) + (below + above)) - 4.0 * x

    def stencil(re, im, first, last):
        lap_re = lap(re, first[0], last[0])
        lap_im = lap(im, first[1], last[1])
        return 2.0 * re - RYZ * lap_im, 2.0 * im + RYZ * lap_re

    def fill(i, unused):
        part = pl.ds(i * group, group)
        laps = []
        for p in range(2):
            x = turned[p, part].reshape(group * planes, lines)
            high = x.astype(jnp.bfloat16)
            low = (x - high.astype(jnp.float32)).astype(jnp.bfloat16)
            y = (jnp.dot(high, band[...], preferred_element_type=jnp.float32)
                 + jnp.dot(low, band[...], preferred_element_type=jnp.float32))
            laps.append(y.reshape(group, planes, lines))
        for n in range(group):
            c = i * group + n
            lap_of = []
            for p in range(2):
                x = turned[p, c]
                below = jnp.where(at_bottom, 0.0, pltpu.roll(x, 1, 0))
                above = jnp.where(at_top, 0.0, pltpu.roll(x, planes - 1, 0))
                lap_of.append(laps[p][n] + (below + above))
            rho[0, c] = -inv * (2.0 * turned[1, c] + RYZ * lap_of[0])
            rho[1, c] = inv * (2.0 * turned[0, c] - RYZ * lap_of[1])
        return unused

    group = chunk
    lax.fori_loop(0, cells // group, fill, 0)

    @pl.when((gx < count - 1) & (beyond > 0))
    def _():
        pl.semaphore_wait(ready.at[count], beyond * (count - 1 - gx))

    @pl.loop(gx + 1, count)
    def _(peer):
        rims(peer, begin)

    @pl.loop(near, count)
    def _(peer):
        pl.semaphore_wait(ready.at[peer], 1)

    def arrival(k):
        return pltpu.make_async_remote_copy(
            fr.at[0], recv.at[k], s_sem.at[k], r_sem.at[k],
            device_id={"gx": k}, device_id_type=MESH)

    def all_rims(side):
        return pltpu.make_async_remote_copy(
            beside.at[side], beside.at[side], es_sem.at[side], er_sem.at[side],
            device_id={"gy": gy - 1 + 2 * side}, device_id_type=MESH)

    def both_rims(do):
        @pl.when(not_low)
        def _():
            do(all_rims(0))

        @pl.when(not_high)
        def _():
            do(all_rims(1))

    zero_rim = jnp.zeros((1, LANES), jnp.float32)

    @pl.when(gy == 0)
    def _():
        beside[0] = jnp.zeros(beside.shape[1:], jnp.float32)

    @pl.when(gy == wide - 1)
    def _():
        beside[1] = jnp.zeros(beside.shape[1:], jnp.float32)

    def sum_rims():
        both_rims(lambda copy: copy.wait_recv())

        def add(k, acc):
            return acc[0] + beside[0, k], acc[1] + beside[1, k]

        for n, row in enumerate(lax.fori_loop(0, gx, add, (zero_rim, zero_rim))
                                + lax.fori_loop(gx, count, add, (zero_rim, zero_rim))):
            rim_sum[n] = row

    def take(k, acc):
        cut = even & (gx == 0)

        @pl.when(cut)
        def _():
            pltpu.make_async_remote_copy(
                fr.at[1, :, rows[1]], recv.at[k, :, rows[1]], s_sem.at[0], r_sem.at[k],
                device_id={"gx": k}, device_id_type=MESH).wait_recv()

        @pl.when(jnp.logical_not(cut))
        def _():
            arrival(k).wait_recv()

        return acc[0] + recv[k, 0], acc[1] + recv[k, 1]

    def keep(which, value):
        total[which, 0] = value[0]
        total[which, 1] = value[1]

    def pass_on(which, value):
        relay[which, 0] = value[0]
        relay[which, 1] = value[1]
        hub_do(which, begin)

    def take_twin(value):
        twin_message(0, gx).wait_recv()
        return value[0] + twin[0], value[1] + twin[1]

    def take_left():
        if not split:
            keep(0, lax.fori_loop(0, gx, take, (zero, zero)))
            return
        above = gx >= half
        value = lax.fori_loop(jnp.where(above, half, 0), gx, take, (zero, zero))
        hub = half - 2 + lax.rem(gx, 2)
        value = lax.fori_loop(hub, hub + jnp.where(above, 1, 0), take, value)
        keep(0, value)
        value = value[0] + fr[0, 0], value[1] + fr[0, 1]

        @pl.when(gx == half - 1)
        def _():
            pass_on(0, value)

        @pl.when(gx == half - 2)
        def _():
            pass_on(0, take_twin(value))

    def take_right():
        own = (fr[1, 0], fr[1, 1])
        value = lax.fori_loop(gx + 1, count, take, own)
        keep(1, value)

        if not split:
            return

        @pl.when((gx == half) & odd)
        def _():
            pass_on(1, value)

        @pl.when((gx == half + 1) & odd)
        def _():
            pass_on(1, take_twin(value))

    def settle():
        @pl.when(not_low)
        def _():
            up.wait_recv()

        @pl.when(not_high)
        def _():
            down.wait_recv()

        wanted = [(inv * RYZ) * (halo[0, p] + halo[1, p]) for p in range(2)]

        def mend(c, unused):
            for p in range(2):
                h = pltpu.roll(wanted[p], LANES - 2 * c, 1)
                for side, at in enumerate((0, lines - LANES)):
                    old = rho[p, c, :, at : at + LANES]
                    rho[p, c, :, at : at + LANES] = jnp.where(lane == side * (LANES - 1), old - h, old)
            return unused

        lax.fori_loop(0, cells, mend, 0, unroll=8)

        @pl.when(even & (gx > 0))
        def _():
            for part in range(2):
                cut_message(part).wait_send()

        @pl.loop(0, count)
        def _(peer):
            @pl.when((peer != gx) & jnp.logical_not(by_hub(peer)) & (odd | (peer > 0)))
            def _():
                message(peer).wait_send()

        @pl.when(not_low)
        def _():
            down.wait_send()

        @pl.when(not_high)
        def _():
            up.wait_send()

        both_rims(end)
        pl.when(gx >= half)(sum_rims)

    def take_right_low():
        between = (gx >= 2) & (gx < half) & odd & split
        stop = jnp.where(between, half, count)

        @pl.when(even & (gx == 0))
        def _():
            lower = recv.at[1:count, :, rows[0]]
            pltpu.make_async_remote_copy(lower, lower, cut_sem.at[0], c_sem.at[0],
                                         device_id={"gx": count - 1}, device_id_type=MESH).wait_recv()

        value = lax.fori_loop(gx + 1, stop, take, (fr[1, 0], fr[1, 1]))
        hub = half + lax.rem(gx, 2)
        keep(1, lax.fori_loop(hub, hub + jnp.where(between, 1, 0), take, value))
        sum_rims()

    pl.when(gx < half)(take_left)
    pl.when(gx >= half)(take_right)
    settle()
    pl.when(gx < half)(take_right_low)
    pl.when(gx >= half)(take_left)
    left = (total[0, 0], total[0, 1], rim_sum[0], rim_sum[1])
    right = (total[1, 0], total[1, 1], rim_sum[2], rim_sum[3])

    def spread(side):
        columns = []
        for tile in side[2:]:
            columns.append(tuple(
                jnp.sum(jnp.where(lane_row == part * planes, tile, 0.0), axis=1, keepdims=True) for part in range(2)))
        return stencil(side[0], side[1], columns[0], columns[1])

    left = spread(left)
    right = spread(right)
    w = both(scalar(4), left, scalar(5), right)
    d = both(scalar(6), left, scalar(7), right)

    for index, value in enumerate(w + d):
        start[index] = value

    if split:
        pl.when((gx == half - 2) | (gx == half - 1))(lambda: hub_do(0, end))
        pl.when(((gx == half) | (gx == half + 1)) & odd)(lambda: hub_do(1, end))

        @pl.when((gx == half - 1) | ((gx == half) & odd))
        def _():
            twin_message(0, gx).wait_send()


def finish(coef, chunk, turned, rho, start, out, out_v, out_sem):
    cells = turned.shape[1]
    chunks = cells // chunk
    inv = np.float32(1.0 / coef)

    def store(i):
        part = pl.ds(i * chunk, chunk)
        return pltpu.make_async_copy(out_v.at[:, part], out.at[:, part], out_sem.at[0])

    def march(c, carry):
        w_re, w_im, d_re, d_im = carry
        w_re = w_re + d_re
        w_im = w_im + d_im
        out_v[0, c] = w_re - turned[0, c]
        out_v[1, c] = w_im - turned[1, c]
        d_re = (d_re + rho[0, c]) + inv * w_im
        d_im = (d_im + rho[1, c]) - inv * w_re
        return w_re, w_im, d_re, d_im

    carry = (start[0], start[1], start[2], start[3])
    for i in range(chunks):
        carry = lax.fori_loop(i * chunk, (i + 1) * chunk, march, carry, unroll=4)
        store(i).start()
    pltpu.make_async_copy(out_v, out, out_sem.at[0]).wait()


def shards(psi, potential):
    unused, cells, planes, lines = psi.shape
    count = lax.axis_size("gx")
    wide = lax.axis_size("gy")
    place, coef = tables(cells, count)
    chunk = 8 if cells % 8 == 0 else cells
    chunks = cells // chunk
    block = (2, cells, planes, lines)
    plane = (planes, lines)
    vmem = pl.BlockSpec(memory_space=pltpu.VMEM)
    held = pl.pallas_call(
        functools.partial(kernel, count, wide, coef, chunk),
        out_shape=[
            jax.ShapeDtypeStruct(block, jnp.float32),
            jax.ShapeDtypeStruct(block, jnp.float32),
            jax.ShapeDtypeStruct((4,) + plane, jnp.float32),
        ],
        in_specs=[
            pl.BlockSpec(memory_space=pltpu.HBM),
            pl.BlockSpec(memory_space=pltpu.HBM),
            pl.BlockSpec(memory_space=pltpu.HBM),
        ],
        out_specs=[vmem] * 3,
        scratch_shapes=[
            pltpu.SMEM(place.shape, jnp.float32),
            pltpu.SemaphoreType.DMA((1,)),
            pltpu.VMEM(block, jnp.float32),
            pltpu.VMEM(block[1:], jnp.float32),
            pltpu.VMEM((2, 2, planes, LANES), jnp.float32),
            pltpu.VMEM((2, 2, planes, LANES), jnp.float32),
            pltpu.VMEM((2, 2) + plane, jnp.float32),
            pltpu.VMEM((count, 2) + plane, jnp.float32),
            pltpu.SemaphoreType.DMA((2, 2, 2)),
            pltpu.SemaphoreType.DMA((2,)),
            pltpu.SemaphoreType.DMA((2,)),
            pltpu.SemaphoreType.DMA((count,)),
            pltpu.SemaphoreType.DMA((count,)),
            pltpu.VMEM((2, 2, 1, LANES), jnp.float32),
            pltpu.VMEM((2, count, 1, LANES), jnp.float32),
            pltpu.SemaphoreType.DMA((2,)),
            pltpu.SemaphoreType.DMA((2,)),
            pltpu.VMEM((lines, lines), jnp.bfloat16),
            pltpu.SemaphoreType.REGULAR((count + 1,)),
            pltpu.VMEM((2, 2) + plane, jnp.float32),
            pltpu.VMEM((4, 1, LANES), jnp.float32),
            pltpu.VMEM((2,) + plane, jnp.float32),
            pltpu.SemaphoreType.DMA((2,)),
            pltpu.VMEM((2, 2) + plane, jnp.float32),
            pltpu.SemaphoreType.DMA((1,)),
            pltpu.SemaphoreType.DMA((1,)),
        ],
        compiler_params=pltpu.CompilerParams(
            collective_id=0, has_side_effects=True, vmem_limit_bytes=24 * 2**20
        ),
    )(*(pltpu.with_memory_space_constraint(x, pltpu.HBM) for x in
        (psi, potential, jnp.asarray(place))))
    return pl.pallas_call(
        functools.partial(finish, coef, chunk),
        out_shape=jax.ShapeDtypeStruct(block, jnp.float32),
        in_specs=[vmem] * 3,
        out_specs=pl.BlockSpec(memory_space=pl.ANY),
        scratch_shapes=[
            pltpu.VMEM(block, jnp.float32),
            pltpu.SemaphoreType.DMA((1,)),
        ],
        compiler_params=pltpu.CompilerParams(vmem_limit_bytes=16 * 2**20),
    )(*held)


def solution(mesh):
    return jax.shard_map(
        shards,
        mesh=mesh,
        in_specs=(P(None, "gx", None, "gy"), P("gx", None, "gy")),
        out_specs=P(None, "gx", None, "gy"),
        check_vma=False,
    )
```

```python
import functools

import jax
import jax.numpy as jnp
import numpy as np
from jax import lax
from jax.experimental import pallas as pl
from jax.experimental.pallas import tpu as pltpu
from jax.sharding import PartitionSpec as P

RYZ = 2.0
LANES = 128
MESH = pl.DeviceIdType.MESH


def tables(cells, count):
    coef = 256.0 * cells * cells
    total = cells * count
    lam = np.arccosh(np.complex128(1.0 - 0.5j / coef))
    sh = lambda m: np.sinh(lam * m)
    scale = -(1j / coef) / (sh(1) * sh(total + 1))
    x0 = cells * np.arange(count, dtype=np.float64)
    end = x0 + cells
    f_q = sh(end) - sh(end + 1)
    f_e = sh(end + 1)
    r_q = sh(total + 1 - end) - sh(total - end)
    r_e = sh(total - end)
    w_l = scale * sh(total + 1 - x0)
    w_r = scale * sh(x0)
    d_l = scale * (sh(total - x0) - sh(total + 1 - x0))
    d_r = scale * (sh(x0 + 1) - sh(x0))
    rows = [f_q, f_e, r_q, r_e, w_l, w_r, d_l, d_r]
    place = np.stack([part for row in rows for part in (row.real, row.imag)], axis=1)
    return place.astype(np.float32).reshape(-1), coef


HALF_SINE = (4.442882834149953, -7.308241154547353, 3.6062889582396482, -0.8457635962213053, 0.10920575376953141)
HALF_COSINE = (1.4142134965650301, -6.9788509882409375, 5.739461170721302, -1.883562987555641, 0.3106981923194725)


def turn(re, im, pot):
    t = (pot + re * re + im * im) * np.float32(0.25 / np.pi)
    f = t - jnp.round(t)
    f2 = f * f
    s = np.float32(HALF_SINE[-1])
    for a in HALF_SINE[-2::-1]:
        s = s * f2 + np.float32(a)
    s = s * f
    c = np.float32(HALF_COSINE[-1])
    for a in HALF_COSINE[-2::-1]:
        c = c * f2 + np.float32(a)
    sine = s * c
    cosine = 1.0 - s * s
    return re * cosine + im * sine, im * cosine - re * sine


def kernel(count, wide, coef, chunk, psi, pot, place_in, turned, rho,
           start, place_ref, table_sem, field, edge, halo, fr, recv, in_sem, hs_sem, hr_sem, s_sem, r_sem,
           rim, beside, es_sem, er_sem, band, ready, relay, rim_sum, twin, t_sem, total, cut_sem, c_sem):
    cells, planes, lines = field.shape[1:]
    gx = lax.axis_index("gx")
    gy = lax.axis_index("gy")
    inv = np.float32(1.0 / coef)

    rows = [pl.ds(part * (planes // 2), planes // 2) for part in range(2)]
    loads = 2 if cells % 2 == 0 else 1
    step = cells // loads

    def load(part, i):
        at = pl.ds(i * step, step)
        return (
            pltpu.make_async_copy(psi.at[:, at, rows[part]], field.at[0:2, at, rows[part]], in_sem.at[part, i]),
            pltpu.make_async_copy(pot.at[at, rows[part]], field.at[2, at, rows[part]], in_sem.at[part, i]),
        )

    for part in range(2):
        for i in range(loads):
            for copy in load(part, i):
                copy.start()

    table = pltpu.make_async_copy(place_in, place_ref, table_sem.at[0])
    table.start()

    barrier = pltpu.get_barrier_semaphore()
    not_low, not_high = gy > 0, gy < wide - 1
    beyond = jnp.where(not_low, 1, 0) + jnp.where(not_high, 1, 0)

    def beside_do(do):
        @pl.when(not_low)
        def _():
            do(gy - 1)

        @pl.when(not_high)
        def _():
            do(gy + 1)

    def greet(x, y):
        pl.semaphore_signal(barrier, inc=1, device_id={"gx": x, "gy": y}, device_id_type=MESH)

    beside_do(lambda y: greet(gx, y))

    @pl.loop(gx + 1, count)
    def _(k):
        greet(k, gy)
        beside_do(lambda y: greet(k, y))

    across = lax.broadcasted_iota(jnp.int32, (lines, lines), 0) - lax.broadcasted_iota(jnp.int32, (lines, lines), 1)
    band[...] = jnp.where(across == 0, -4.0, jnp.where(jnp.abs(across) == 1, 1.0, 0.0)).astype(jnp.bfloat16)

    def tell(x, y):
        pl.semaphore_signal(ready.at[jnp.where(y == gy, gx, count)], inc=1, device_id={"gx": x, "gy": y},
                            device_id_type=MESH)

    def meet():
        pl.semaphore_wait(barrier, gx * (1 + beyond) + beyond)

        @pl.loop(0, gx)
        def _(k):
            tell(k, gy)
            beside_do(lambda y: tell(k, y))

    def scalar(index):
        return place_ref[gx * 16 + 2 * index], place_ref[gx * 16 + 2 * index + 1]

    def both(a, x, b, y):
        return (
            (a[0] * x[0] - a[1] * x[1]) + (b[0] * y[0] - b[1] * y[1]),
            (a[0] * x[1] + a[1] * x[0]) + (b[0] * y[1] + b[1] * y[0]),
        )

    lane = lax.broadcasted_iota(jnp.int32, (planes, LANES), 1)
    lane_row = lane - lax.broadcasted_iota(jnp.int32, (planes, LANES), 0)
    row_rim = lane_row[0 : planes // 2]

    def interface(which, part):
        e_re, e_im, q_re, q_im = sums[part]
        value = both(scalar(2 * which), (q_re, q_im), scalar(2 * which + 1), (e_re, e_im))
        fr[which, 0, rows[part]] = value[0]
        fr[which, 1, rows[part]] = value[1]
        shift = part * (planes // 2)
        for side in range(2):
            at = side * (lines - 1)
            tile = jnp.where(row_rim == shift, value[0][:, at : at + 1],
                             jnp.where(row_rim == shift + planes, value[1][:, at : at + 1], 0.0))
            row = jnp.sum(tile, axis=0, keepdims=True)
            rim[which, side] = row if part == 0 else rim[which, side] + row

    half = count // 2
    split = count >= 8 and count % 4 == 0
    odd = lax.rem(gy, 2) == 1

    def by_hub(peer):
        if not split:
            return peer < 0
        return ((gx < half) & (peer >= half)) | ((gx >= half) & (peer >= 2) & (peer < half) & odd)

    def message(peer):
        return pltpu.make_async_remote_copy(
            fr.at[jnp.where(peer < gx, 1, 0)], recv.at[gx], s_sem.at[peer], r_sem.at[gx],
            device_id={"gx": peer}, device_id_type=MESH)

    def cut_message(part):
        return pltpu.make_async_remote_copy(
            fr.at[1, :, rows[part]], recv.at[gx, :, rows[part]], s_sem.at[0] if part else cut_sem.at[0], r_sem.at[gx] if part else c_sem.at[0],
            device_id={"gx": 0}, device_id_type=MESH)

    def hub_message(which, peer):
        return pltpu.make_async_remote_copy(
            relay.at[which], recv.at[gx], s_sem.at[peer], r_sem.at[gx],
            device_id={"gx": peer}, device_id_type=MESH)

    def twin_message(which, peer):
        return pltpu.make_async_remote_copy(
            fr.at[which], twin, t_sem.at[0], t_sem.at[1],
            device_id={"gx": peer}, device_id_type=MESH)

    def hub_do(which, do):
        parity = lax.rem(gx, 2)

        @pl.loop(0, half // 2 - which)
        def _(n):
            do(hub_message(which, (half if which == 0 else 2) + 2 * n + parity))

    def rim_message(peer, side):
        return pltpu.make_async_remote_copy(
            rim.at[jnp.where(peer <= gx, 1, 0), side], beside.at[1 - side, gx],
            es_sem.at[side], er_sem.at[1 - side],
            device_id={"gx": peer, "gy": gy - 1 + 2 * side}, device_id_type=MESH)

    def rims(peer, do):
        @pl.when(not_low)
        def _():
            do(rim_message(peer, 0))

        @pl.when(not_high)
        def _():
            do(rim_message(peer, 1))

    def begin(copy):
        copy.start()

    def end(copy):
        copy.wait_send()

    def advance(part):
        at = rows[part]

        def one(c, carry):
            e_re, e_im, q_re, q_im = carry
            t_re, t_im = turn(field[0, c, at], field[1, c, at], field[2, c, at])
            turned[0, c, at] = t_re
            turned[1, c, at] = t_im
            e_re = (e_re + t_re) + inv * q_im
            e_im = (e_im + t_im) - inv * q_re
            return e_re, e_im, q_re + e_re, q_im + e_im

        carry = (jnp.zeros((planes // 2, lines), jnp.float32),) * 4
        for i in range(loads):
            both_in = field.at[:, pl.ds(i * step, step), at]
            pltpu.make_async_copy(both_in, both_in, in_sem.at[part, i]).wait()
            carry = lax.fori_loop(i * step, (i + 1) * step, one, carry, unroll=8)
        return carry

    zero = jnp.zeros((planes, lines), jnp.float32)
    even = jnp.logical_not(odd)
    pl.when(even)(meet)
    sums = [advance(0)]
    table.wait()
    interface(1, 0)

    @pl.when(even & (gx > 0))
    def _():
        cut_message(0).start()

    sums.append(advance(1))
    interface(1, 1)
    pl.when(odd)(meet)

    def send_down(start, stop):
        @pl.loop(start, stop)
        def _(peer):
            @pl.when(jnp.logical_not(by_hub(peer)))
            def _():
                message(peer).start()

    urgent = jnp.minimum(gx, 2)

    @pl.loop(0, urgent)
    def _(peer):
        rims(peer, begin)

    @pl.when(odd)
    def _():
        send_down(0, jnp.minimum(gx, 1))
        send_down(2, gx)

    @pl.when(even & (gx > 0))
    def _():
        cut_message(1).start()

    @pl.loop(urgent, gx + 1)
    def _(peer):
        rims(peer, begin)

    interface(0, 0)
    interface(0, 1)

    if split:
        @pl.when(gx == half - 1)
        def _():
            twin_message(0, half - 2).start()

    def pack(c, acc):
        new = []
        for part in range(2):
            src = turned.at[part, c]
            first = src[:, 0:LANES][:, 0:1]
            last = src[:, lines - LANES : lines][:, LANES - 1 : LANES]
            new.append(jnp.where(lane == lax.rem(2 * c + LANES - 1, LANES), first, acc[2 * part]))
            new.append(jnp.where(lane == 2 * c, last, acc[2 * part + 1]))
        return tuple(new)

    zero_edge = jnp.zeros((planes, LANES), jnp.float32)
    packed = lax.fori_loop(0, cells, pack, (zero_edge,) * 4, unroll=4)
    for part in range(2):
        edge[0, part] = packed[2 * part]
        edge[1, part] = packed[2 * part + 1]

    down = pltpu.make_async_remote_copy(edge.at[0], halo.at[1], hs_sem.at[0], hr_sem.at[1],
                                        device_id={"gy": gy - 1}, device_id_type=MESH)
    up = pltpu.make_async_remote_copy(edge.at[1], halo.at[0], hs_sem.at[1], hr_sem.at[0],
                                      device_id={"gy": gy + 1}, device_id_type=MESH)

    @pl.when(gy > 0)
    def _():
        down.start()

    @pl.when(gy == 0)
    def _():
        halo[0] = jnp.zeros(halo.shape[1:], jnp.float32)

    @pl.when(gy < wide - 1)
    def _():
        up.start()

    @pl.when(gy == wide - 1)
    def _():
        halo[1] = jnp.zeros(halo.shape[1:], jnp.float32)

    pl.when(odd)(lambda: send_down(1, jnp.minimum(gx, 2)))
    pl.when(even)(lambda: send_down(1, gx))

    near = jnp.where(gx < half, half, count) if split else count

    @pl.loop(gx + 1, near)
    def _(peer):
        pl.semaphore_wait(ready.at[peer], 1)
        message(peer).start()

    if split:
        @pl.when((gx == half) & odd)
        def _():
            twin_message(1, half + 1).start()

    col = lax.broadcasted_iota(jnp.int32, (planes, lines), 1)
    row = lax.broadcasted_iota(jnp.int32, (planes, lines), 0)
    at_first, at_last = col == 0, col == lines - 1
    at_bottom, at_top = row == 0, row == planes - 1

    def lap(x, first, last):
        left = jnp.where(at_first, first, pltpu.roll(x, 1, 1))
        right = jnp.where(at_last, last, pltpu.roll(x, lines - 1, 1))
        below = jnp.where(at_bottom, 0.0, pltpu.roll(x, 1, 0))
        above = jnp.where(at_top, 0.0, pltpu.roll(x, planes - 1, 0))
        return ((left + right) + (below + above)) - 4.0 * x

    def stencil(re, im, first, last):
        lap_re = lap(re, first[0], last[0])
        lap_im = lap(im, first[1], last[1])
        return 2.0 * re - RYZ * lap_im, 2.0 * im + RYZ * lap_re

    def fill(i, unused):
        part = pl.ds(i * group, group)
        laps = []
        for p in range(2):
            x = turned[p, part].reshape(group * planes, lines)
            high = x.astype(jnp.bfloat16)
            low = (x - high.astype(jnp.float32)).astype(jnp.bfloat16)
            y = (jnp.dot(high, band[...], preferred_element_type=jnp.float32)
                 + jnp.dot(low, band[...], preferred_element_type=jnp.float32))
            laps.append(y.reshape(group, planes, lines))
        for n in range(group):
            c = i * group + n
            lap_of = []
            for p in range(2):
                x = turned[p, c]
                below = jnp.where(at_bottom, 0.0, pltpu.roll(x, 1, 0))
                above = jnp.where(at_top, 0.0, pltpu.roll(x, planes - 1, 0))
                lap_of.append(laps[p][n] + (below + above))
            rho[0, c] = -inv * (2.0 * turned[1, c] + RYZ * lap_of[0])
            rho[1, c] = inv * (2.0 * turned[0, c] - RYZ * lap_of[1])
        return unused

    group = chunk
    lax.fori_loop(0, cells // group, fill, 0)

    @pl.when((gx < count - 1) & (beyond > 0))
    def _():
        pl.semaphore_wait(ready.at[count], beyond * (count - 1 - gx))

    @pl.loop(gx + 1, count)
    def _(peer):
        rims(peer, begin)

    @pl.loop(near, count)
    def _(peer):
        pl.semaphore_wait(ready.at[peer], 1)

    def arrival(k):
        return pltpu.make_async_remote_copy(
            fr.at[0], recv.at[k], s_sem.at[k], r_sem.at[k],
            device_id={"gx": k}, device_id_type=MESH)

    def all_rims(side):
        return pltpu.make_async_remote_copy(
            beside.at[side], beside.at[side], es_sem.at[side], er_sem.at[side],
            device_id={"gy": gy - 1 + 2 * side}, device_id_type=MESH)

    def both_rims(do):
        @pl.when(not_low)
        def _():
            do(all_rims(0))

        @pl.when(not_high)
        def _():
            do(all_rims(1))

    zero_rim = jnp.zeros((1, LANES), jnp.float32)

    @pl.when(gy == 0)
    def _():
        beside[0] = jnp.zeros(beside.shape[1:], jnp.float32)

    @pl.when(gy == wide - 1)
    def _():
        beside[1] = jnp.zeros(beside.shape[1:], jnp.float32)

    def sum_rims():
        both_rims(lambda copy: copy.wait_recv())

        def add(k, acc):
            return acc[0] + beside[0, k], acc[1] + beside[1, k]

        for n, row in enumerate(lax.fori_loop(0, gx, add, (zero_rim, zero_rim))
                                + lax.fori_loop(gx, count, add, (zero_rim, zero_rim))):
            rim_sum[n] = row

    def take(k, acc):
        cut = even & (gx == 0)

        @pl.when(cut)
        def _():
            pltpu.make_async_remote_copy(
                fr.at[1, :, rows[1]], recv.at[k, :, rows[1]], s_sem.at[0], r_sem.at[k],
                device_id={"gx": k}, device_id_type=MESH).wait_recv()

        @pl.when(jnp.logical_not(cut))
        def _():
            arrival(k).wait_recv()

        return acc[0] + recv[k, 0], acc[1] + recv[k, 1]

    def keep(which, value):
        total[which, 0] = value[0]
        total[which, 1] = value[1]

    def pass_on(which, value):
        relay[which, 0] = value[0]
        relay[which, 1] = value[1]
        hub_do(which, begin)

    def take_twin(value):
        twin_message(0, gx).wait_recv()
        return value[0] + twin[0], value[1] + twin[1]

    def take_left():
        if not split:
            keep(0, lax.fori_loop(0, gx, take, (zero, zero)))
            return
        above = gx >= half
        value = lax.fori_loop(jnp.where(above, half, 0), gx, take, (zero, zero))
        hub = half - 2 + lax.rem(gx, 2)
        value = lax.fori_loop(hub, hub + jnp.where(above, 1, 0), take, value)
        keep(0, value)
        value = value[0] + fr[0, 0], value[1] + fr[0, 1]

        @pl.when(gx == half - 1)
        def _():
            pass_on(0, value)

        @pl.when(gx == half - 2)
        def _():
            pass_on(0, take_twin(value))

    def take_right():
        own = (fr[1, 0], fr[1, 1])
        value = lax.fori_loop(gx + 1, count, take, own)
        keep(1, value)

        if not split:
            return

        @pl.when((gx == half) & odd)
        def _():
            pass_on(1, value)

        @pl.when((gx == half + 1) & odd)
        def _():
            pass_on(1, take_twin(value))

    def settle():
        @pl.when(not_low)
        def _():
            up.wait_recv()

        @pl.when(not_high)
        def _():
            down.wait_recv()

        wanted = [(inv * RYZ) * (halo[0, p] + halo[1, p]) for p in range(2)]

        def mend(c, unused):
            for p in range(2):
                h = pltpu.roll(wanted[p], LANES - 2 * c, 1)
                for side, at in enumerate((0, lines - LANES)):
                    old = rho[p, c, :, at : at + LANES]
                    rho[p, c, :, at : at + LANES] = jnp.where(lane == side * (LANES - 1), old - h, old)
            return unused

        lax.fori_loop(0, cells, mend, 0, unroll=8)

        @pl.when(even & (gx > 0))
        def _():
            for part in range(2):
                cut_message(part).wait_send()

        @pl.loop(0, count)
        def _(peer):
            @pl.when((peer != gx) & jnp.logical_not(by_hub(peer)) & (odd | (peer > 0)))
            def _():
                message(peer).wait_send()

        @pl.when(not_low)
        def _():
            down.wait_send()

        @pl.when(not_high)
        def _():
            up.wait_send()

        both_rims(end)
        pl.when(gx >= half)(sum_rims)

    def take_right_low():
        between = (gx >= 2) & (gx < half) & odd & split
        stop = jnp.where(between, half, count)

        @pl.when(even & (gx == 0))
        def _():
            lower = recv.at[1:count, :, rows[0]]
            pltpu.make_async_remote_copy(lower, lower, cut_sem.at[0], c_sem.at[0],
                                         device_id={"gx": count - 1}, device_id_type=MESH).wait_recv()

        value = lax.fori_loop(gx + 1, stop, take, (fr[1, 0], fr[1, 1]))
        hub = half + lax.rem(gx, 2)
        keep(1, lax.fori_loop(hub, hub + jnp.where(between, 1, 0), take, value))
        sum_rims()

    pl.when(gx < half)(take_left)
    pl.when(gx >= half)(take_right)
    settle()
    pl.when(gx < half)(take_right_low)
    pl.when(gx >= half)(take_left)
    left = (total[0, 0], total[0, 1], rim_sum[0], rim_sum[1])
    right = (total[1, 0], total[1, 1], rim_sum[2], rim_sum[3])

    def spread(side):
        columns = []
        for tile in side[2:]:
            columns.append(tuple(
                jnp.sum(jnp.where(lane_row == part * planes, tile, 0.0), axis=1, keepdims=True) for part in range(2)))
        return stencil(side[0], side[1], columns[0], columns[1])

    left = spread(left)
    right = spread(right)
    w = both(scalar(4), left, scalar(5), right)
    d = both(scalar(6), left, scalar(7), right)

    for index, value in enumerate(w + d):
        start[index] = value

    if split:
        pl.when((gx == half - 2) | (gx == half - 1))(lambda: hub_do(0, end))
        pl.when(((gx == half) | (gx == half + 1)) & odd)(lambda: hub_do(1, end))

        @pl.when((gx == half - 1) | ((gx == half) & odd))
        def _():
            twin_message(0, gx).wait_send()


def finish(coef, chunk, turned, rho, start, out, out_v, out_sem):
    cells = turned.shape[1]
    chunks = cells // chunk
    inv = np.float32(1.0 / coef)

    def store(i):
        part = pl.ds(i * chunk, chunk)
        return pltpu.make_async_copy(out_v.at[:, part], out.at[:, part], out_sem.at[0])

    def march(c, carry):
        w_re, w_im, d_re, d_im = carry
        w_re = w_re + d_re
        w_im = w_im + d_im
        out_v[0, c] = w_re - turned[0, c]
        out_v[1, c] = w_im - turned[1, c]
        d_re = (d_re + rho[0, c]) + inv * w_im
        d_im = (d_im + rho[1, c]) - inv * w_re
        return w_re, w_im, d_re, d_im

    carry = (start[0], start[1], start[2], start[3])
    for i in range(chunks):
        carry = lax.fori_loop(i * chunk, (i + 1) * chunk, march, carry, unroll=4)
        store(i).start()
    pltpu.make_async_copy(out_v, out, out_sem.at[0]).wait()


def shards(psi, potential):
    unused, cells, planes, lines = psi.shape
    count = lax.axis_size("gx")
    wide = lax.axis_size("gy")
    place, coef = tables(cells, count)
    chunk = 8 if cells % 8 == 0 else cells
    chunks = cells // chunk
    block = (2, cells, planes, lines)
    plane = (planes, lines)
    vmem = pl.BlockSpec(memory_space=pltpu.VMEM)
    held = pl.pallas_call(
        functools.partial(kernel, count, wide, coef, chunk),
        out_shape=[
            jax.ShapeDtypeStruct(block, jnp.float32),
            jax.ShapeDtypeStruct(block, jnp.float32),
            jax.ShapeDtypeStruct((4,) + plane, jnp.float32),
        ],
        in_specs=[
            pl.BlockSpec(memory_space=pltpu.HBM),
            pl.BlockSpec(memory_space=pltpu.HBM),
            pl.BlockSpec(memory_space=pltpu.HBM),
        ],
        out_specs=[vmem] * 3,
        scratch_shapes=[
            pltpu.SMEM(place.shape, jnp.float32),
            pltpu.SemaphoreType.DMA((1,)),
            pltpu.VMEM((3,) + block[1:], jnp.float32),
            pltpu.VMEM((2, 2, planes, LANES), jnp.float32),
            pltpu.VMEM((2, 2, planes, LANES), jnp.float32),
            pltpu.VMEM((2, 2) + plane, jnp.float32),
            pltpu.VMEM((count, 2) + plane, jnp.float32),
            pltpu.SemaphoreType.DMA((2, 2)),
            pltpu.SemaphoreType.DMA((2,)),
            pltpu.SemaphoreType.DMA((2,)),
            pltpu.SemaphoreType.DMA((count,)),
            pltpu.SemaphoreType.DMA((count,)),
            pltpu.VMEM((2, 2, 1, LANES), jnp.float32),
            pltpu.VMEM((2, count, 1, LANES), jnp.float32),
            pltpu.SemaphoreType.DMA((2,)),
            pltpu.SemaphoreType.DMA((2,)),
            pltpu.VMEM((lines, lines), jnp.bfloat16),
            pltpu.SemaphoreType.REGULAR((count + 1,)),
            pltpu.VMEM((2, 2) + plane, jnp.float32),
            pltpu.VMEM((4, 1, LANES), jnp.float32),
            pltpu.VMEM((2,) + plane, jnp.float32),
            pltpu.SemaphoreType.DMA((2,)),
            pltpu.VMEM((2, 2) + plane, jnp.float32),
            pltpu.SemaphoreType.DMA((1,)),
            pltpu.SemaphoreType.DMA((1,)),
        ],
        compiler_params=pltpu.CompilerParams(
            collective_id=0, has_side_effects=True, vmem_limit_bytes=24 * 2**20
        ),
    )(*(pltpu.with_memory_space_constraint(x, pltpu.HBM) for x in
        (psi, potential, jnp.asarray(place))))
    return pl.pallas_call(
        functools.partial(finish, coef, chunk),
        out_shape=jax.ShapeDtypeStruct(block, jnp.float32),
        in_specs=[vmem] * 3,
        out_specs=pl.BlockSpec(memory_space=pl.ANY),
        scratch_shapes=[
            pltpu.VMEM(block, jnp.float32),
            pltpu.SemaphoreType.DMA((1,)),
        ],
        compiler_params=pltpu.CompilerParams(vmem_limit_bytes=16 * 2**20),
    )(*held)


def solution(mesh):
    return jax.shard_map(
        shards,
        mesh=mesh,
        in_specs=(P(None, "gx", None, "gy"), P("gx", None, "gy")),
        out_specs=P(None, "gx", None, "gy"),
        check_vma=False,
    )
```
